32 devices in a mesh: dp: 4 (over z), wide: 8 (over y, x, core).
Axes of the slice: x: 2, y: 2, z: 4, core: 2. Of those that a mesh axis runs over, the one named last changes fastest.
Arguments:
- tokens: bfloat16 [32768, 768], P(('dp', 'wide')), may hold values from -6 to 6
- segment_ids: int32 [64, 512], P(('dp', 'wide')), may hold values from 0 to 7, never falling along the last dimension, each value on 1 to 256 neighbouring positions
- cotangent: bfloat16 [32768, 768], P(('dp', 'wide')), may hold values from -6 to 6
- query_frozen_weight: bfloat16 [768, 768], replicated, may hold values from -0.21875 to 0.21875
- query_bias_vector: bfloat16 [768], replicated, may hold values from -3 to 3
- w_key: bfloat16 [768, 768], replicated, may hold values from -0.21875 to 0.21875
- value_frozen_weight: bfloat16 [768, 768], replicated, may hold values from -0.21875 to 0.21875
- value_bias_vector: bfloat16 [768], replicated, may hold values from -3 to 3
- w_out: bfloat16 [768, 768], replicated, may hold values from -0.625 to 0.625
- b_out: bfloat16 [768], replicated, may hold values from -2 to 2
- norm1_gain: bfloat16 [768], replicated, may hold values from 0.5 to 1.5
- norm1_bias: bfloat16 [768], replicated, may hold values from -2 to 2
- w_up: bfloat16 [768, 3072], replicated, may hold values from -0.21875 to 0.21875
- b_up: bfloat16 [3072], replicated, may hold values from -3 to 3
- w_down: bfloat16 [3072, 768], replicated, may hold values from -0.109375 to 0.109375
- b_down: bfloat16 [768], replicated, may hold values from -2 to 2
- norm2_gain: bfloat16 [768], replicated, may hold values from 0.5 to 1.5
- norm2_bias: bfloat16 [768], replicated, may hold values from -2 to 2
- factors: float32 [24576], replicated, may hold values from -0.4 to 0.4
- moment_first: float32 [24576], P('wide'), may hold values from -0.006 to 0.006
- moment_second: float32 [24576], P('wide'), may hold values from 1e-08 to 1e-07
- step_count: int32 [1], replicated, may hold values from 1 to 10
- learn_rate: float32 [1], replicated, may hold values from 0.003 to 0.03
Outputs:
- output: bfloat16 [32768, 768], P(('dp', 'wide'))
- grad_tokens: bfloat16 [32768, 768], P(('dp', 'wide'))
- grad_factors: float32 [24576], P('wide')
- new_factors: float32 [24576], replicated
- new_first: float32 [24576], P('wide')
- new_second: float32 [24576], P('wide')
The draws below stay inside these ranges and needn't reach their ends.
Inputs may be any that keep to these rules, and one draw needn't show every extreme that they name: `segment_ids`: segment ids never fall along a pack; each segment holds 1 to 256 rows, one exactly 256.
All inputs are finite; a program needn't handle non-finite values.
Results may differ from the reference program's by a relative error of at most 0.014.
Values sent between devices are 32-bit elements; how exact they have to be, the bound alone decides.
No kernel may reach another device: no remote copies, remote signals or barrier semaphores. Data moves between devices by JAX's collectives and lax.ppermute only.
A program may use at most 192 MiB of HBM per device.

```python
import math
import jax
import jax.numpy as jnp
import numpy as np
from jax import lax

D = 768
HEADS = 12
FF = 3072
RANK = 8
SEQ = 512
SEGS = 8
HEAD_DIM = 64
PACKS = 64
TOKENS = 32768
NPAR = 24576


def draw_factors(key, part):
    base = jnp.clip(jax.random.normal(key, (NPAR,), jnp.float32), -3.0, 3.0)
    scales = jnp.where(jnp.arange(NPAR) < 2 * D * RANK, D ** (-0.5), 0.1)
    return (base * scales).astype(jnp.float32)


def block_levels(rng, shape, cuts, smallest, largest):
    loudness, own = 1.0, jax.random.fold_in(rng, 6)
    for position, blocks in cuts:
        steps = jnp.exp(jax.random.uniform(jax.random.fold_in(own, position), (blocks,), jnp.float32, smallest / len(cuts), largest / len(cuts)))
        loudness = loudness * jnp.repeat(steps, shape[position] // blocks).reshape([-1 if axis == position else 1 for axis in range(len(shape))])
    return loudness


def profile(number_of, total, bound, lean):
    weights = [(1 << 20) // math.isqrt(standing ** lean) + 1 for standing in range(2, number_of + 1)]
    spare, given = total - bound - (number_of - 1), [1] * (number_of - 1)
    while spare > 0:
        free = [i for i in range(number_of - 1) if given[i] < bound]
        mass, left = sum([weights[i] for i in free]), spare
        for i in free:
            extra = min(bound - given[i], max(1, left * weights[i] // mass), spare)
            given[i] = given[i] + extra
            spare = spare - extra
    return np.array([bound] + given)


def ragged_sizes(rng, count, total, reach, slope):
    if count == 2:
        one = jax.random.randint(rng, (), max(1, total - reach), min(reach, total - 1) + 1)
        return jnp.stack([one, total - one])
    sizes = jnp.asarray(profile(count, total, reach, slope), jnp.int32)
    twos = (count - 1) // 2
    source_of, sink = sizes[1:1 + 2 * twos:2], sizes[2:2 + 2 * twos:2]
    margin = jnp.minimum(source_of - 1, reach - sink)
    passed = jax.random.randint(jax.random.fold_in(rng, 1), (twos,), 0, 1 << 20) % (margin + 1)
    sizes = sizes.at[1:1 + 2 * twos:2].set(source_of - passed).at[2:2 + 2 * twos:2].set(sink + passed)
    return sizes[jax.random.permutation(jax.random.fold_in(rng, 2), count)]


def normal_values(stream_key, dims, scale, reach, split=(), dtype=jnp.bfloat16):
    result = scale * jax.random.normal(stream_key, dims, jnp.float32)
    if split:
        result = result * block_levels(stream_key, dims, split, -0.22, 0.18)
    return jnp.clip(result, -reach, reach).astype(dtype)


def setup_inputs(seed: int = 0) -> dict:
    streams_of = jax.random.split(jax.random.key(seed), 24)
    return {
        "tokens": normal_values(streams_of[0], (TOKENS, D), 1.0, 6.0, ((0, 32),)),
        "segment_ids": jax.vmap(lambda own: jnp.searchsorted(jnp.cumsum(ragged_sizes(own, SEGS, SEQ, SEQ // 2, 2)), jnp.arange(SEQ), side="right"))(jax.random.split(streams_of[1], PACKS)).reshape((PACKS, SEQ)).astype(jnp.int32),
        "cotangent": normal_values(streams_of[2], (TOKENS, D), 1.0, 6.0, ((0, 32),)),
        "query_frozen_weight": normal_values(streams_of[3], (D, D), D ** -0.5, 0.21875),
        "query_bias_vector": normal_values(streams_of[4], (D,), 0.5, 3.0),
        "w_key": normal_values(streams_of[5], (D, D), D ** -0.5, 0.21875),
        "value_frozen_weight": normal_values(streams_of[6], (D, D), D ** -0.5, 0.21875),
        "value_bias_vector": normal_values(streams_of[7], (D,), 0.5, 3.0),
        "w_out": normal_values(streams_of[8], (D, D), (D // 8) ** -0.5, 0.625),
        "b_out": normal_values(streams_of[9], (D,), 0.3, 2.0),
        "norm1_gain": jnp.clip(1.0 + 0.1 * jax.random.normal(streams_of[10], (D,), jnp.float32), 0.5, 1.5).astype(jnp.bfloat16),
        "norm1_bias": normal_values(streams_of[11], (D,), 0.3, 2.0),
        "w_up": normal_values(streams_of[12], (D, FF), D ** -0.5, 0.21875),
        "b_up": normal_values(streams_of[13], (FF,), 0.5, 3.0),
        "w_down": normal_values(streams_of[14], (FF, D), FF ** -0.5, 0.109375),
        "b_down": normal_values(streams_of[15], (D,), 0.3, 2.0),
        "norm2_gain": jnp.clip(1.0 + 0.1 * jax.random.normal(streams_of[16], (D,), jnp.float32), 0.5, 1.5).astype(jnp.bfloat16),
        "norm2_bias": normal_values(streams_of[17], (D,), 0.3, 2.0),
        "factors": draw_factors(jax.random.fold_in(streams_of[23], 71), 0),
        "moment_first": normal_values(streams_of[19], (NPAR,), 0.001, 0.006, ((0, 8),), jnp.float32),
        "moment_second": jnp.clip(jnp.exp(math.log(1.0000000116860974e-07) - 2.3025851 * jax.random.uniform(streams_of[20], (NPAR,), jnp.float32) ** block_levels(streams_of[20], (NPAR,), ((0, 8),), -0.2, 0.2)), 9.99999993922529e-09, 1.0000000116860974e-07),
        "step_count": jax.random.randint(streams_of[21], (1,), 1, 11).astype(jnp.int32),
        "learn_rate": jnp.clip(jnp.exp(jax.random.uniform(streams_of[22], (1,), jnp.float32, math.log(0.003), math.log(0.03))), 0.003, 0.03),
    }


@jax.custom_vjp
def reduced_rank_input(v):
    return lax.optimization_barrier(v.astype(jnp.bfloat16)).astype(jnp.float32)

@jax.custom_vjp
def reduced_rank_gradient(v):
    return v

def low_keep(v):
    return (reduced_rank_input(v), None)

def low_pass(kept, grad):
    return (grad,)

def back_keep(v):
    return (v, None)

def back_low(kept, grad):
    return (reduced_rank_input(grad),)
reduced_rank_input.defvjp(low_keep, low_pass)
reduced_rank_gradient.defvjp(back_keep, back_low)
norm_eps = 1e-05
adapter_scale = 2.0
beta_one = 0.9
beta_two = 0.999
adam_eps = 1e-08
decay_rate = 0.01
rate_ratio = 16.0
highest = lax.Precision.HIGHEST

def precise_product(left, right):
    return jnp.dot(left, right, precision=highest, preferred_element_type=jnp.float32)

def layer_norm(layer_input, gain_vec, shift_vec):
    row_mean = lax.optimization_barrier(jnp.mean(layer_input, axis=-1, keepdims=True))
    centered = layer_input - row_mean
    spread = lax.optimization_barrier(jnp.mean(centered * centered, axis=-1, keepdims=True))
    return centered * lax.rsqrt(spread + norm_eps) * gain_vec + shift_vec

def forward(layer_input, factors, segments, frozen):
    query_frozen_weight, query_bias_vector, w_key, value_frozen_weight, value_bias_vector, w_out, b_out, norm1_gain, norm1_bias, w_up, b_up, w_down, b_down, norm2_gain, norm2_bias = frozen
    block_len = D * RANK
    rounded = reduced_rank_input(factors)
    query_down_weight = rounded[:block_len].reshape(D, RANK)
    value_down_weight = rounded[block_len:2 * block_len].reshape(D, RANK)
    query_up_weight = rounded[2 * block_len:3 * block_len].reshape(RANK, D)
    value_up_weight = rounded[3 * block_len:].reshape(RANK, D)
    query_adapter_output = reduced_rank_input(reduced_rank_gradient(precise_product(layer_input, query_down_weight)))
    value_adapter_output = reduced_rank_input(reduced_rank_gradient(precise_product(layer_input, value_down_weight)))
    query_rows = reduced_rank_input(reduced_rank_gradient(precise_product(layer_input, query_frozen_weight) + query_bias_vector + adapter_scale * precise_product(query_adapter_output, query_up_weight)))
    keys_all = reduced_rank_input(reduced_rank_gradient(precise_product(layer_input, w_key)))
    value_rows_full = reduced_rank_input(reduced_rank_gradient(precise_product(layer_input, value_frozen_weight) + value_bias_vector + adapter_scale * precise_product(value_adapter_output, value_up_weight)))
    pack_count = segments.shape[0]
    head_shape = (pack_count, SEQ, HEADS, HEAD_DIM)
    query_heads = query_rows.reshape(head_shape)
    key_heads = keys_all.reshape(head_shape)
    value_heads = value_rows_full.reshape(head_shape)
    scores = jnp.einsum('pqhd,pkhd->phqk', query_heads, key_heads, precision=highest)
    scores = reduced_rank_gradient(scores * HEAD_DIM ** (-0.5))
    same_segment = segments[:, None, :, None] == segments[:, None, None, :]
    soft_weights = jax.nn.softmax(jnp.where(same_segment, scores, -1000000000.0), axis=-1)
    attended = jnp.einsum('phqk,pkhd->pqhd', reduced_rank_input(soft_weights), value_heads, precision=highest)
    attended = reduced_rank_input(reduced_rank_gradient(attended.reshape(pack_count * SEQ, D)))
    branch = reduced_rank_gradient(precise_product(attended, w_out) + b_out)
    hidden = layer_norm(layer_input + branch, norm1_gain, norm1_bias)
    pre_act = reduced_rank_gradient(precise_product(reduced_rank_input(hidden), w_up) + b_up)
    activated = reduced_rank_input(jax.nn.gelu(pre_act, approximate=False))
    mixed = reduced_rank_gradient(precise_product(activated, w_down) + b_down)
    return layer_norm(hidden + mixed, norm2_gain, norm2_bias)

def reference(tokens, segment_ids, cotangent, query_frozen_weight, query_bias_vector, w_key, value_frozen_weight, value_bias_vector, w_out, b_out, norm1_gain, norm1_bias, w_up, b_up, w_down, b_down, norm2_gain, norm2_bias, factors, moment_first, moment_second, step_count, learn_rate):
    frozen = tuple((item.astype(jnp.float32) for item in (query_frozen_weight, query_bias_vector, w_key, value_frozen_weight, value_bias_vector, w_out, b_out, norm1_gain, norm1_bias, w_up, b_up, w_down, b_down, norm2_gain, norm2_bias)))
    group_packs = 8 if PACKS % 8 == 0 else 1
    groups = PACKS // group_packs
    inputs_all = tokens.astype(jnp.float32).reshape(groups, group_packs * SEQ, D)
    cot_all = cotangent.astype(jnp.float32).reshape(groups, group_packs * SEQ, D)
    seg_all = segment_ids.reshape(groups, group_packs, SEQ)
    factor_full = factors.astype(jnp.float32)

    def one_group(summed, items):
        inputs_now, cot_now, seg_now = items
        outputs, pull = jax.vjp(lambda inputs_var, factor_var: forward(inputs_var, factor_var, seg_now, frozen), inputs_now, factor_full)
        grad_inputs, grad_factor = pull(cot_now)
        return (summed + grad_factor, (outputs.astype(jnp.bfloat16), grad_inputs.astype(jnp.bfloat16)))
    grad_sum, (outputs, grad_inputs) = lax.scan(one_group, jnp.zeros((NPAR,), jnp.float32), (inputs_all, cot_all, seg_all))
    squares = jnp.sum(grad_sum * grad_sum)
    clip = jnp.minimum(1.0, lax.rsqrt(squares + 1e-06))
    clipped = grad_sum * clip
    rate_each = jnp.where(jnp.arange(NPAR) < NPAR // 2, learn_rate[0], rate_ratio * learn_rate[0])
    steps_done = step_count[0].astype(jnp.float32)
    first_new = beta_one * moment_first + (1.0 - beta_one) * clipped
    second_new = beta_two * moment_second + (1.0 - beta_two) * clipped * clipped
    fix_one = 1.0 - jnp.power(beta_one, steps_done)
    fix_two = 1.0 - jnp.power(beta_two, steps_done)
    update = first_new / fix_one / (jnp.sqrt(second_new / fix_two) + adam_eps) + decay_rate * factor_full
    new_factors = factor_full - rate_each * update
    return (outputs.reshape(TOKENS, D), grad_inputs.reshape(TOKENS, D), grad_sum, new_factors, first_new, second_new)
```

```python
import functools

import jax
import jax.numpy as jnp
from jax import lax
from jax.experimental import pallas as pl
from jax.experimental.pallas import tpu as pltpu
from jax.sharding import PartitionSpec as P

HEADS = 12
RANK = 8
BIG = 256
HEAD_DIM = 64
LANES = 128

norm_eps = 1e-05
adapter_scale = 2.0
beta_one = 0.9
beta_two = 0.999
adam_eps = 1e-08
decay_rate = 0.01
rate_ratio = 16.0

bf16 = jnp.bfloat16
f32 = jnp.float32


def dot(left, right, ca=1, cb=0):
    return lax.dot_general(left, right, (((ca,), (cb,)), ((), ())), preferred_element_type=f32)


def rotate_rows(src, shift, emit):
    groups, _, width = src.shape
    coarse, fine = shift // 8, shift % 8
    back = lax.rem(8 - fine, 8)
    keep = lax.broadcasted_iota(jnp.int32, (8, width), 0) < 8 - fine
    spun = [
        pltpu.roll(src[lax.rem(coarse + i, groups)], back, 0) for i in range(groups + 1)
    ]
    moved = [jnp.where(keep, spun[i], spun[i + 1]) for i in range(groups)]
    for i in range(0, groups, 2):
        emit(i * 8, jnp.concatenate([moved[i], moved[i + 1]], axis=0))


def norm_rows(z):
    mean = jnp.mean(z, axis=-1, keepdims=True)
    centered = z - mean
    spread = jnp.mean(centered * centered, axis=-1, keepdims=True)
    root = lax.rsqrt(spread + norm_eps)
    return centered * root, root


def norm_rows_back(c, n, root):
    return root * (
        c - jnp.mean(c, axis=-1, keepdims=True) - n * jnp.mean(c * n, axis=-1, keepdims=True)
    )


def main_kernel(
    start_ref,
    tok_ref,
    cot_ref,
    seg_lo,
    seg_hi,
    wq_hbm,
    wk_hbm,
    wv_hbm,
    wo_hbm,
    wu_hbm,
    wd_hbm,
    dcat,
    uq,
    uv,
    bq,
    bv,
    bo,
    g1,
    b1,
    bu,
    bd,
    g2,
    b2,
    out_ref,
    dfirst_ref,
    dq_ref,
    dk_ref,
    dv_ref,
    dl_ref,
    grad_ref,
    wq,
    wk,
    wv,
    wo,
    wu,
    wd,
    sems,
    spin,
    xr,
    cr,
    qs,
    ks,
    vs,
    lora,
    probs,
    att,
    zs,
    n1,
    r1,
    hb,
    act,
    gp,
):
    pid = pl.program_id(0)
    rows, width = tok_ref.shape
    pairs = width // LANES
    copies = [
        pltpu.make_async_copy(src, dst, sems.at[i])
        for i, (src, dst) in enumerate(
            ((wq_hbm, wq), (wk_hbm, wk), (wv_hbm, wv), (wo_hbm, wo), (wu_hbm, wu), (wd_hbm, wd))
        )
    ]

    @pl.when(pid == 0)
    def _():
        for copy in copies:
            copy.start()

    def arrive(*which):
        @pl.when(pid == 0)
        def _():
            for i in which:
                copies[i].wait()

    start = start_ref[pid]

    def put(dst):
        def emit(at, block):
            dst[pl.ds(at, 16), :] = block.astype(dst.dtype)

        return emit

    spin[...] = tok_ref[...].astype(f32).reshape(spin.shape)
    rotate_rows(spin, start, put(xr))
    spin[...] = cot_ref[...].astype(f32).reshape(spin.shape)
    rotate_rows(spin, start, put(cr))

    lora[...] = dot(xr[...], dcat[...]).astype(bf16)
    arrive(0, 1, 2)
    query = dot(xr[...], wq[...]) + dot(lora[...], uq[...]) + bq[...].astype(f32)
    qs[...] = query.astype(bf16) * bf16(HEAD_DIM**-0.5)
    ks[...] = dot(xr[...], wk[...]).astype(bf16)
    value = dot(xr[...], wv[...]) + dot(lora[...], uv[...]) + bv[...].astype(f32)
    vs[...] = value.astype(bf16)

    row = lax.broadcasted_iota(jnp.int32, (BIG, LANES), 0) + (BIG + start)
    row = jnp.where(row >= rows, row - rows, row)
    lane = lax.broadcasted_iota(jnp.int32, (BIG, LANES), 1)
    inside = (row >= seg_lo[pl.ds(pid, 1), :]) & (row < seg_hi[pl.ds(pid, 1), :])
    own = jnp.where(inside, 1.0, 0.0)
    used = (lane % HEAD_DIM) < 8
    own_q = own.astype(bf16)
    other_k = jnp.where(used & jnp.logical_not(inside), -1e30, 0.0).astype(bf16)
    low = lane < HEAD_DIM
    none = jnp.zeros((BIG, LANES), bf16)

    def pair_forward(p, carry):
        at = pl.ds(pl.multiple_of(p * LANES, LANES), LANES)
        for block in range(2):
            span = pl.ds(block * BIG, BIG)
            qp, kp, vp = qs[span, at], ks[span, at], vs[span, at]
            fq, fk = (none, none) if block == 0 else (own_q, other_k)
            heads = []
            for half in range(2):
                mine = low if half == 0 else jnp.logical_not(low)
                scores = dot(jnp.where(mine, qp, fq), jnp.where(mine, kp, fk), 1, 1)
                top = jnp.max(scores, axis=-1, keepdims=True)
                e = jnp.exp(scores - top)
                total = jnp.sum(e, axis=-1, keepdims=True)
                soft = (e * (1.0 / total)).astype(bf16)
                probs[2 * p + half, block] = soft
                heads.append(dot(soft, vp))
            att[span, at] = jnp.where(low, heads[0], heads[1]).astype(bf16)
        return carry

    lax.fori_loop(0, pairs, pair_forward, 0)

    arrive(3)
    zs[...] = dot(att[...], wo[...])
    step = 64

    def first_norm(i, carry):
        at = pl.ds(pl.multiple_of(i * step, step), step)
        z = xr[at, :].astype(f32) + zs[at, :] + bo[...].astype(f32)
        n, root = norm_rows(z)
        n1[at, :] = n
        r1[at, :] = root
        hb[at, :] = (n * g1[...].astype(f32) + b1[...].astype(f32)).astype(bf16)
        return carry

    lax.fori_loop(0, rows // step, first_norm, 0)

    arrive(4)
    chunk = width
    count = act.shape[1] // chunk

    def up(c, carry):
        at = pl.ds(pl.multiple_of(c * chunk, chunk), chunk)
        u = dot(hb[...], wu[:, at]) + bu[:, at].astype(f32)
        half_cdf = 0.5 + 0.5 * lax.erf(u * (0.5**0.5))
        act[:, at] = (u * half_cdf).astype(bf16)
        bell = jnp.exp(u * u * -0.5) * 0.3989422804014327
        gp[:, at] = (half_cdf + u * bell).astype(bf16)
        return carry

    lax.fori_loop(0, count, up, 0)
    arrive(5)

    def down(c, carry):
        at = pl.ds(pl.multiple_of(c * BIG, BIG), BIG)
        zs[:, at] = dot(act[...], wd[:, at])
        return carry

    lax.fori_loop(0, width // BIG, down, 0)

    def second_norm(i, carry):
        at = pl.ds(pl.multiple_of(i * step, step), step)
        hidden = n1[at, :] * g1[...].astype(f32) + b1[...].astype(f32)
        z = hidden + zs[at, :] + bd[...].astype(f32)
        n, root = norm_rows(z)
        gain = g2[...].astype(f32)
        result = n * gain + b2[...].astype(f32)
        spin[pl.ds(i * (step // 8), step // 8)] = result.reshape(step // 8, 8, width)
        d = norm_rows_back(cr[at, :].astype(f32) * gain, n, root)
        zs[at, :] = d
        hb[at, :] = d.astype(bf16)
        return carry

    lax.fori_loop(0, rows // step, second_norm, 0)
    rotate_rows(spin, rows - start, put(out_ref))

    def up_back(c, carry):
        at = pl.ds(pl.multiple_of(c * chunk, chunk), chunk)
        t = dot(hb[...], wd[at, :], 1, 1)
        act[:, at] = (t * gp[:, at].astype(f32)).astype(bf16)
        return carry

    lax.fori_loop(0, count, up_back, 0)

    def down_back(c, carry):
        at = pl.ds(pl.multiple_of(c * BIG, BIG), BIG)
        zs[:, at] = zs[:, at] + dot(act[...], wu[at, :], 1, 1)
        return carry

    lax.fori_loop(0, width // BIG, down_back, 0)

    def first_norm_back(i, carry):
        at = pl.ds(pl.multiple_of(i * step, step), step)
        d = norm_rows_back(zs[at, :] * g1[...].astype(f32), n1[at, :], r1[at, :])
        dfirst_ref[at, :] = d
        hb[at, :] = d.astype(bf16)
        return carry

    lax.fori_loop(0, rows // step, first_norm_back, 0)
    cr[...] = dot(hb[...], wo[...], 1, 1).astype(bf16)

    def pair_back(p, carry):
        at = pl.ds(pl.multiple_of(p * LANES, LANES), LANES)
        for block in range(2):
            span = pl.ds(block * BIG, BIG)
            qp, kp, vp, dp = qs[span, at], ks[span, at], vs[span, at], cr[span, at]
            both = dp.astype(f32) * att[span, at].astype(f32)
            dqs, dks, dvs = [], [], []
            for half in range(2):
                mine = low if half == 0 else jnp.logical_not(low)
                delta = jnp.sum(jnp.where(mine, both, 0.0), axis=-1, keepdims=True)
                d_soft = dot(jnp.where(mine, dp, none), vp, 1, 1)
                soft = probs[2 * p + half, block]
                ds = (soft.astype(f32) * (d_soft - delta)).astype(bf16)
                dqs.append(dot(ds, kp))
                dks.append(dot(ds, qp, 0, 0))
                dvs.append(dot(soft, dp, 0, 0))
            dq_ref[span, at] = (jnp.where(low, *dqs) * HEAD_DIM**-0.5).astype(bf16)
            dk_ref[span, at] = jnp.where(low, *dks).astype(bf16)
            dv_ref[span, at] = jnp.where(low, *dvs).astype(bf16)
        return carry

    lax.fori_loop(0, pairs, pair_back, 0)

    dl = (dot(dq_ref[...], uq[...], 1, 1) + dot(dv_ref[...], uv[...], 1, 1)).astype(bf16)
    dl_ref[...] = dl
    gd = dot(dl, xr[...], 0, 0)
    gq = adapter_scale * dot(lora[...], dq_ref[...], 0, 0)
    gv = adapter_scale * dot(lora[...], dv_ref[...], 0, 0)
    grads = jnp.concatenate([gd[: 2 * RANK], gq[:RANK], gv[RANK : 2 * RANK]], axis=0)

    @pl.when(pid == 0)
    def _():
        grad_ref[...] = grads

    @pl.when(pid > 0)
    def _():
        grad_ref[...] += grads


def token_kernel(start_ref, dfirst, dq, dk, dv, dl, wq, wk, wv, dcat, out_ref, spin):
    pid = pl.program_id(0)
    rows, width = dfirst.shape
    total = dot(dq[...], wq[...], 1, 1) + dot(dk[...], wk[...], 1, 1)
    total = total + dot(dv[...], wv[...], 1, 1) + dot(dl[...], dcat[...], 1, 1)
    spin[...] = (dfirst[...] + total).reshape(spin.shape)

    def emit(at, block):
        out_ref[pl.ds(at, 16), :] = block.astype(bf16)

    rotate_rows(spin, rows - start_ref[pid], emit)


def swap(x, axis, bit):
    n = lax.axis_size(axis)
    return lax.ppermute(x, axis, [(i, i ^ bit) for i in range(n)])


def bits_of(axis):
    n = lax.axis_size(axis)
    return [1 << k for k in range(n.bit_length() - 1)]


def gather_shares(share, axis):
    index = lax.axis_index(axis)
    held = share[None]
    for bit in bits_of(axis):
        other = swap(held, axis, bit)
        first = (index & bit) == 0
        held = jnp.where(
            first, jnp.concatenate([held, other]), jnp.concatenate([other, held])
        )
    return held.reshape(-1)


def adam_update(params, gradient, first, second, norm_sq, steps_done, rate_now):
    clip = jnp.minimum(1.0, lax.rsqrt(norm_sq + 1e-06))
    clipped = gradient * clip
    first_new = beta_one * first + (1.0 - beta_one) * clipped
    second_new = beta_two * second + (1.0 - beta_two) * clipped * clipped
    fix_one = 1.0 - jnp.power(beta_one, steps_done)
    fix_two = 1.0 - jnp.power(beta_two, steps_done)
    update = first_new / fix_one / (jnp.sqrt(second_new / fix_two) + adam_eps) + decay_rate * params
    return (params - rate_now * update, first_new, second_new)


def shards(
    tokens,
    segment_ids,
    cotangent,
    query_frozen_weight,
    query_bias_vector,
    w_key,
    value_frozen_weight,
    value_bias_vector,
    w_out,
    b_out,
    norm1_gain,
    norm1_bias,
    w_up,
    b_up,
    w_down,
    b_down,
    norm2_gain,
    norm2_bias,
    factors,
    moment_first,
    moment_second,
    step_count,
    learn_rate,
):
    width = tokens.shape[1]
    packs, rows = segment_ids.shape
    ff = w_up.shape[1]
    block_len = width * RANK
    low = factors.astype(bf16)
    dcat = jnp.zeros((width, LANES), bf16)
    dcat = dcat.at[:, :RANK].set(low[:block_len].reshape(width, RANK))
    dcat = dcat.at[:, RANK : 2 * RANK].set(low[block_len : 2 * block_len].reshape(width, RANK))
    ups = low[2 * block_len :].reshape(2 * RANK, width) * bf16(adapter_scale)
    uq = jnp.zeros((LANES, width), bf16).at[:RANK].set(ups[:RANK])
    uv = jnp.zeros((LANES, width), bf16).at[RANK : 2 * RANK].set(ups[RANK:])

    same = segment_ids[:, : rows - BIG + 1] == segment_ids[:, BIG - 1 :]
    start = jnp.sum(jnp.where(same, jnp.arange(rows - BIG + 1), 0), axis=1).astype(jnp.int32)
    slot = jnp.arange(LANES) % HEAD_DIM
    seg_lo = jnp.sum(segment_ids[:, None, :] < slot[None, :, None], axis=2).astype(jnp.int32)
    seg_hi = jnp.sum(segment_ids[:, None, :] <= slot[None, :, None], axis=2).astype(jnp.int32)

    def vec(v):
        return v.reshape(1, -1)

    per_pack = pl.BlockSpec((rows, width), lambda i, s: (i, 0))
    whole = lambda shape: pl.BlockSpec(shape, lambda i, s: (0,) * len(shape))
    anywhere = pl.BlockSpec(memory_space=pl.ANY)
    total_rows = packs * rows
    result = lambda shape, dtype: jax.ShapeDtypeStruct(shape, dtype)
    weights = (query_frozen_weight, w_key, value_frozen_weight, w_out, w_up, w_down)
    vectors = (
        query_bias_vector,
        value_bias_vector,
        b_out,
        norm1_gain,
        norm1_bias,
        b_up,
        b_down,
        norm2_gain,
        norm2_bias,
    )
    output, dfirst, dq, dk, dv, dl, grads = pl.pallas_call(
        main_kernel,
        out_shape=(
            result((total_rows, width), bf16),
            result((total_rows, width), f32),
            result((total_rows, width), bf16),
            result((total_rows, width), bf16),
            result((total_rows, width), bf16),
            result((total_rows, LANES), bf16),
            result((4 * RANK, width), f32),
        ),
        grid_spec=pltpu.PrefetchScalarGridSpec(
            num_scalar_prefetch=1,
            grid=(packs,),
            in_specs=[per_pack, per_pack, whole((packs, LANES)), whole((packs, LANES))]
            + [anywhere] * 6
            + [whole((width, LANES)), whole((LANES, width)), whole((LANES, width))]
            + [whole((1, v.shape[0])) for v in vectors],
            out_specs=[per_pack] * 5
            + [pl.BlockSpec((rows, LANES), lambda i, s: (i, 0)), whole((4 * RANK, width))],
            scratch_shapes=[pltpu.VMEM(w.shape, bf16) for w in weights]
            + [
                pltpu.SemaphoreType.DMA((6,)),
                pltpu.VMEM((rows // 8, 8, width), f32),
                pltpu.VMEM((rows, width), bf16),
                pltpu.VMEM((rows, width), bf16),
                pltpu.VMEM((rows, width), bf16),
                pltpu.VMEM((rows, width), bf16),
                pltpu.VMEM((rows, width), bf16),
                pltpu.VMEM((rows, LANES), bf16),
                pltpu.VMEM((HEADS, 2, BIG, BIG), bf16),
                pltpu.VMEM((rows, width), bf16),
                pltpu.VMEM((rows, width), f32),
                pltpu.VMEM((rows, width), f32),
                pltpu.VMEM((rows, 1), f32),
                pltpu.VMEM((rows, width), bf16),
                pltpu.VMEM((rows, ff), bf16),
                pltpu.VMEM((rows, ff), bf16),
            ],
        ),
        compiler_params=pltpu.CompilerParams(
            dimension_semantics=("arbitrary",), vmem_limit_bytes=60 * 2**20
        ),
    )(
        start,
        tokens,
        cotangent,
        seg_lo,
        seg_hi,
        *weights,
        dcat,
        uq,
        uv,
        *[vec(v) for v in vectors],
    )

    down_grads = grads[: 2 * RANK].reshape(2, RANK, width).transpose(0, 2, 1).reshape(-1)
    total = jnp.concatenate([down_grads, grads[2 * RANK :].reshape(-1)])
    for axis in ("wide", "dp"):
        for bit in bits_of(axis):
            total = total + swap(total, axis, bit)

    grad_tokens = pl.pallas_call(
        token_kernel,
        out_shape=result((total_rows, width), bf16),
        grid_spec=pltpu.PrefetchScalarGridSpec(
            num_scalar_prefetch=1,
            grid=(packs,),
            in_specs=[per_pack] * 4
            + [pl.BlockSpec((rows, LANES), lambda i, s: (i, 0))]
            + [whole((width, width))] * 3
            + [whole((width, LANES))],
            out_specs=per_pack,
            scratch_shapes=[pltpu.VMEM((rows // 8, 8, width), f32)],
        ),
        compiler_params=pltpu.CompilerParams(
            dimension_semantics=("arbitrary",), vmem_limit_bytes=40 * 2**20
        ),
    )(start, dfirst, dq, dk, dv, dl, *weights[:3], dcat)

    wide_count = lax.axis_size("wide")
    wide_index = lax.axis_index("wide")
    own_len = factors.shape[0] // wide_count
    steps_done = step_count[0].astype(f32)
    rate_now = jnp.where(wide_index < wide_count // 2, learn_rate[0], rate_ratio * learn_rate[0])
    norm_sq = jnp.sum(total * total)
    owned_grad = lax.dynamic_slice_in_dim(total, wide_index * own_len, own_len)
    own_params = lax.dynamic_slice_in_dim(factors, wide_index * own_len, own_len)
    params_new, new_first, new_second = adam_update(
        own_params, owned_grad, moment_first, moment_second, norm_sq, steps_done, rate_now
    )
    new_factors = gather_shares(params_new, "wide")
    return (output, grad_tokens, owned_grad, new_factors, new_first, new_second)


def solution(mesh):
    rows = P(("dp", "wide"), None)
    in_specs = (rows,) * 3 + (P(),) * 16 + (P("wide"), P("wide"), P(), P())
    out_specs = (rows, rows, P("wide"), P(), P("wide"), P("wide"))
    return jax.shard_map(shards, mesh=mesh, in_specs=in_specs, out_specs=out_specs, check_vma=False)
```

```python
import functools

import jax
import jax.numpy as jnp
from jax import lax
from jax.experimental import pallas as pl
from jax.experimental.pallas import tpu as pltpu
from jax.sharding import PartitionSpec as P

HEADS = 12
RANK = 8
BIG = 256
HEAD_DIM = 64
LANES = 128
GROUP = 3
LOG2E = 1.4426950408889634

norm_eps = 1e-05
adapter_scale = 2.0
beta_one = 0.9
beta_two = 0.999
adam_eps = 1e-08
decay_rate = 0.01
rate_ratio = 16.0

bf16 = jnp.bfloat16
f32 = jnp.float32


def dot(left, right, ca=1, cb=0):
    return lax.dot_general(left, right, (((ca,), (cb,)), ((), ())), preferred_element_type=f32)


def line(vector):
    return vector.astype(f32).reshape(1, -1)


def unpack_factors(fac_ref, dcat, uq, uv):
    width = dcat.shape[0]
    per = width * RANK // LANES
    group = LANES // RANK
    lane = lax.broadcasted_iota(jnp.int32, (width, LANES), 1)
    sub = lax.broadcasted_iota(jnp.int32, (width, LANES), 0)
    keep = (lane // RANK) == (sub % group)
    spread = []
    for which in range(2):
        flat = fac_ref[which * per : (which + 1) * per, :].astype(bf16).astype(f32)
        wide = jnp.broadcast_to(flat[:, None, :], (per, group, LANES)).reshape(width, LANES)
        wide = jnp.where(keep, wide, 0.0)
        for hop in (8, 16, 32, 64):
            wide = wide + pltpu.roll(wide, hop, 1)
        spread.append(wide)
    dcat[...] = jnp.where(lane < HEAD_DIM, *spread).astype(bf16)
    tiles = width // LANES
    none = jnp.zeros((HEAD_DIM, width), bf16)
    for which, ref in enumerate((uq, uv)):
        base = 2 * per + which * per
        block = jnp.concatenate(
            [fac_ref[pl.ds(base + j, RANK, stride=tiles), :] for j in range(tiles)], axis=1
        )
        block = (block * adapter_scale).astype(bf16)
        half = jnp.concatenate([block] * (HEAD_DIM // RANK), axis=0)
        ref[...] = jnp.concatenate([half, none] if which == 0 else [none, half], axis=0)


def pack_grads(grad_ref, gd, gq, gv):
    width = gd.shape[1]
    per = width * RANK // LANES
    group = LANES // RANK
    tiles = width // LANES
    lane = lax.broadcasted_iota(jnp.int32, (width, LANES), 1)
    sub = lax.broadcasted_iota(jnp.int32, (width, LANES), 0)
    keep = (lane // RANK) == (sub % group)
    turned = jnp.concatenate(
        [gd[:, j * LANES : (j + 1) * LANES].T for j in range(tiles)], axis=0
    )
    other = pltpu.roll(turned, HEAD_DIM, 1)
    for which, (first, second) in enumerate(((turned, other), (other, turned))):
        full = jnp.where(lane < HEAD_DIM, first, second)
        picked = jnp.where(keep, full, 0.0).reshape(per, group, LANES)
        grad_ref[which * per : (which + 1) * per, :] = jnp.sum(picked, axis=1)
    for which, block in enumerate((gq, gv)):
        base = 2 * per + which * per
        for j in range(tiles):
            grad_ref[pl.ds(base + j, RANK, stride=tiles), :] = block[:, j * LANES : (j + 1) * LANES]


def rotate_rows(src, shift, emit):
    groups, _, width = src.shape
    coarse, fine = shift // 8, shift % 8
    back = lax.rem(8 - fine, 8)
    keep = lax.broadcasted_iota(jnp.int32, (8, width), 0) < 8 - fine
    spun = [
        pltpu.roll(src[lax.rem(coarse + i, groups)], back, 0) for i in range(groups + 1)
    ]
    moved = [jnp.where(keep, spun[i], spun[i + 1]) for i in range(groups)]
    for i in range(0, groups, 2):
        emit(i * 8, jnp.concatenate([moved[i], moved[i + 1]], axis=0))


def norm_rows(z):
    mean = jnp.mean(z, axis=-1, keepdims=True)
    centered = z - mean
    spread = jnp.mean(centered * centered, axis=-1, keepdims=True)
    root = lax.rsqrt(spread + norm_eps)
    return centered * root, root


def norm_rows_back(c, n, root):
    return root * (
        c - jnp.mean(c, axis=-1, keepdims=True) - n * jnp.mean(c * n, axis=-1, keepdims=True)
    )


def main_kernel(
    seg_ref,
    fac_ref,
    first_ref,
    second_ref,
    tok_ref,
    cot_ref,
    wq_hbm,
    wk_hbm,
    wv_hbm,
    wo_hbm,
    wu_hbm,
    wd_hbm,
    bq,
    bv,
    bo,
    g1,
    b1,
    bu,
    bd,
    g2,
    b2,
    start_ref,
    dcat,
    out_ref,
    dfirst_ref,
    dq_ref,
    dk_ref,
    dv_ref,
    dl_ref,
    grad_ref,
    wq,
    wk,
    wv,
    wo,
    wu,
    wd,
    sems,
    spin,
    xr,
    cr,
    qs,
    ks,
    vs,
    lora,
    probs,
    att,
    zs,
    n1,
    r1,
    hb,
    act,
    gp,
    uq,
    uv,
    gd_sum,
    gu_sum,
    inv,
):
    pid = pl.program_id(0)
    rows, width = tok_ref.shape
    pairs = width // LANES
    copies = [
        pltpu.make_async_copy(src, dst, sems.at[i])
        for i, (src, dst) in enumerate(
            ((wq_hbm, wq), (wk_hbm, wk), (wv_hbm, wv), (wo_hbm, wo), (wu_hbm, wu), (wd_hbm, wd))
        )
    ]

    @pl.when(pid == 0)
    def _():
        for copy in copies:
            copy.start()

    def arrive(*which):
        @pl.when(pid == 0)
        def _():
            for i in which:
                copies[i].wait()

    @pl.when(pid == 0)
    def _():
        unpack_factors(fac_ref, dcat, uq, uv)

    seg = jnp.broadcast_to(seg_ref[pl.ds(pid, 1), :], (LANES, rows))
    slot = lax.broadcasted_iota(jnp.int32, (LANES, rows), 0) % HEAD_DIM
    ones = jnp.ones((8, rows), bf16)
    seg_lo = dot(ones, jnp.where(seg < slot, 1.0, 0.0).astype(bf16), 1, 1)[:1]
    seg_hi = dot(ones, jnp.where(seg <= slot, 1.0, 0.0).astype(bf16), 1, 1)[:1]
    low_lane = lax.broadcasted_iota(jnp.int32, (1, LANES), 1) < HEAD_DIM
    start = jnp.sum(jnp.where(low_lane & (seg_hi - seg_lo == BIG), seg_lo, 0.0)).astype(jnp.int32)
    start_ref[pid] = start
    seg_lo = seg_lo.astype(jnp.int32)
    seg_hi = seg_hi.astype(jnp.int32)

    def put(dst):
        def emit(at, block):
            dst[pl.ds(at, 16), :] = block.astype(dst.dtype)

        return emit

    spin[...] = tok_ref[...].astype(f32).reshape(spin.shape)
    rotate_rows(spin, start, put(xr))
    spin[...] = cot_ref[...].astype(f32).reshape(spin.shape)
    rotate_rows(spin, start, put(cr))

    lora[...] = dot(xr[...], dcat[...]).astype(bf16)
    narrow = lax.broadcasted_iota(jnp.int32, (rows, LANES), 1) % HEAD_DIM < RANK
    lora_once = jnp.where(narrow, lora[...], jnp.zeros((rows, LANES), bf16))
    arrive(0, 1, 2)
    query = dot(xr[...], wq[...]) + dot(lora_once, uq[...]) + line(bq[...])
    qs[...] = (query * (HEAD_DIM**-0.5 * LOG2E)).astype(bf16)
    ks[...] = dot(xr[...], wk[...]).astype(bf16)
    value = dot(xr[...], wv[...]) + dot(lora_once, uv[...]) + line(bv[...])
    vs[...] = value.astype(bf16)

    row = lax.broadcasted_iota(jnp.int32, (BIG, LANES), 0) + (BIG + start)
    row = jnp.where(row >= rows, row - rows, row)
    lane = lax.broadcasted_iota(jnp.int32, (BIG, LANES), 1)
    inside = (row >= seg_lo) & (row < seg_hi)
    own = jnp.where(inside, 1.0, 0.0)
    used = (lane % HEAD_DIM) < 8
    own_q = own.astype(bf16)
    other_k = jnp.where(used & jnp.logical_not(inside), -1e30, 0.0).astype(bf16)
    low = lane < HEAD_DIM
    high = jnp.logical_not(low)
    none = jnp.zeros((BIG, LANES), bf16)
    ones_pair = jnp.ones((BIG, LANES), bf16)

    def heads_of(group):
        units = []
        for k in range(GROUP):
            pair = group * GROUP + k
            at = pl.ds(pl.multiple_of(pair * LANES, LANES), LANES)
            for block in range(2):
                for half in range(2):
                    units.append((pair, block, pl.ds(block * BIG, BIG), at, half))
        return units

    def pipeline(units, first, second, third, finish):
        count = len(units)
        begun, middle, ended = {}, {}, {}

        def close(k):
            ended[k] = third(units[k], middle.pop(k))
            if k % 2:
                finish(units[k], ended.pop(k - 1), ended.pop(k))

        for k in range(min(2, count)):
            begun[k] = first(units[k])
        for k in range(count):
            if k + 2 < count:
                begun[k + 2] = first(units[k + 2])
            middle[k] = second(units[k], begun.pop(k))
            if k:
                close(k - 1)
        close(count - 1)

    def group_forward(group, carry):
        def scores(unit):
            _, block, span, at, half = unit
            mine = low if half == 0 else high
            if block == 0:
                return dot(qs[span, at], jnp.where(mine, ks[span, at], none), 1, 1)
            query = jnp.where(mine, qs[span, at], own_q)
            return dot(query, jnp.where(mine, ks[span, at], other_k), 1, 1)

        def soften(unit, s):
            pair, block, _, _, half = unit
            e = jnp.exp2(s - jnp.max(s, axis=-1, keepdims=True))
            low_e = e.astype(bf16)
            probs[2 * pair + half, block] = low_e
            return low_e, jnp.sum(e, axis=-1, keepdims=True)

        def mix(unit, held):
            _, _, span, at, _ = unit
            return dot(held[0], vs[span, at]), held[1]

        def finish(unit, one, two):
            _, _, span, at, _ = unit
            scale = 1.0 / jnp.where(low, one[1], two[1])
            inv[span, at] = scale
            att[span, at] = (jnp.where(low, one[0], two[0]) * scale).astype(bf16)

        pipeline(heads_of(group), scores, soften, mix, finish)
        return carry

    lax.fori_loop(0, pairs // GROUP, group_forward, 0)

    arrive(3)
    zs[...] = dot(att[...], wo[...])
    step = 64

    def first_norm(i, carry):
        at = pl.ds(pl.multiple_of(i * step, step), step)
        z = xr[at, :].astype(f32) + zs[at, :] + line(bo[...])
        n, root = norm_rows(z)
        n1[at, :] = n
        r1[at, :] = root
        hb[at, :] = (n * line(g1[...]) + line(b1[...])).astype(bf16)
        return carry

    lax.fori_loop(0, rows // step, first_norm, 0)

    arrive(4)
    chunk = width
    count = act.shape[1] // chunk

    def up(c, carry):
        at = pl.ds(pl.multiple_of(c * chunk, chunk), chunk)
        u = dot(hb[...], wu[:, at]) + line(bu[at])
        half_cdf = 0.5 + 0.5 * lax.erf(u * (0.5**0.5))
        act[:, at] = (u * half_cdf).astype(bf16)
        bell = jnp.exp(u * u * -0.5) * 0.3989422804014327
        gp[:, at] = (half_cdf + u * bell).astype(bf16)
        return carry

    lax.fori_loop(0, count, up, 0)
    arrive(5)

    def down(c, carry):
        at = pl.ds(pl.multiple_of(c * BIG, BIG), BIG)
        zs[:, at] = dot(act[...], wd[:, at])
        return carry

    lax.fori_loop(0, width // BIG, down, 0)

    def second_norm(i, carry):
        at = pl.ds(pl.multiple_of(i * step, step), step)
        hidden = n1[at, :] * line(g1[...]) + line(b1[...])
        z = hidden + zs[at, :] + line(bd[...])
        n, root = norm_rows(z)
        gain = line(g2[...])
        result = n * gain + line(b2[...])
        spin[pl.ds(i * (step // 8), step // 8)] = result.reshape(step // 8, 8, width)
        d = norm_rows_back(cr[at, :].astype(f32) * gain, n, root)
        zs[at, :] = d
        hb[at, :] = d.astype(bf16)
        return carry

    lax.fori_loop(0, rows // step, second_norm, 0)
    rotate_rows(spin, rows - start, put(out_ref))

    def up_back(c, carry):
        at = pl.ds(pl.multiple_of(c * chunk, chunk), chunk)
        t = dot(hb[...], wd[at, :], 1, 1)
        act[:, at] = (t * gp[:, at].astype(f32)).astype(bf16)
        return carry

    lax.fori_loop(0, count, up_back, 0)

    def down_back(c, carry):
        at = pl.ds(pl.multiple_of(c * BIG, BIG), BIG)
        zs[:, at] = zs[:, at] + dot(act[...], wu[at, :], 1, 1)
        return carry

    lax.fori_loop(0, width // BIG, down_back, 0)

    def first_norm_back(i, carry):
        at = pl.ds(pl.multiple_of(i * step, step), step)
        d = norm_rows_back(zs[at, :] * line(g1[...]), n1[at, :], r1[at, :])
        dfirst_ref[at, :] = d
        hb[at, :] = d.astype(bf16)
        return carry

    lax.fori_loop(0, rows // step, first_norm_back, 0)
    cr[...] = dot(hb[...], wo[...], 1, 1).astype(bf16)

    def group_back(group, carry):
        ready = {}

        def slopes(unit):
            _, block, span, at, half = unit
            if half == 0:
                scaled = cr[span, at].astype(f32) * inv[span, at]
                minus = pltpu.roll(-scaled * att[span, at].astype(f32), HEAD_DIM, 1)
                scaled = scaled.astype(bf16)
                ready[id(at), block] = scaled, minus.astype(bf16), scaled.T, qs[span, at].T
            scaled, minus = ready[id(at), block][:2]
            mine = low if half == 0 else high
            left = jnp.where(mine, scaled, minus)
            return dot(left, jnp.where(mine, vs[span, at], ones_pair), 1, 1)

        def weigh(unit, d):
            pair, block, _, _, half = unit
            e = probs[2 * pair + half, block]
            return e * d.astype(bf16), e

        def grads_of(unit, held):
            _, block, span, at, half = unit
            ds, e = held
            _, _, scaled_t, query_t = ready[id(at), block]
            lines = slice(half * HEAD_DIM, (half + 1) * HEAD_DIM)
            return dot(ds, ks[span, at]), dot(query_t[lines], ds), dot(scaled_t[lines], e)

        def finish(unit, one, two):
            _, block, span, at, _ = unit
            ready.pop((id(at), block))
            dq_ref[span, at] = (jnp.where(low, one[0], two[0]) * HEAD_DIM**-0.5).astype(bf16)
            dk = jnp.concatenate([one[1], two[1]], axis=0) * (1.0 / LOG2E)
            dk_ref[span, at] = dk.astype(bf16).T
            dv_ref[span, at] = jnp.concatenate([one[2], two[2]], axis=0).astype(bf16).T

        pipeline(heads_of(group), slopes, weigh, grads_of, finish)
        return carry

    lax.fori_loop(0, pairs // GROUP, group_back, 0)

    dl = (dot(dq_ref[...], uq[...], 1, 1) + dot(dv_ref[...], uv[...], 1, 1)).astype(bf16)
    dl_ref[...] = jnp.where(narrow, dl, jnp.zeros((rows, LANES), bf16))
    gd = dot(dl, xr[...], 0, 0)
    gq = adapter_scale * dot(lora[...], dq_ref[...], 0, 0)[:RANK]
    gv = adapter_scale * dot(lora[...], dv_ref[...], 0, 0)[HEAD_DIM : HEAD_DIM + RANK]

    @pl.when(pid == 0)
    def _():
        gd_sum[...] = gd
        gu_sum[0] = gq
        gu_sum[1] = gv

    @pl.when(pid > 0)
    def _():
        gd_sum[...] += gd
        gu_sum[0] += gq
        gu_sum[1] += gv

    @pl.when(pid == pl.num_programs(0) - 1)
    def _():
        pack_grads(grad_ref, gd_sum[...], gu_sum[0], gu_sum[1])
        base, more = fac_ref.shape[0], first_ref.shape[0]
        grad_ref[base : base + more, :] = first_ref[...]
        grad_ref[base + more :, :] = second_ref[...]


def token_kernel(pack, start_ref, dfirst, dq, dk, dv, dl, wq, wk, wv, dcat, *rest):
    out_ref, spin = rest[-2:]
    total = dot(dq[...], wq[...], 1, 1) + dot(dk[...], wk[...], 1, 1)
    total = total + dot(dv[...], wv[...], 1, 1) + dot(dl[...], dcat[...], 1, 1)
    spin[...] = (dfirst[...] + total).reshape(spin.shape)

    def emit(at, block):
        out_ref[pl.ds(at, 16), :] = block.astype(bf16)

    rotate_rows(spin, dfirst.shape[0] - start_ref[pack], emit)


def optimizer_kernel(steps_ref, rate_ref, place_ref, total, params, moments, grad_out, new_params, first_out, second_out):
    shares = total.shape[0]
    norm_sq = jnp.sum(jnp.sum(total[...] * total[...], axis=0), keepdims=True)
    clip = jnp.minimum(1.0, lax.rsqrt(norm_sq + 1e-06))
    place = place_ref[0]

    def power(base):
        return lax.fori_loop(0, steps_ref[0], lambda _, value: value * base, jnp.float32(1.0))

    shape = total.shape[1:]
    fix_one = jnp.full(shape, 1.0 - power(beta_one), f32)
    fix_two = jnp.full(shape, 1.0 - power(beta_two), f32)
    grad_out[...] = total[place]
    for j in range(shares):
        share = place ^ j
        clipped = total[share] * clip
        first = beta_one * moments[j, 0] + (1.0 - beta_one) * clipped
        second = beta_two * moments[j, 1] + (1.0 - beta_two) * clipped * clipped
        if j == 0:
            first_out[...] = first
            second_out[...] = second
        held = params[share]
        update = first / fix_one / (jnp.sqrt(second / fix_two) + adam_eps) + decay_rate * held
        rate = rate_ref[0] * jnp.where(share < shares // 2, 1.0, rate_ratio)
        new_params[share] = held - rate * update


def swap(x, axis, bit):
    n = lax.axis_size(axis)
    return lax.ppermute(x, axis, [(i, i ^ bit) for i in range(n)])


def bits_of(axis):
    n = lax.axis_size(axis)
    return [1 << k for k in range(n.bit_length() - 1)]


def shards(
    tokens,
    segment_ids,
    cotangent,
    query_frozen_weight,
    query_bias_vector,
    w_key,
    value_frozen_weight,
    value_bias_vector,
    w_out,
    b_out,
    norm1_gain,
    norm1_bias,
    w_up,
    b_up,
    w_down,
    b_down,
    norm2_gain,
    norm2_bias,
    factors,
    moment_first,
    moment_second,
    step_count,
    learn_rate,
):
    width = tokens.shape[1]
    packs, rows = segment_ids.shape
    ff = w_up.shape[1]
    flat_rows = factors.shape[0] // LANES
    flat = factors.reshape(flat_rows, LANES)
    shares = lax.axis_size("wide")
    own_rows = flat_rows // shares

    per_pack = pl.BlockSpec((rows, width), lambda i: (i, 0))
    whole = lambda shape: pl.BlockSpec(shape, lambda i: (0,) * len(shape))
    anywhere = pl.BlockSpec(memory_space=pl.ANY)
    scalars = pl.BlockSpec(memory_space=pltpu.SMEM)
    total_rows = packs * rows
    result = lambda shape, dtype: jax.ShapeDtypeStruct(shape, dtype)
    weights = (query_frozen_weight, w_key, value_frozen_weight, w_out, w_up, w_down)
    vectors = (
        query_bias_vector,
        value_bias_vector,
        b_out,
        norm1_gain,
        norm1_bias,
        b_up,
        b_down,
        norm2_gain,
        norm2_bias,
    )
    start, dcat, output, dfirst, dq, dk, dv, dl, grads = pl.pallas_call(
        main_kernel,
        out_shape=(
            result((packs,), jnp.int32),
            result((width, LANES), bf16),
            result((total_rows, width), bf16),
            result((total_rows, width), f32),
            result((total_rows, width), bf16),
            result((total_rows, width), bf16),
            result((total_rows, width), bf16),
            result((total_rows, LANES), bf16),
            result((flat_rows + 2 * own_rows, LANES), f32),
        ),
        grid_spec=pltpu.PrefetchScalarGridSpec(
            num_scalar_prefetch=0,
            grid=(packs,),
            in_specs=[whole((packs, rows)), whole((flat_rows, LANES))]
            + [whole((own_rows, LANES))] * 2
            + [per_pack] * 2
            + [anywhere] * 6
            + [whole(v.shape) for v in vectors],
            out_specs=[scalars, whole((width, LANES))]
            + [per_pack] * 5
            + [pl.BlockSpec((rows, LANES), lambda i: (i, 0)), whole((flat_rows + 2 * own_rows, LANES))],
            scratch_shapes=[pltpu.VMEM(w.shape, bf16) for w in weights]
            + [
                pltpu.SemaphoreType.DMA((6,)),
                pltpu.VMEM((rows // 8, 8, width), f32),
                pltpu.VMEM((rows, width), bf16),
                pltpu.VMEM((rows, width), bf16),
                pltpu.VMEM((rows, width), bf16),
                pltpu.VMEM((rows, width), bf16),
                pltpu.VMEM((rows, width), bf16),
                pltpu.VMEM((rows, LANES), bf16),
                pltpu.VMEM((HEADS, 2, BIG, BIG), bf16),
                pltpu.VMEM((rows, width), bf16),
                pltpu.VMEM((rows, width), f32),
                pltpu.VMEM((rows, width), f32),
                pltpu.VMEM((rows, 1), f32),
                pltpu.VMEM((rows, width), bf16),
                pltpu.VMEM((rows, ff), bf16),
                pltpu.VMEM((rows, ff), bf16),
                pltpu.VMEM((LANES, width), bf16),
                pltpu.VMEM((LANES, width), bf16),
                pltpu.VMEM((LANES, width), f32),
                pltpu.VMEM((2, RANK, width), f32),
                pltpu.VMEM((rows, width), f32),
            ],
        ),
        compiler_params=pltpu.CompilerParams(
            dimension_semantics=("arbitrary",), vmem_limit_bytes=60 * 2**20
        ),
    )(
        segment_ids,
        flat,
        moment_first.reshape(own_rows, LANES),
        moment_second.reshape(own_rows, LANES),
        tokens,
        cotangent,
        *weights,
        *vectors,
    )

    parts = 2
    cut = width // parts
    grad_tokens = None

    def piece(number, before, tie):
        pack, part = divmod(number, parts)
        rows_of = lambda w: pl.BlockSpec((rows, w), lambda i: (pack, 0))
        cut_spec = pl.BlockSpec((rows, cut), lambda i: (pack, part))
        weight_of = lambda w: pl.BlockSpec((cut, w), lambda i: (part, 0))
        held = [] if before is None else [before]
        tied, _ = lax.optimization_barrier((start, tie))
        return pl.pallas_call(
            functools.partial(token_kernel, pack),
            out_shape=result((total_rows, width), bf16),
            grid=(1,),
            in_specs=[scalars, cut_spec]
            + [rows_of(width)] * 3
            + [rows_of(LANES)]
            + [weight_of(width)] * 3
            + [weight_of(LANES)]
            + [anywhere] * len(held),
            out_specs=cut_spec,
            scratch_shapes=[pltpu.VMEM((rows // 8, 8, cut), f32)],
            input_output_aliases={10: 0} if held else {},
            compiler_params=pltpu.CompilerParams(vmem_limit_bytes=60 * 2**20),
            cost_estimate=pl.CostEstimate(
                flops=2 * rows * cut * (3 * width + LANES),
                bytes_accessed=3 * rows * width * 2 + 3 * cut * width * 2 + rows * cut * 6,
                transcendentals=0,
            ),
        )(tied, dfirst, dq, dk, dv, dl, *weights[:3], dcat, *held)

    stages = [("wide", bit) for bit in bits_of("wide")] + [("dp", bit) for bit in bits_of("dp")]
    pieces = packs * parts
    after = max(len(stages) - pieces, 0)
    done = 0
    held = grads
    for number, (axis, bit) in enumerate(stages):
        got = swap(held, axis, bit)
        if number >= after and done < pieces:
            grad_tokens = piece(done, grad_tokens, held)
            done += 1
            got, grad_tokens = lax.optimization_barrier((got, grad_tokens))
        if axis == "wide":
            held = jnp.concatenate(
                [held[:flat_rows] + got[:flat_rows], held[flat_rows:], got[flat_rows:]]
            )
        else:
            held = held + got
        if number == len(bits_of("wide")) - 1:
            moments = held[flat_rows:]
            held = held[:flat_rows]
    if not stages:
        moments, held = held[flat_rows:], held[:flat_rows]
    while done < pieces:
        grad_tokens = piece(done, grad_tokens, held)
        done += 1
    total = held

    own = result((own_rows, LANES), f32)
    vmem = pl.BlockSpec(memory_space=pltpu.VMEM)
    shaped = (shares, own_rows, LANES)
    grad_own, new_factors, new_first, new_second = pl.pallas_call(
        optimizer_kernel,
        out_shape=(own, result(shaped, f32), own, own),
        in_specs=[scalars] * 3 + [vmem] * 3,
        out_specs=[vmem] * 4,
    )(
        step_count,
        learn_rate,
        lax.axis_index("wide").astype(jnp.int32).reshape(1),
        total.reshape(shaped),
        factors.reshape(shaped),
        moments.reshape(shares, 2, own_rows, LANES),
    )
    return (
        output,
        grad_tokens,
        grad_own.reshape(-1),
        new_factors.reshape(-1),
        new_first.reshape(-1),
        new_second.reshape(-1),
    )


def solution(mesh):
    rows = P(("dp", "wide"), None)
    in_specs = (rows,) * 3 + (P(),) * 16 + (P("wide"), P("wide"), P(), P())
    out_specs = (rows, rows, P("wide"), P(), P("wide"), P("wide"))
    return jax.shard_map(shards, mesh=mesh, in_specs=in_specs, out_specs=out_specs, check_vma=False)
```

```python
import functools

import jax
import jax.numpy as jnp
from jax import lax
from jax.experimental import pallas as pl
from jax.experimental.pallas import tpu as pltpu
from jax.sharding import PartitionSpec as P

HEADS = 12
RANK = 8
BIG = 256
HEAD_DIM = 64
LANES = 128
GROUP = 3
STEP = 256
CHUNK = 512
VMEM_LIMIT = 63 * 2**20
LOG2E = 1.4426950408889634
LOG2_ROOT = 1.3257480647361592

norm_eps = 1e-05
adapter_scale = 2.0
beta_one = 0.9
beta_two = 0.999
adam_eps = 1e-08
decay_rate = 0.01
rate_ratio = 16.0

bf16 = jnp.bfloat16
f32 = jnp.float32


def dot(left, right, ca=1, cb=0):
    return lax.dot_general(left, right, (((ca,), (cb,)), ((), ())), preferred_element_type=f32)


def line(vector):
    return vector.astype(f32).reshape(1, -1)


def unpack_factors(fac_ref, dcat, uq, uv):
    width = dcat.shape[0]
    per = width * RANK // LANES
    group = LANES // RANK
    lane = lax.broadcasted_iota(jnp.int32, (width, LANES), 1)
    sub = lax.broadcasted_iota(jnp.int32, (width, LANES), 0)
    keep = (lane // RANK) == (sub % group)
    spread = []
    for which in range(2):
        flat = fac_ref[which * per : (which + 1) * per, :].astype(bf16).astype(f32)
        wide = jnp.broadcast_to(flat[:, None, :], (per, group, LANES)).reshape(width, LANES)
        wide = jnp.where(keep, wide, 0.0)
        for hop in (8, 16, 32, 64):
            wide = wide + pltpu.roll(wide, hop, 1)
        spread.append(wide)
    dcat[...] = jnp.where(lane < HEAD_DIM, *spread).astype(bf16)
    tiles = width // LANES
    none = jnp.zeros((HEAD_DIM, width), bf16)
    for which, ref in enumerate((uq, uv)):
        base = 2 * per + which * per
        block = jnp.concatenate(
            [fac_ref[pl.ds(base + j, RANK, stride=tiles), :] for j in range(tiles)], axis=1
        )
        block = (block * adapter_scale).astype(bf16)
        half = jnp.concatenate([block] * (HEAD_DIM // RANK), axis=0)
        ref[...] = jnp.concatenate([half, none] if which == 0 else [none, half], axis=0)


def pack_grads(grad_ref, gd, gq, gv):
    width = gd.shape[1]
    per = width * RANK // LANES
    group = LANES // RANK
    tiles = width // LANES
    lane = lax.broadcasted_iota(jnp.int32, (width, LANES), 1)
    sub = lax.broadcasted_iota(jnp.int32, (width, LANES), 0)
    keep = (lane // RANK) == (sub % group)
    turned = jnp.concatenate(
        [gd[:, j * LANES : (j + 1) * LANES].T for j in range(tiles)], axis=0
    )
    other = pltpu.roll(turned, HEAD_DIM, 1)
    for which, (first, second) in enumerate(((turned, other), (other, turned))):
        full = jnp.where(lane < HEAD_DIM, first, second)
        picked = jnp.where(keep, full, 0.0).reshape(per, group, LANES)
        grad_ref[which * per : (which + 1) * per, :] = jnp.sum(picked, axis=1)
    for which, block in enumerate((gq, gv)):
        base = 2 * per + which * per
        for j in range(tiles):
            grad_ref[pl.ds(base + j, RANK, stride=tiles), :] = block[:, j * LANES : (j + 1) * LANES]


def rotate_rows(src, base, count, shift, emit):
    width = src.shape[1]
    groups = count // 8
    coarse, fine = shift // 8, shift % 8
    back = lax.rem(8 - fine, 8)
    keep = lax.broadcasted_iota(jnp.int32, (8, width), 0) < 8 - fine

    def turned(i):
        at = pl.multiple_of(base + 8 * lax.rem(coarse + i, groups), 8)
        return pltpu.roll(src[pl.ds(at, 8), :], back, 0)

    spun = [turned(i) for i in range(groups + 1)]
    moved = [jnp.where(keep, spun[i], spun[i + 1]) for i in range(groups)]
    for i in range(0, groups, 2):
        emit(i * 8, jnp.concatenate([moved[i], moved[i + 1]], axis=0))


def norm_rows(z):
    mean = jnp.mean(z, axis=-1, keepdims=True)
    centered = z - mean
    spread = jnp.mean(centered * centered, axis=-1, keepdims=True)
    root = lax.rsqrt(spread + norm_eps)
    return centered * root, root


def norm_rows_back(c, n, root):
    return root * (
        c - jnp.mean(c, axis=-1, keepdims=True) - n * jnp.mean(c * n, axis=-1, keepdims=True)
    )


def main_kernel(
    side_ref,
    seg_ref,
    fac_ref,
    first_ref,
    second_ref,
    bq,
    bv,
    bo,
    g1,
    b1,
    bu,
    bd,
    g2,
    b2,
    tok_hbm,
    cot_hbm,
    wq_hbm,
    wk_hbm,
    wv_hbm,
    wo_hbm,
    wu_hbm,
    wd_hbm,
    keep_ref,
    send_ref,
    out_hbm,
    tgrad_hbm,
    wq,
    wk,
    wv,
    wo,
    wu,
    wd,
    sems,
    spin,
    xr,
    cr,
    qs,
    ks,
    vs,
    lora,
    probs,
    att,
    inv,
    zs,
    n1,
    r1,
    hb,
    act,
    gp,
    dcat,
    uq,
    uv,
    own_q,
    other_k,
    flat,
):
    packs, rows = seg_ref.shape
    total_rows, width = xr.shape
    pairs = width // LANES
    copies = []
    for src, dst in (
        (tok_hbm, xr),
        (wq_hbm, wq),
        (wk_hbm, wk),
        (wv_hbm, wv),
        (cot_hbm, cr),
        (wo_hbm, wo),
        (wu_hbm, wu),
        (wd_hbm, wd),
    ):
        copies.append(pltpu.make_async_copy(src, dst, sems.at[len(copies)]))
        copies[-1].start()

    def arrive(*which):
        for i in which:
            copies[i].wait()

    unpack_factors(fac_ref, dcat, uq, uv)

    lane = lax.broadcasted_iota(jnp.int32, (BIG, LANES), 1)
    low = lane < HEAD_DIM
    high = jnp.logical_not(low)
    used = (lane % HEAD_DIM) < 8
    none = jnp.zeros((BIG, LANES), bf16)
    ones_pair = jnp.ones((BIG, LANES), bf16)
    low_lane = lax.broadcasted_iota(jnp.int32, (1, LANES), 1) < HEAD_DIM
    slot = lax.broadcasted_iota(jnp.int32, (LANES, rows), 0) % HEAD_DIM
    ones = jnp.ones((8, rows), bf16)
    starts = []
    for pack in range(packs):
        seg = jnp.broadcast_to(seg_ref[pack : pack + 1, :], (LANES, rows))
        seg_lo = dot(ones, jnp.where(seg < slot, 1.0, 0.0).astype(bf16), 1, 1)[:1]
        seg_hi = dot(ones, jnp.where(seg <= slot, 1.0, 0.0).astype(bf16), 1, 1)[:1]
        large = low_lane & (seg_hi - seg_lo == BIG)
        start = jnp.sum(jnp.where(large, seg_lo, 0.0)).astype(jnp.int32)
        starts.append(start)
        row = lax.broadcasted_iota(jnp.int32, (BIG, LANES), 0) + (BIG + start)
        row = jnp.where(row >= rows, row - rows, row)
        inside = (row >= seg_lo.astype(jnp.int32)) & (row < seg_hi.astype(jnp.int32))
        own_q[pack] = jnp.where(inside, 1.0, 0.0).astype(bf16)
        other_k[pack] = jnp.where(used & jnp.logical_not(inside), -1e30, 0.0).astype(bf16)

    def put(dst, base):
        def emit(at, block):
            dst[pl.ds(base + at, 16), :] = block.astype(dst.dtype)

        return emit

    def turn(ref):
        for pack in range(packs):
            spin[...] = ref[pack * rows : (pack + 1) * rows, :].astype(f32)
            rotate_rows(spin, 0, rows, starts[pack], put(ref, pack * rows))

    arrive(0)
    turn(xr)

    lora[...] = dot(xr[...], dcat[...]).astype(bf16)
    narrow = lax.broadcasted_iota(jnp.int32, (total_rows, LANES), 1) % HEAD_DIM < RANK
    lora_once = jnp.where(narrow, lora[...], jnp.zeros((total_rows, LANES), bf16))
    arrive(1, 2, 3)
    for c in range(width // BIG):
        at = slice(c * BIG, (c + 1) * BIG)
        query = dot(xr[...], wq[:, at]) + dot(lora_once, uq[:, at]) + line(bq[at])
        qs[:, at] = (query * (HEAD_DIM**-0.5 * LOG2E)).astype(bf16)
        ks[:, at] = dot(xr[...], wk[:, at]).astype(bf16)
        value = dot(xr[...], wv[:, at]) + dot(lora_once, uv[:, at]) + line(bv[at])
        vs[:, at] = value.astype(bf16)

    def heads_of(turn_no):
        per = pairs // GROUP
        pack, group = turn_no // per, turn_no % per
        units = []
        for k in range(GROUP):
            pair = group * GROUP + k
            at = pl.ds(pl.multiple_of(pair * LANES, LANES), LANES)
            for block in range(2):
                span = pl.ds(pl.multiple_of(pack * rows + block * BIG, BIG), BIG)
                for half in range(2):
                    place = (pack * HEADS + 2 * pair + half) * 2 + block
                    units.append((pack, place, block, span, at, half))
        return units

    def pipeline(units, first, second, third, finish):
        count = len(units)
        begun, middle, ended = {}, {}, {}

        def close(k):
            ended[k] = third(units[k], middle.pop(k))
            if k % 2:
                finish(units[k], ended.pop(k - 1), ended.pop(k))

        for k in range(min(2, count)):
            begun[k] = first(units[k])
        for k in range(count):
            if k + 2 < count:
                begun[k + 2] = first(units[k + 2])
            middle[k] = second(units[k], begun.pop(k))
            if k:
                close(k - 1)
        close(count - 1)

    def group_forward(turn_no, carry):
        def scores(unit):
            pack, _, block, span, at, half = unit
            mine = low if half == 0 else high
            if block == 0:
                return dot(qs[span, at], jnp.where(mine, ks[span, at], none), 1, 1)
            query = jnp.where(mine, qs[span, at], own_q[pack])
            return dot(query, jnp.where(mine, ks[span, at], other_k[pack]), 1, 1)

        def soften(unit, s):
            e = jnp.exp2(s - jnp.max(s, axis=-1, keepdims=True))
            low_e = e.astype(bf16)
            probs[unit[1]] = low_e
            return low_e, jnp.sum(e, axis=-1, keepdims=True)

        def mix(unit, held):
            _, _, _, span, at, _ = unit
            return dot(held[0], vs[span, at]), held[1]

        def finish(unit, one, two):
            _, _, _, span, at, _ = unit
            scale = 1.0 / jnp.where(low, one[1], two[1])
            inv[span, at] = scale
            att[span, at] = (jnp.where(low, one[0], two[0]) * scale).astype(bf16)

        pipeline(heads_of(turn_no), scores, soften, mix, finish)
        return carry

    turns = packs * pairs // GROUP
    lax.fori_loop(0, turns, group_forward, 0)
    arrive(4)
    turn(cr)

    arrive(5)
    zs[...] = dot(att[...], wo[...])
    step = STEP

    def steps(body):
        def run(i, carry):
            body(pl.ds(pl.multiple_of(i * step, step), step))
            return carry

        lax.fori_loop(0, total_rows // step, run, 0)

    def first_norm(at):
        z = xr[at, :].astype(f32) + zs[at, :] + line(bo[...])
        n, root = norm_rows(z)
        n1[at, :] = n
        r1[at, :] = root
        hb[at, :] = (n * line(g1[...]) + line(b1[...])).astype(bf16)

    steps(first_norm)

    arrive(6)
    chunk = CHUNK
    count = act.shape[1] // chunk

    def up(c, carry):
        at = pl.ds(pl.multiple_of(c * chunk, chunk), chunk)
        u = dot(hb[...], wu[:, at]) + line(bu[at])
        z = u * (0.5**0.5)
        half_cdf = 0.5 + 0.5 * lax.erf(z)
        act[:, at] = (u * half_cdf).astype(bf16)
        bell = jnp.exp2(z * z * -LOG2E - LOG2_ROOT)
        gp[:, at] = (half_cdf + u * bell).astype(bf16)
        return carry

    lax.fori_loop(0, count, up, 0)
    arrive(7)

    def down(c, carry):
        at = pl.ds(pl.multiple_of(c * BIG, BIG), BIG)
        zs[:, at] = dot(act[...], wd[:, at])
        return carry

    lax.fori_loop(0, width // BIG, down, 0)
    results = []
    for pack in range(packs):
        for part in range(rows // step):
            at = slice(pack * rows + part * step, pack * rows + (part + 1) * step)
            hidden = n1[at, :] * line(g1[...]) + line(b1[...])
            z = hidden + zs[at, :] + line(bd[...])
            n, root = norm_rows(z)
            gain = line(g2[...])
            spin[part * step : (part + 1) * step, :] = n * gain + line(b2[...])
            d = norm_rows_back(cr[at, :].astype(f32) * gain, n, root)
            zs[at, :] = d
            hb[at, :] = d.astype(bf16)
        span = pl.ds(pack * rows, rows)
        rotate_rows(spin, 0, rows, rows - starts[pack], put(cr, pack * rows))
        results.append(
            pltpu.make_async_copy(cr.at[span, :], out_hbm.at[span, :], sems.at[8 + pack])
        )
        results[-1].start()

    def up_back(c, carry):
        at = pl.ds(pl.multiple_of(c * chunk, chunk), chunk)
        t = dot(hb[...], wd[at, :], 1, 1)
        act[:, at] = (t * gp[:, at].astype(f32)).astype(bf16)
        return carry

    lax.fori_loop(0, count, up_back, 0)

    def down_back(c, carry):
        at = pl.ds(pl.multiple_of(c * BIG, BIG), BIG)
        zs[:, at] = zs[:, at] + dot(act[...], wu[at, :], 1, 1)
        return carry

    lax.fori_loop(0, width // BIG, down_back, 0)

    def first_norm_back(at):
        d = norm_rows_back(zs[at, :] * line(g1[...]), n1[at, :], r1[at, :])
        zs[at, :] = d
        hb[at, :] = d.astype(bf16)

    steps(first_norm_back)
    for copy in results:
        copy.wait()
    cr[...] = dot(hb[...], wo[...], 1, 1).astype(bf16)

    def group_back(turn_no, carry):
        ready = {}

        def slopes(unit):
            _, _, block, span, at, half = unit
            if half == 0:
                scaled = cr[span, at].astype(f32) * inv[span, at]
                minus = pltpu.roll(-scaled * att[span, at].astype(f32), HEAD_DIM, 1)
                scaled = scaled.astype(bf16)
                ready[id(at), block] = scaled, minus.astype(bf16), scaled.T, qs[span, at].T
            scaled, minus = ready[id(at), block][:2]
            mine = low if half == 0 else high
            left = jnp.where(mine, scaled, minus)
            return dot(left, jnp.where(mine, vs[span, at], ones_pair), 1, 1)

        def weigh(unit, d):
            e = probs[unit[1]]
            return e * d.astype(bf16), e

        def grads_of(unit, held):
            _, _, block, span, at, half = unit
            ds, e = held
            _, _, scaled_t, query_t = ready[id(at), block]
            lines = slice(half * HEAD_DIM, (half + 1) * HEAD_DIM)
            return dot(ds, ks[span, at]), dot(query_t[lines], ds), dot(scaled_t[lines], e)

        def finish(unit, one, two):
            _, _, block, span, at, _ = unit
            ready.pop((id(at), block))
            qs[span, at] = (jnp.where(low, one[0], two[0]) * HEAD_DIM**-0.5).astype(bf16)
            dk = jnp.concatenate([one[1], two[1]], axis=0) * (1.0 / LOG2E)
            ks[span, at] = dk.astype(bf16).T
            vs[span, at] = jnp.concatenate([one[2], two[2]], axis=0).astype(bf16).T

        pipeline(heads_of(turn_no), slopes, weigh, grads_of, finish)
        return carry

    lax.fori_loop(0, turns, group_back, 0)

    dl = (dot(qs[...], uq[...], 1, 1) + dot(vs[...], uv[...], 1, 1)).astype(bf16)
    gd = dot(dl, xr[...], 0, 0)
    gq = adapter_scale * dot(lora[...], qs[...], 0, 0)[:RANK]
    gv = adapter_scale * dot(lora[...], vs[...], 0, 0)[HEAD_DIM : HEAD_DIM + RANK]
    pack_grads(flat, gd, gq, gv)
    half_rows = flat.shape[0] // 2
    side = side_ref[0]
    kept = flat[pl.ds(pl.multiple_of(side * half_rows, 8), half_rows), :]
    send_ref[...] = flat[pl.ds(pl.multiple_of((1 - side) * half_rows, 8), half_rows), :]
    more = first_ref.shape[0]
    keep_ref[:half_rows, :] = kept
    keep_ref[half_rows : half_rows + more, :] = first_ref[...]
    keep_ref[half_rows + more :, :] = second_ref[...]

    dl_once = jnp.where(narrow, dl, jnp.zeros((total_rows, LANES), bf16))
    for c in range(width // BIG):
        at = slice(c * BIG, (c + 1) * BIG)
        term = dot(qs[...], wq[at, :], 1, 1) + dot(ks[...], wk[at, :], 1, 1)
        term = term + dot(vs[...], wv[at, :], 1, 1) + dot(dl_once, dcat[at, :], 1, 1)
        zs[:, at] = zs[:, at] + term
    results = []
    for pack in range(packs):
        span = pl.ds(pack * rows, rows)
        rotate_rows(zs, pack * rows, rows, rows - starts[pack], put(hb, pack * rows))
        results.append(
            pltpu.make_async_copy(hb.at[span, :], tgrad_hbm.at[span, :], sems.at[8 + pack])
        )
        results[-1].start()
    for copy in results:
        copy.wait()


def optimizer_kernel(places, *refs):
    steps_ref, rate_ref, place_ref, held, other, params = refs[:6]
    grad_out, new_params, first_out, second_out, total = refs[6:]
    shares, own_rows = params.shape[:2]
    half = shares // 2
    place = place_ref[0]
    side = place & 1
    total[side] = held[:half]
    total[1 - side] = other[:half]
    norm_sq = jnp.sum(jnp.sum(total[...] * total[...], axis=(0, 1)), keepdims=True)
    clip = jnp.minimum(1.0, lax.rsqrt(norm_sq + 1e-06))

    def power(base):
        return lax.fori_loop(0, steps_ref[0], lambda _, value: value * base, jnp.float32(1.0))

    shape = (own_rows, LANES)
    fix_one = jnp.full(shape, 1.0 - power(beta_one), f32)
    fix_two = jnp.full(shape, 1.0 - power(beta_two), f32)
    grad_out[...] = total[place // half, place % half]
    for j, mask in enumerate(places + [mask ^ 1 for mask in places]):
        source, at = (held, half + 2 * j) if j < half else (other, half + 2 * (j - half))
        share = place ^ mask
        clipped = total[share // half, share % half] * clip
        first = beta_one * source[at] + (1.0 - beta_one) * clipped
        second = beta_two * source[at + 1] + (1.0 - beta_two) * clipped * clipped
        if j == 0:
            first_out[...] = first
            second_out[...] = second
        before = params[share]
        update = first / fix_one / (jnp.sqrt(second / fix_two) + adam_eps) + decay_rate * before
        rate = rate_ref[0] * jnp.where(share < half, 1.0, rate_ratio)
        new_params[share] = before - rate * update


def swap(x, axis, bit):
    n = lax.axis_size(axis)
    return lax.ppermute(x, axis, [(i, i ^ bit) for i in range(n)])


def bits_of(axis):
    n = lax.axis_size(axis)
    return [1 << k for k in range(n.bit_length() - 1)]


def shards(
    tokens,
    segment_ids,
    cotangent,
    query_frozen_weight,
    query_bias_vector,
    w_key,
    value_frozen_weight,
    value_bias_vector,
    w_out,
    b_out,
    norm1_gain,
    norm1_bias,
    w_up,
    b_up,
    w_down,
    b_down,
    norm2_gain,
    norm2_bias,
    factors,
    moment_first,
    moment_second,
    step_count,
    learn_rate,
):
    width = tokens.shape[1]
    packs, rows = segment_ids.shape
    ff = w_up.shape[1]
    total_rows = packs * rows
    flat_rows = factors.shape[0] // LANES
    shares = lax.axis_size("wide")
    own_rows = flat_rows // shares
    half_rows = flat_rows // 2
    place = lax.axis_index("wide").astype(jnp.int32)

    whole = pl.BlockSpec(memory_space=pltpu.VMEM)
    anywhere = pl.BlockSpec(memory_space=pl.ANY)
    scalars = pl.BlockSpec(memory_space=pltpu.SMEM)
    result = lambda shape, dtype: jax.ShapeDtypeStruct(shape, dtype)
    weights = (query_frozen_weight, w_key, value_frozen_weight, w_out, w_up, w_down)
    vectors = (
        query_bias_vector,
        value_bias_vector,
        b_out,
        norm1_gain,
        norm1_bias,
        b_up,
        b_down,
        norm2_gain,
        norm2_bias,
    )
    tall = lambda dtype: pltpu.VMEM((total_rows, width), dtype)
    kept, sent, output, grad_tokens = pl.pallas_call(
        main_kernel,
        out_shape=(
            result((half_rows + 2 * own_rows, LANES), f32),
            result((half_rows, LANES), f32),
            result((total_rows, width), bf16),
            result((total_rows, width), bf16),
        ),
        in_specs=[scalars] + [whole] * (4 + len(vectors)) + [anywhere] * 8,
        out_specs=[whole, whole, anywhere, anywhere],
        scratch_shapes=[pltpu.VMEM(w.shape, bf16) for w in weights]
        + [
            pltpu.SemaphoreType.DMA((8 + packs,)),
            pltpu.VMEM((rows, width), f32),
            tall(bf16),
            tall(bf16),
            tall(bf16),
            tall(bf16),
            tall(bf16),
            pltpu.VMEM((total_rows, LANES), bf16),
            pltpu.VMEM((packs * HEADS * 2, BIG, BIG), bf16),
            tall(bf16),
            tall(f32),
            tall(f32),
            tall(f32),
            pltpu.VMEM((total_rows, 1), f32),
            tall(bf16),
            pltpu.VMEM((total_rows, ff), bf16),
            pltpu.VMEM((total_rows, ff), bf16),
            pltpu.VMEM((width, LANES), bf16),
            pltpu.VMEM((LANES, width), bf16),
            pltpu.VMEM((LANES, width), bf16),
            pltpu.VMEM((packs, BIG, LANES), bf16),
            pltpu.VMEM((packs, BIG, LANES), bf16),
            pltpu.VMEM((flat_rows, LANES), f32),
        ],
        compiler_params=pltpu.CompilerParams(vmem_limit_bytes=VMEM_LIMIT),
    )(
        (place & 1).reshape(1),
        segment_ids,
        factors.reshape(flat_rows, LANES),
        moment_first.reshape(own_rows, LANES),
        moment_second.reshape(own_rows, LANES),
        *vectors,
        tokens,
        cotangent,
        *weights,
    )

    held = kept.at[:half_rows].add(swap(sent, "wide", 1))
    bits = bits_of("wide")[1:]
    places = [0]
    while bits:
        now, bits = bits[:2], bits[2:]
        masks = [now[0]] if len(now) == 1 else [now[0], now[1], now[0] | now[1]]
        got = [swap(held, "wide", mask) for mask in masks]
        if len(got) == 1:
            total = held[:half_rows] + got[0][:half_rows]
        else:
            total = (held[:half_rows] + got[0][:half_rows]) + (
                got[1][:half_rows] + got[2][:half_rows]
            )
        places = places + [old ^ mask for mask in masks for old in places]
        if bits:
            held = jnp.concatenate([total] + [part[half_rows:] for part in [held] + got])
        else:
            moments = [part[half_rows:] for part in [held] + got]
    for bit in bits_of("dp"):
        total = total + swap(total, "dp", bit)
    held = jnp.concatenate([total] + moments)
    other = swap(held, "wide", 1)

    own = result((own_rows, LANES), f32)
    shaped = (shares, own_rows, LANES)
    grad_own, new_factors, new_first, new_second = pl.pallas_call(
        functools.partial(optimizer_kernel, places),
        out_shape=(own, result(shaped, f32), own, own),
        in_specs=[scalars] * 3 + [whole] * 3,
        out_specs=[whole] * 4,
        scratch_shapes=[pltpu.VMEM((2, shares // 2, own_rows, LANES), f32)],
    )(
        step_count,
        learn_rate,
        place.reshape(1),
        held.reshape(-1, own_rows, LANES),
        other.reshape(-1, own_rows, LANES),
        factors.reshape(shaped),
    )
    return (
        output,
        grad_tokens,
        grad_own.reshape(-1),
        new_factors.reshape(-1),
        new_first.reshape(-1),
        new_second.reshape(-1),
    )


def solution(mesh):
    rows = P(("dp", "wide"), None)
    in_specs = (rows,) * 3 + (P(),) * 16 + (P("wide"), P("wide"), P(), P())
    out_specs = (rows, rows, P("wide"), P(), P("wide"), P("wide"))
    return jax.shard_map(shards, mesh=mesh, in_specs=in_specs, out_specs=out_specs, check_vma=False)
```

```python
import functools

import jax
import jax.numpy as jnp
from jax import lax
from jax.experimental import pallas as pl
from jax.experimental.pallas import tpu as pltpu
from jax.sharding import PartitionSpec as P

HEADS = 12
RANK = 8
BIG = 256
HEAD_DIM = 64
LANES = 128
GROUP = 6
STEP = 256
CHUNK = 768
VMEM_LIMIT = 50 * 2**20
LOG2E = 1.4426950408889634
LOG2_ROOT = 1.3257480647361592

norm_eps = 1e-05
adapter_scale = 2.0
beta_one = 0.9
beta_two = 0.999
adam_eps = 1e-08
decay_rate = 0.01
rate_ratio = 16.0

bf16 = jnp.bfloat16
f32 = jnp.float32


def dot(left, right, ca=1, cb=0):
    return lax.dot_general(left, right, (((ca,), (cb,)), ((), ())), preferred_element_type=f32)


def line(vector):
    return vector.astype(f32).reshape(1, -1)


def unpack_factors(fac_ref, dcat, uq, uv):
    width = dcat.shape[0]
    per = width * RANK // LANES
    group = LANES // RANK
    lane = lax.broadcasted_iota(jnp.int32, (width, LANES), 1)
    sub = lax.broadcasted_iota(jnp.int32, (width, LANES), 0)
    keep = (lane // RANK) == (sub % group)
    spread = []
    for which in range(2):
        flat = fac_ref[which * per : (which + 1) * per, :].astype(bf16).astype(f32)
        wide = jnp.broadcast_to(flat[:, None, :], (per, group, LANES)).reshape(width, LANES)
        wide = jnp.where(keep, wide, 0.0)
        for hop in (8, 16, 32, 64):
            wide = wide + pltpu.roll(wide, hop, 1)
        spread.append(wide)
    dcat[...] = jnp.where(lane < HEAD_DIM, *spread).astype(bf16)
    tiles = width // LANES
    none = jnp.zeros((HEAD_DIM, width), bf16)
    for which, ref in enumerate((uq, uv)):
        base = 2 * per + which * per
        block = jnp.concatenate(
            [fac_ref[pl.ds(base + j, RANK, stride=tiles), :] for j in range(tiles)], axis=1
        )
        block = (block * adapter_scale).astype(bf16)
        half = jnp.concatenate([block] * (HEAD_DIM // RANK), axis=0)
        ref[...] = jnp.concatenate([half, none] if which == 0 else [none, half], axis=0)


def pack_grads(grad_ref, gd, gq, gv):
    width = gd.shape[1]
    per = width * RANK // LANES
    group = LANES // RANK
    tiles = width // LANES
    lane = lax.broadcasted_iota(jnp.int32, (width, LANES), 1)
    sub = lax.broadcasted_iota(jnp.int32, (width, LANES), 0)
    keep = (lane // RANK) == (sub % group)
    turned = jnp.concatenate(
        [gd[:, j * LANES : (j + 1) * LANES].T for j in range(tiles)], axis=0
    )
    other = pltpu.roll(turned, HEAD_DIM, 1)
    for which, (first, second) in enumerate(((turned, other), (other, turned))):
        full = jnp.where(lane < HEAD_DIM, first, second)
        picked = jnp.where(keep, full, 0.0).reshape(per, group, LANES)
        grad_ref[which * per : (which + 1) * per, :] = jnp.sum(picked, axis=1)
    for which, block in enumerate((gq, gv)):
        base = 2 * per + which * per
        for j in range(tiles):
            grad_ref[pl.ds(base + j, RANK, stride=tiles), :] = block[:, j * LANES : (j + 1) * LANES]


def rotate_rows(src, base, count, shift, emit):
    width = src.shape[1]
    groups = count // 8
    coarse, fine = shift // 8, shift % 8
    back = lax.rem(8 - fine, 8)
    keep = lax.broadcasted_iota(jnp.int32, (8, width), 0) < 8 - fine

    def turned(i):
        at = pl.multiple_of(base + 8 * lax.rem(coarse + i, groups), 8)
        return pltpu.roll(src[pl.ds(at, 8), :], back, 0)

    spun = [turned(i) for i in range(groups + 1)]
    moved = [jnp.where(keep, spun[i], spun[i + 1]) for i in range(groups)]
    for i in range(0, groups, 2):
        emit(i * 8, jnp.concatenate([moved[i], moved[i + 1]], axis=0))


def norm_rows(z):
    mean = jnp.mean(z, axis=-1, keepdims=True)
    centered = z - mean
    spread = jnp.mean(centered * centered, axis=-1, keepdims=True)
    root = lax.rsqrt(spread + norm_eps)
    return centered * root, root


def norm_rows_back(c, n, root):
    return root * (
        c - jnp.mean(c, axis=-1, keepdims=True) - n * jnp.mean(c * n, axis=-1, keepdims=True)
    )


def main_kernel(
    side_ref,
    seg_ref,
    fac_ref,
    first_ref,
    second_ref,
    bq,
    bv,
    bo,
    g1,
    b1,
    bu,
    bd,
    g2,
    b2,
    tok_hbm,
    cot_hbm,
    wq_hbm,
    wk_hbm,
    wv_hbm,
    wo_hbm,
    wu_hbm,
    wd_hbm,
    keep_ref,
    send_ref,
    out_hbm,
    start_ref,
    wq,
    wk,
    wv,
    dcat,
    act,
    zs,
    dl_once,
    wo,
    wu,
    wd,
    sems,
    spin,
    xr,
    cr,
    qs,
    ks,
    vs,
    lora,
    probs,
    att,
    inv,
    n1,
    r1,
    hb,
    gp,
    uq,
    uv,
    own_q,
    other_k,
    flat,
):
    packs, rows = seg_ref.shape
    total_rows, width = xr.shape
    pairs = width // LANES
    copies = []
    for src, dst in (
        (tok_hbm, xr),
        (wq_hbm, wq),
        (wk_hbm, wk),
        (wv_hbm, wv),
        (cot_hbm, cr),
        (wo_hbm, wo),
        (wu_hbm, wu),
        (wd_hbm, wd),
    ):
        copies.append(pltpu.make_async_copy(src, dst, sems.at[len(copies)]))
        copies[-1].start()

    def arrive(*which):
        for i in which:
            copies[i].wait()

    unpack_factors(fac_ref, dcat, uq, uv)

    lane = lax.broadcasted_iota(jnp.int32, (BIG, LANES), 1)
    low = lane < HEAD_DIM
    high = jnp.logical_not(low)
    used = (lane % HEAD_DIM) < 8
    none = jnp.zeros((BIG, LANES), bf16)
    ones_pair = jnp.ones((BIG, LANES), bf16)
    low_lane = lax.broadcasted_iota(jnp.int32, (1, LANES), 1) < HEAD_DIM
    slot = lax.broadcasted_iota(jnp.int32, (LANES, rows), 0) % HEAD_DIM
    ones = jnp.ones((8, rows), bf16)
    starts = []
    for pack in range(packs):
        seg = jnp.broadcast_to(seg_ref[pack : pack + 1, :], (LANES, rows))
        seg_lo = dot(ones, jnp.where(seg < slot, 1.0, 0.0).astype(bf16), 1, 1)[:1]
        seg_hi = dot(ones, jnp.where(seg <= slot, 1.0, 0.0).astype(bf16), 1, 1)[:1]
        large = low_lane & (seg_hi - seg_lo == BIG)
        start = jnp.sum(jnp.where(large, seg_lo, 0.0)).astype(jnp.int32)
        starts.append(start)
        start_ref[pack] = start
        row = lax.broadcasted_iota(jnp.int32, (BIG, LANES), 0) + (BIG + start)
        row = jnp.where(row >= rows, row - rows, row)
        inside = (row >= seg_lo.astype(jnp.int32)) & (row < seg_hi.astype(jnp.int32))
        own_q[pack] = jnp.where(inside, 1.0, 0.0).astype(bf16)
        other_k[pack] = jnp.where(used & jnp.logical_not(inside), -1e30, 0.0).astype(bf16)

    def put(dst, base):
        def emit(at, block):
            dst[pl.ds(base + at, 16), :] = block.astype(dst.dtype)

        return emit

    def turn(ref):
        for pack in range(packs):
            spin[...] = ref[pack * rows : (pack + 1) * rows, :].astype(f32)
            rotate_rows(spin, 0, rows, starts[pack], put(ref, pack * rows))

    arrive(0)
    turn(xr)

    lora[...] = dot(xr[...], dcat[...]).astype(bf16)
    narrow = lax.broadcasted_iota(jnp.int32, (total_rows, LANES), 1) % HEAD_DIM < RANK
    lora_once = jnp.where(narrow, lora[...], jnp.zeros((total_rows, LANES), bf16))
    arrive(1, 2, 3)
    for c in range(width // BIG):
        at = slice(c * BIG, (c + 1) * BIG)
        query = dot(xr[...], wq[:, at]) + dot(lora_once, uq[:, at]) + line(bq[at])
        qs[:, at] = (query * (HEAD_DIM**-0.5 * LOG2E)).astype(bf16)
        ks[:, at] = dot(xr[...], wk[:, at]).astype(bf16)
        value = dot(xr[...], wv[:, at]) + dot(lora_once, uv[:, at]) + line(bv[at])
        vs[:, at] = value.astype(bf16)

    def heads_of(turn_no):
        per = pairs // GROUP
        pack, group = turn_no // per, turn_no % per
        units = []
        for k in range(GROUP):
            pair = group * GROUP + k
            at = pl.ds(pl.multiple_of(pair * LANES, LANES), LANES)
            for block in range(2):
                span = pl.ds(pl.multiple_of(pack * rows + block * BIG, BIG), BIG)
                for half in range(2):
                    place = (pack * HEADS + 2 * pair + half) * 2 + block
                    units.append((pack, place, block, span, at, half))
        return units

    def pipeline(units, first, second, third, finish):
        count = len(units)
        begun, middle, ended = {}, {}, {}

        def close(k):
            ended[k] = third(units[k], middle.pop(k))
            if k % 2:
                finish(units[k], ended.pop(k - 1), ended.pop(k))

        for k in range(min(2, count)):
            begun[k] = first(units[k])
        for k in range(count):
            if k + 2 < count:
                begun[k + 2] = first(units[k + 2])
            middle[k] = second(units[k], begun.pop(k))
            if k:
                close(k - 1)
        close(count - 1)

    def group_forward(turn_no, carry):
        def scores(unit):
            pack, _, block, span, at, half = unit
            mine = low if half == 0 else high
            if block == 0:
                return dot(qs[span, at], jnp.where(mine, ks[span, at], none), 1, 1)
            query = jnp.where(mine, qs[span, at], own_q[pack])
            return dot(query, jnp.where(mine, ks[span, at], other_k[pack]), 1, 1)

        def soften(unit, s):
            e = jnp.exp2(s - jnp.max(s, axis=-1, keepdims=True))
            low_e = e.astype(bf16)
            probs[unit[1]] = low_e
            return low_e, jnp.sum(e, axis=-1, keepdims=True)

        def mix(unit, held):
            _, _, _, span, at, _ = unit
            return dot(held[0], vs[span, at]), held[1]

        def finish(unit, one, two):
            _, _, _, span, at, _ = unit
            scale = 1.0 / jnp.where(low, one[1], two[1])
            inv[span, at] = scale
            att[span, at] = (jnp.where(low, one[0], two[0]) * scale).astype(bf16)

        pipeline(heads_of(turn_no), scores, soften, mix, finish)
        return carry

    turns = packs * pairs // GROUP
    lax.fori_loop(0, turns, group_forward, 0)
    arrive(4)
    turn(cr)

    arrive(5)
    zs[...] = dot(att[...], wo[...])
    step = STEP

    def steps(body):
        def run(i, carry):
            body(pl.ds(pl.multiple_of(i * step, step), step))
            return carry

        lax.fori_loop(0, total_rows // step, run, 0)

    def first_norm(at):
        z = xr[at, :].astype(f32) + zs[at, :] + line(bo[...])
        n, root = norm_rows(z)
        n1[at, :] = n
        r1[at, :] = root
        hb[at, :] = (n * line(g1[...]) + line(b1[...])).astype(bf16)

    steps(first_norm)

    arrive(6)
    chunk = CHUNK
    count = act.shape[1] // chunk

    def up(c, carry):
        at = pl.ds(pl.multiple_of(c * chunk, chunk), chunk)
        u = dot(hb[...], wu[:, at]) + line(bu[at])
        z = u * (0.5**0.5)
        half_cdf = 0.5 + 0.5 * lax.erf(z)
        act[:, at] = (u * half_cdf).astype(bf16)
        bell = jnp.exp2(z * z * -LOG2E - LOG2_ROOT)
        gp[:, at] = (half_cdf + u * bell).astype(bf16)
        return carry

    lax.fori_loop(0, count, up, 0)
    arrive(7)

    def down(c, carry):
        at = pl.ds(pl.multiple_of(c * BIG, BIG), BIG)
        zs[:, at] = dot(act[...], wd[:, at])
        return carry

    lax.fori_loop(0, width // BIG, down, 0)
    results = []
    for pack in range(packs):
        for part in range(rows // step):
            at = slice(pack * rows + part * step, pack * rows + (part + 1) * step)
            hidden = n1[at, :] * line(g1[...]) + line(b1[...])
            z = hidden + zs[at, :] + line(bd[...])
            n, root = norm_rows(z)
            gain = line(g2[...])
            spin[part * step : (part + 1) * step, :] = n * gain + line(b2[...])
            d = norm_rows_back(cr[at, :].astype(f32) * gain, n, root)
            zs[at, :] = d
            hb[at, :] = d.astype(bf16)
        span = pl.ds(pack * rows, rows)
        rotate_rows(spin, 0, rows, rows - starts[pack], put(cr, pack * rows))
        results.append(
            pltpu.make_async_copy(cr.at[span, :], out_hbm.at[span, :], sems.at[8 + pack])
        )
        results[-1].start()

    def up_back(c, carry):
        at = pl.ds(pl.multiple_of(c * chunk, chunk), chunk)
        t = dot(hb[...], wd[at, :], 1, 1)
        act[:, at] = (t * gp[:, at].astype(f32)).astype(bf16)
        return carry

    lax.fori_loop(0, count, up_back, 0)

    def down_back(c, carry):
        at = pl.ds(pl.multiple_of(c * BIG, BIG), BIG)
        zs[:, at] = zs[:, at] + dot(act[...], wu[at, :], 1, 1)
        return carry

    lax.fori_loop(0, width // BIG, down_back, 0)

    def first_norm_back(at):
        d = norm_rows_back(zs[at, :] * line(g1[...]), n1[at, :], r1[at, :])
        zs[at, :] = d
        hb[at, :] = d.astype(bf16)

    steps(first_norm_back)
    for copy in results:
        copy.wait()
    cr[...] = dot(hb[...], wo[...], 1, 1).astype(bf16)

    dq, dk, dv = (act.at[:, k * width : (k + 1) * width] for k in range(3))

    def group_back(turn_no, carry):
        ready = {}

        def slopes(unit):
            _, _, block, span, at, half = unit
            if half == 0:
                scaled = cr[span, at].astype(f32) * inv[span, at]
                minus = pltpu.roll(-scaled * att[span, at].astype(f32), HEAD_DIM, 1)
                scaled = scaled.astype(bf16)
                ready[id(at), block] = scaled, minus.astype(bf16), scaled.T, qs[span, at].T
            scaled, minus = ready[id(at), block][:2]
            mine = low if half == 0 else high
            left = jnp.where(mine, scaled, minus)
            return dot(left, jnp.where(mine, vs[span, at], ones_pair), 1, 1)

        def weigh(unit, d):
            e = probs[unit[1]]
            return e * d.astype(bf16), e

        def grads_of(unit, held):
            _, _, block, span, at, half = unit
            ds, e = held
            _, _, scaled_t, query_t = ready[id(at), block]
            lines = slice(half * HEAD_DIM, (half + 1) * HEAD_DIM)
            return dot(ds, ks[span, at]), dot(query_t[lines], ds), dot(scaled_t[lines], e)

        def finish(unit, one, two):
            _, _, block, span, at, _ = unit
            ready.pop((id(at), block))
            dq[span, at] = (jnp.where(low, one[0], two[0]) * HEAD_DIM**-0.5).astype(bf16)
            turned = jnp.concatenate([one[1], two[1]], axis=0) * (1.0 / LOG2E)
            dk[span, at] = turned.astype(bf16).T
            dv[span, at] = jnp.concatenate([one[2], two[2]], axis=0).astype(bf16).T

        pipeline(heads_of(turn_no), slopes, weigh, grads_of, finish)
        return carry

    lax.fori_loop(0, turns, group_back, 0)

    dl = (dot(dq[...], uq[...], 1, 1) + dot(dv[...], uv[...], 1, 1)).astype(bf16)
    gd = dot(dl, xr[...], 0, 0)
    gq = adapter_scale * dot(lora[...], dq[...], 0, 0)[:RANK]
    gv = adapter_scale * dot(lora[...], dv[...], 0, 0)[HEAD_DIM : HEAD_DIM + RANK]
    pack_grads(flat, gd, gq, gv)
    half_rows = flat.shape[0] // 2
    side = side_ref[0]
    kept = flat[pl.ds(pl.multiple_of(side * half_rows, 8), half_rows), :]
    send_ref[...] = flat[pl.ds(pl.multiple_of((1 - side) * half_rows, 8), half_rows), :]
    more = first_ref.shape[0]
    keep_ref[:half_rows, :] = kept
    keep_ref[half_rows : half_rows + more, :] = first_ref[...]
    keep_ref[half_rows + more :, :] = second_ref[...]

    dl_once[...] = jnp.where(narrow, dl, jnp.zeros((total_rows, LANES), bf16))


def token_kernel(begin, start_ref, wq, wk, wv, dcat, grads, first, dl_once, *rest):
    out_hbm, total, stage, sems = rest[-4:]
    total_rows, cut = total.shape
    packs = start_ref.shape[0]
    rows = total_rows // packs
    width = first.shape[1]
    for c in range(cut // BIG):
        here = slice(c * BIG, (c + 1) * BIG)
        at = slice(begin + c * BIG, begin + (c + 1) * BIG)
        term = first[:, at] + dot(dl_once[...], dcat[at, :], 1, 1)
        for k, weight in enumerate((wq, wk, wv)):
            term = term + dot(grads[:, k * width : (k + 1) * width], weight[at, :], 1, 1)
        total[:, here] = term
    copies = []
    for pack in range(packs):
        span = pl.ds(pack * rows, rows)

        def emit(at, block, base=pack * rows):
            stage[pl.ds(base + at, 16), :] = block.astype(bf16)

        rotate_rows(total, pack * rows, rows, rows - start_ref[pack], emit)
        to = out_hbm.at[span, begin : begin + cut]
        copies.append(pltpu.make_async_copy(stage.at[span, :], to, sems.at[pack]))
        copies[-1].start()
    for copy in copies:
        copy.wait()


def optimizer_kernel(places, *refs):
    steps_ref, rate_ref, place_ref, held, other, params = refs[:6]
    grad_out, new_params, first_out, second_out, total = refs[6:]
    shares, own_rows = params.shape[:2]
    half = shares // 2
    place = place_ref[0]
    side = place & 1
    total[side] = held[:half]
    total[1 - side] = other[:half]
    norm_sq = jnp.sum(jnp.sum(total[...] * total[...], axis=(0, 1)), keepdims=True)
    clip = jnp.minimum(1.0, lax.rsqrt(norm_sq + 1e-06))

    def power(base):
        return lax.fori_loop(0, steps_ref[0], lambda _, value: value * base, jnp.float32(1.0))

    shape = (own_rows, LANES)
    fix_one = jnp.full(shape, 1.0 - power(beta_one), f32)
    fix_two = jnp.full(shape, 1.0 - power(beta_two), f32)
    grad_out[...] = total[place // half, place % half]
    for j, mask in enumerate(places + [mask ^ 1 for mask in places]):
        source, at = (held, half + 2 * j) if j < half else (other, half + 2 * (j - half))
        share = place ^ mask
        clipped = total[share // half, share % half] * clip
        first = beta_one * source[at] + (1.0 - beta_one) * clipped
        second = beta_two * source[at + 1] + (1.0 - beta_two) * clipped * clipped
        if j == 0:
            first_out[...] = first
            second_out[...] = second
        before = params[share]
        update = first / fix_one / (jnp.sqrt(second / fix_two) + adam_eps) + decay_rate * before
        rate = rate_ref[0] * jnp.where(share < half, 1.0, rate_ratio)
        new_params[share] = before - rate * update


def swap(x, axis, bit):
    n = lax.axis_size(axis)
    return lax.ppermute(x, axis, [(i, i ^ bit) for i in range(n)])


def bits_of(axis):
    n = lax.axis_size(axis)
    return [1 << k for k in range(n.bit_length() - 1)]


def shards(
    tokens,
    segment_ids,
    cotangent,
    query_frozen_weight,
    query_bias_vector,
    w_key,
    value_frozen_weight,
    value_bias_vector,
    w_out,
    b_out,
    norm1_gain,
    norm1_bias,
    w_up,
    b_up,
    w_down,
    b_down,
    norm2_gain,
    norm2_bias,
    factors,
    moment_first,
    moment_second,
    step_count,
    learn_rate,
):
    width = tokens.shape[1]
    packs, rows = segment_ids.shape
    ff = w_up.shape[1]
    total_rows = packs * rows
    flat_rows = factors.shape[0] // LANES
    shares = lax.axis_size("wide")
    own_rows = flat_rows // shares
    half_rows = flat_rows // 2
    place = lax.axis_index("wide").astype(jnp.int32)

    whole = pl.BlockSpec(memory_space=pltpu.VMEM)
    anywhere = pl.BlockSpec(memory_space=pl.ANY)
    scalars = pl.BlockSpec(memory_space=pltpu.SMEM)
    result = lambda shape, dtype: jax.ShapeDtypeStruct(shape, dtype)
    weights = (query_frozen_weight, w_key, value_frozen_weight, w_out, w_up, w_down)
    vectors = (
        query_bias_vector,
        value_bias_vector,
        b_out,
        norm1_gain,
        norm1_bias,
        b_up,
        b_down,
        norm2_gain,
        norm2_bias,
    )
    tall = lambda dtype: pltpu.VMEM((total_rows, width), dtype)
    kept, sent, output, *for_tokens = pl.pallas_call(
        main_kernel,
        out_shape=(
            result((half_rows + 2 * own_rows, LANES), f32),
            result((half_rows, LANES), f32),
            result((total_rows, width), bf16),
            result((packs,), jnp.int32),
            *[pltpu.VMEM((width, width), bf16)] * 3,
            pltpu.VMEM((width, LANES), bf16),
            pltpu.VMEM((total_rows, ff), bf16),
            tall(f32),
            pltpu.VMEM((total_rows, LANES), bf16),
        ),
        in_specs=[scalars] + [whole] * (4 + len(vectors)) + [anywhere] * 8,
        out_specs=[whole, whole, anywhere, scalars] + [whole] * 7,
        scratch_shapes=[pltpu.VMEM(w.shape, bf16) for w in weights[3:]]
        + [
            pltpu.SemaphoreType.DMA((8 + packs,)),
            pltpu.VMEM((rows, width), f32),
            tall(bf16),
            tall(bf16),
            tall(bf16),
            tall(bf16),
            tall(bf16),
            pltpu.VMEM((total_rows, LANES), bf16),
            pltpu.VMEM((packs * HEADS * 2, BIG, BIG), bf16),
            tall(bf16),
            tall(f32),
            tall(f32),
            pltpu.VMEM((total_rows, 1), f32),
            tall(bf16),
            pltpu.VMEM((total_rows, ff), bf16),
            pltpu.VMEM((LANES, width), bf16),
            pltpu.VMEM((LANES, width), bf16),
            pltpu.VMEM((packs, BIG, LANES), bf16),
            pltpu.VMEM((packs, BIG, LANES), bf16),
            pltpu.VMEM((flat_rows, LANES), f32),
        ],
        compiler_params=pltpu.CompilerParams(vmem_limit_bytes=VMEM_LIMIT),
    )(
        (place & 1).reshape(1),
        segment_ids,
        factors.reshape(flat_rows, LANES),
        moment_first.reshape(own_rows, LANES),
        moment_second.reshape(own_rows, LANES),
        *vectors,
        tokens,
        cotangent,
        *weights,
    )

    def token_piece(begin, cut, before, tie):
        held = [] if before is None else [before]
        start, _ = lax.optimization_barrier((for_tokens[0], tie))
        return pl.pallas_call(
            functools.partial(token_kernel, begin),
            out_shape=result((total_rows, width), bf16),
            in_specs=[scalars] + [whole] * 7 + [anywhere] * len(held),
            out_specs=anywhere,
            scratch_shapes=[
                pltpu.VMEM((total_rows, cut), f32),
                pltpu.VMEM((total_rows, cut), bf16),
                pltpu.SemaphoreType.DMA((packs,)),
            ],
            input_output_aliases={8: 0} if held else {},
            compiler_params=pltpu.CompilerParams(vmem_limit_bytes=16 * 2**20),
            cost_estimate=pl.CostEstimate(
                flops=2 * total_rows * cut * (3 * width + LANES),
                bytes_accessed=total_rows * cut * 2,
                transcendentals=0,
            ),
        )(start, *for_tokens[1:], *held)

    held = kept.at[:half_rows].add(swap(sent, "wide", 1))
    bits = bits_of("wide")[1:]
    places = [0]
    grad_tokens = None
    while bits:
        now, bits = bits[:2], bits[2:]
        masks = [now[0]] if len(now) == 1 else [now[0], now[1], now[0] | now[1]]
        got = [swap(held, "wide", mask) for mask in masks]
        if grad_tokens is None:
            grad_tokens = token_piece(0, width - BIG, None, held)
            grad_tokens, *got = lax.optimization_barrier((grad_tokens, *got))
        if len(got) == 1:
            total = held[:half_rows] + got[0][:half_rows]
        else:
            total = (held[:half_rows] + got[0][:half_rows]) + (
                got[1][:half_rows] + got[2][:half_rows]
            )
        places = places + [old ^ mask for mask in masks for old in places]
        if bits:
            held = jnp.concatenate([total] + [part[half_rows:] for part in [held] + got])
        else:
            moments = [part[half_rows:] for part in [held] + got]
    for k, bit in enumerate(bits_of("dp")):
        got = swap(total, "dp", bit)
        if k == 0:
            grad_tokens = token_piece(width - BIG, BIG, grad_tokens, total)
            grad_tokens, got = lax.optimization_barrier((grad_tokens, got))
        total = total + got
    held = jnp.concatenate([total] + moments)
    other = swap(held, "wide", 1)

    own = result((own_rows, LANES), f32)
    shaped = (shares, own_rows, LANES)
    grad_own, new_factors, new_first, new_second = pl.pallas_call(
        functools.partial(optimizer_kernel, places),
        out_shape=(own, result(shaped, f32), own, own),
        in_specs=[scalars] * 3 + [whole] * 3,
        out_specs=[whole] * 4,
        scratch_shapes=[pltpu.VMEM((2, shares // 2, own_rows, LANES), f32)],
    )(
        step_count,
        learn_rate,
        place.reshape(1),
        held.reshape(-1, own_rows, LANES),
        other.reshape(-1, own_rows, LANES),
        factors.reshape(shaped),
    )
    return (
        output,
        grad_tokens,
        grad_own.reshape(-1),
        new_factors.reshape(-1),
        new_first.reshape(-1),
        new_second.reshape(-1),
    )


def solution(mesh):
    rows = P(("dp", "wide"), None)
    in_specs = (rows,) * 3 + (P(),) * 16 + (P("wide"), P("wide"), P(), P())
    out_specs = (rows, rows, P("wide"), P(), P("wide"), P("wide"))
    return jax.shard_map(shards, mesh=mesh, in_specs=in_specs, out_specs=out_specs, check_vma=False)
```

```python
import functools

import jax
import jax.numpy as jnp
from jax import lax
from jax.experimental import pallas as pl
from jax.experimental.pallas import tpu as pltpu
from jax.sharding import PartitionSpec as P

HEADS = 12
RANK = 8
BIG = 256
HEAD_DIM = 64
LANES = 128
GROUP = 6
STEP = 256
CHUNK = 768
VMEM_LIMIT = 199 * 2**18
LOG2E = 1.4426950408889634
LOG2_ROOT = 1.3257480647361592

norm_eps = 1e-05
adapter_scale = 2.0
beta_one = 0.9
beta_two = 0.999
adam_eps = 1e-08
decay_rate = 0.01
rate_ratio = 16.0

bf16 = jnp.bfloat16
f32 = jnp.float32


def dot(left, right, ca=1, cb=0):
    return lax.dot_general(left, right, (((ca,), (cb,)), ((), ())), preferred_element_type=f32)


def line(vector):
    return vector.astype(f32).reshape(1, -1)


def unpack_factors(fac_ref, dcat, uq, uv):
    width = dcat.shape[0]
    per = width * RANK // LANES
    group = LANES // RANK
    lane = lax.broadcasted_iota(jnp.int32, (width, LANES), 1)
    sub = lax.broadcasted_iota(jnp.int32, (width, LANES), 0)
    keep = (lane // RANK) == (sub % group)
    spread = []
    for which in range(2):
        flat = fac_ref[which * per : (which + 1) * per, :].astype(bf16).astype(f32)
        wide = jnp.broadcast_to(flat[:, None, :], (per, group, LANES)).reshape(width, LANES)
        wide = jnp.where(keep, wide, 0.0)
        for hop in (8, 16, 32, 64):
            wide = wide + pltpu.roll(wide, hop, 1)
        spread.append(wide)
    dcat[...] = jnp.where(lane < HEAD_DIM, *spread).astype(bf16)
    tiles = width // LANES
    none = jnp.zeros((HEAD_DIM, width), bf16)
    for which, ref in enumerate((uq, uv)):
        base = 2 * per + which * per
        block = jnp.concatenate(
            [fac_ref[pl.ds(base + j, RANK, stride=tiles), :] for j in range(tiles)], axis=1
        )
        block = (block * adapter_scale).astype(bf16)
        half = jnp.concatenate([block] * (HEAD_DIM // RANK), axis=0)
        ref[...] = jnp.concatenate([half, none] if which == 0 else [none, half], axis=0)


def pack_grads(grad_ref, gd, gq, gv):
    width = gd.shape[1]
    per = width * RANK // LANES
    group = LANES // RANK
    tiles = width // LANES
    lane = lax.broadcasted_iota(jnp.int32, (width, LANES), 1)
    sub = lax.broadcasted_iota(jnp.int32, (width, LANES), 0)
    keep = (lane // RANK) == (sub % group)
    turned = jnp.concatenate(
        [gd[:, j * LANES : (j + 1) * LANES].T for j in range(tiles)], axis=0
    )
    other = pltpu.roll(turned, HEAD_DIM, 1)
    for which, (first, second) in enumerate(((turned, other), (other, turned))):
        full = jnp.where(lane < HEAD_DIM, first, second)
        picked = jnp.where(keep, full, 0.0).reshape(per, group, LANES)
        grad_ref[which * per : (which + 1) * per, :] = jnp.sum(picked, axis=1)
    for which, block in enumerate((gq, gv)):
        base = 2 * per + which * per
        for j in range(tiles):
            grad_ref[pl.ds(base + j, RANK, stride=tiles), :] = block[:, j * LANES : (j + 1) * LANES]


def rotate_rows(src, base, count, shift, emit):
    width = src.shape[1]
    groups = count // 8
    coarse, fine = shift // 8, shift % 8
    back = lax.rem(8 - fine, 8)
    keep = lax.broadcasted_iota(jnp.int32, (8, width), 0) < 8 - fine

    def turned(i):
        at = pl.multiple_of(base + 8 * lax.rem(coarse + i, groups), 8)
        return pltpu.roll(src[pl.ds(at, 8), :].astype(f32), back, 0)

    spun = [turned(i) for i in range(groups + 1)]
    moved = [jnp.where(keep, spun[i], spun[i + 1]) for i in range(groups)]
    for i in range(0, groups, 2):
        emit(i * 8, jnp.concatenate([moved[i], moved[i + 1]], axis=0))


def norm_rows(z):
    mean = jnp.mean(z, axis=-1, keepdims=True)
    centered = z - mean
    spread = jnp.mean(centered * centered, axis=-1, keepdims=True)
    root = lax.rsqrt(spread + norm_eps)
    return centered * root, root


def norm_rows_back(c, n, root):
    return root * (
        c - jnp.mean(c, axis=-1, keepdims=True) - n * jnp.mean(c * n, axis=-1, keepdims=True)
    )


def main_kernel(
    side_ref,
    seg_ref,
    fac_ref,
    first_ref,
    second_ref,
    bq,
    bv,
    bo,
    g1,
    b1,
    bu,
    bd,
    g2,
    b2,
    tok_hbm,
    cot_hbm,
    wq_hbm,
    wk_hbm,
    wv_hbm,
    wo_hbm,
    wu_hbm,
    wd_hbm,
    keep_ref,
    send_ref,
    out_hbm,
    start_ref,
    wcat,
    act,
    zs,
    wo,
    wu,
    wd,
    sems,
    xr,
    cr,
    qs,
    ks,
    vs,
    lora,
    probs,
    att,
    inv,
    n1,
    r1,
    hb,
    gp,
    uq,
    uv,
    own_q,
    other_k,
    flat,
):
    packs, rows = seg_ref.shape
    total_rows, width = xr.shape
    pairs = width // LANES
    wq, wk, wv = (wcat.at[:, k * width : (k + 1) * width] for k in range(3))
    dcat = wcat.at[:, 3 * width :]
    raw_tokens = act.at[:, :width]
    raw_cotangent = act.at[:, width : 2 * width]
    copies = []
    for src, dst in (
        (tok_hbm, raw_tokens),
        (wq_hbm, wq),
        (wk_hbm, wk),
        (wv_hbm, wv),
        (cot_hbm, raw_cotangent),
        (wo_hbm, wo),
        (wu_hbm, wu),
        (wd_hbm, wd),
    ):
        copies.append(pltpu.make_async_copy(src, dst, sems.at[len(copies)]))
        copies[-1].start()

    def arrive(*which):
        for i in which:
            copies[i].wait()

    unpack_factors(fac_ref, dcat, uq, uv)

    lane = lax.broadcasted_iota(jnp.int32, (BIG, LANES), 1)
    low = lane < HEAD_DIM
    high = jnp.logical_not(low)
    used = (lane % HEAD_DIM) < 8
    none = jnp.zeros((BIG, LANES), bf16)
    ones_pair = jnp.ones((BIG, LANES), bf16)
    low_lane = lax.broadcasted_iota(jnp.int32, (1, LANES), 1) < HEAD_DIM
    slot = lax.broadcasted_iota(jnp.int32, (LANES, rows), 0) % HEAD_DIM
    ones = jnp.ones((8, rows), bf16)
    starts = []
    for pack in range(packs):
        seg = jnp.broadcast_to(seg_ref[pack : pack + 1, :], (LANES, rows))
        seg_lo = dot(ones, jnp.where(seg < slot, 1.0, 0.0).astype(bf16), 1, 1)[:1]
        seg_hi = dot(ones, jnp.where(seg <= slot, 1.0, 0.0).astype(bf16), 1, 1)[:1]
        large = low_lane & (seg_hi - seg_lo == BIG)
        start = jnp.sum(jnp.where(large, seg_lo, 0.0)).astype(jnp.int32)
        starts.append(start)
        start_ref[pack : pack + 1, :] = jnp.full((1, LANES), start.astype(f32))
        row = lax.broadcasted_iota(jnp.int32, (BIG, LANES), 0) + (BIG + start)
        row = jnp.where(row >= rows, row - rows, row)
        inside = (row >= seg_lo.astype(jnp.int32)) & (row < seg_hi.astype(jnp.int32))
        own_q[pack] = jnp.where(inside, 1.0, 0.0).astype(bf16)
        other_k[pack] = jnp.where(used & jnp.logical_not(inside), -1e30, 0.0).astype(bf16)

    def put(dst, base):
        def emit(at, block):
            dst[pl.ds(base + at, 16), :] = block.astype(dst.dtype)

        return emit

    def turn(src, dst):
        for pack in range(packs):
            rotate_rows(src, pack * rows, rows, starts[pack], put(dst, pack * rows))

    arrive(0)
    turn(raw_tokens, xr)

    lora[...] = dot(xr[...], dcat[...]).astype(bf16)
    narrow = lax.broadcasted_iota(jnp.int32, (total_rows, LANES), 1) % HEAD_DIM < RANK
    lora_once = jnp.where(narrow, lora[...], jnp.zeros((total_rows, LANES), bf16))
    arrive(1, 2, 3)
    for c in range(width // BIG):
        at = slice(c * BIG, (c + 1) * BIG)
        query = dot(xr[...], wq[:, at]) + dot(lora_once, uq[:, at]) + line(bq[at])
        qs[:, at] = (query * (HEAD_DIM**-0.5 * LOG2E)).astype(bf16)
        ks[:, at] = dot(xr[...], wk[:, at]).astype(bf16)
        value = dot(xr[...], wv[:, at]) + dot(lora_once, uv[:, at]) + line(bv[at])
        vs[:, at] = value.astype(bf16)

    def heads_of(turn_no):
        per = pairs // GROUP
        pack, group = turn_no // per, turn_no % per
        units = []
        for k in range(GROUP):
            pair = group * GROUP + k
            at = pl.ds(pl.multiple_of(pair * LANES, LANES), LANES)
            for block in range(2):
                span = pl.ds(pl.multiple_of(pack * rows + block * BIG, BIG), BIG)
                for half in range(2):
                    place = (pack * HEADS + 2 * pair + half) * 2 + block
                    units.append((pack, place, block, span, at, half))
        return units

    def pipeline(units, first, second, third, finish):
        count = len(units)
        begun, middle, ended = {}, {}, {}

        def close(k):
            ended[k] = third(units[k], middle.pop(k))
            if k % 2:
                finish(units[k], ended.pop(k - 1), ended.pop(k))

        for k in range(min(2, count)):
            begun[k] = first(units[k])
        for k in range(count):
            if k + 2 < count:
                begun[k + 2] = first(units[k + 2])
            middle[k] = second(units[k], begun.pop(k))
            if k:
                close(k - 1)
        close(count - 1)

    def group_forward(turn_no, carry):
        def scores(unit):
            pack, _, block, span, at, half = unit
            mine = low if half == 0 else high
            if block == 0:
                return dot(qs[span, at], jnp.where(mine, ks[span, at], none), 1, 1)
            query = jnp.where(mine, qs[span, at], own_q[pack])
            return dot(query, jnp.where(mine, ks[span, at], other_k[pack]), 1, 1)

        def soften(unit, s):
            e = jnp.exp2(s - jnp.max(s, axis=-1, keepdims=True))
            low_e = e.astype(bf16)
            probs[unit[1]] = low_e
            return low_e, jnp.sum(e, axis=-1, keepdims=True)

        def mix(unit, held):
            _, _, _, span, at, _ = unit
            return dot(held[0], vs[span, at]), held[1]

        def finish(unit, one, two):
            _, _, _, span, at, _ = unit
            scale = 1.0 / jnp.where(low, one[1], two[1])
            inv[span, at] = scale
            att[span, at] = (jnp.where(low, one[0], two[0]) * scale).astype(bf16)

        pipeline(heads_of(turn_no), scores, soften, mix, finish)
        return carry

    turns = packs * pairs // GROUP
    lax.fori_loop(0, turns, group_forward, 0)

    arrive(4, 5)
    halves = [slice(pack * rows, (pack + 1) * rows) for pack in range(packs)]
    for at in halves:
        zs[at, :] = dot(att[at, :], wo[...])
    step = STEP

    def pieces_of(at):
        return [slice(k, k + step) for k in range(at.start, at.stop, step)]

    for half in halves:
        for at in pieces_of(half):
            z = xr[at, :].astype(f32) + zs[at, :] + line(bo[...])
            n, root = norm_rows(z)
            n1[at, :] = n
            r1[at, :] = root
            hb[at, :] = (n * line(g1[...]) + line(b1[...])).astype(bf16)
    turn(raw_cotangent, cr)

    arrive(6)
    chunk = CHUNK
    count = act.shape[1] // chunk

    def up(c, carry):
        at = pl.ds(pl.multiple_of(c * chunk, chunk), chunk)
        u = dot(hb[...], wu[:, at]) + line(bu[at])
        z = u * (0.5**0.5)
        half_cdf = 0.5 + 0.5 * lax.erf(z)
        act[:, at] = (u * half_cdf).astype(bf16)
        bell = jnp.exp2(z * z * -LOG2E - LOG2_ROOT)
        gp[:, at] = (half_cdf + u * bell).astype(bf16)
        return carry

    lax.fori_loop(0, count, up, 0)
    arrive(7)

    for half in halves:
        for c in range(width // BIG):
            at = slice(c * BIG, (c + 1) * BIG)
            zs[half, at] = dot(act[half, :], wd[:, at])
    results = []
    for pack in range(packs):
        for at in pieces_of(halves[pack]):
            hidden = n1[at, :] * line(g1[...]) + line(b1[...])
            z = hidden + zs[at, :] + line(bd[...])
            n, root = norm_rows(z)
            gain = line(g2[...])
            raw_tokens[at, :] = (n * gain + line(b2[...])).astype(bf16)
            d = norm_rows_back(cr[at, :].astype(f32) * gain, n, root)
            zs[at, :] = d
            hb[at, :] = d.astype(bf16)
        span = pl.ds(pack * rows, rows)
        rotate_rows(raw_tokens, pack * rows, rows, rows - starts[pack], put(cr, pack * rows))
        results.append(
            pltpu.make_async_copy(cr.at[span, :], out_hbm.at[span, :], sems.at[8 + pack])
        )
        results[-1].start()

    def up_back(c, carry):
        at = pl.ds(pl.multiple_of(c * chunk, chunk), chunk)
        t = dot(hb[...], wd[at, :], 1, 1)
        act[:, at] = (t * gp[:, at].astype(f32)).astype(bf16)
        return carry

    lax.fori_loop(0, count, up_back, 0)

    def down_back(c, carry):
        at = pl.ds(pl.multiple_of(c * BIG, BIG), BIG)
        zs[:, at] = zs[:, at] + dot(act[...], wu[at, :], 1, 1)
        return carry

    lax.fori_loop(0, width // BIG, down_back, 0)

    for copy in results:
        copy.wait()
    for half in halves:
        for at in pieces_of(half):
            d = norm_rows_back(zs[at, :] * line(g1[...]), n1[at, :], r1[at, :])
            zs[at, :] = d
            hb[at, :] = d.astype(bf16)
        cr[half, :] = dot(hb[half, :], wo[...], 1, 1).astype(bf16)

    dq, dk, dv = (act.at[:, k * width : (k + 1) * width] for k in range(3))

    def group_back(turn_no, carry):
        ready = {}

        def slopes(unit):
            _, _, block, span, at, half = unit
            if half == 0:
                scaled = cr[span, at].astype(f32) * inv[span, at]
                minus = pltpu.roll(-scaled * att[span, at].astype(f32), HEAD_DIM, 1)
                scaled = scaled.astype(bf16)
                ready[id(at), block] = scaled, minus.astype(bf16), scaled.T, qs[span, at].T
            scaled, minus = ready[id(at), block][:2]
            mine = low if half == 0 else high
            left = jnp.where(mine, scaled, minus)
            return dot(left, jnp.where(mine, vs[span, at], ones_pair), 1, 1)

        def weigh(unit, d):
            e = probs[unit[1]]
            return e * d.astype(bf16), e

        def grads_of(unit, held):
            _, _, block, span, at, half = unit
            ds, e = held
            _, _, scaled_t, query_t = ready[id(at), block]
            lines = slice(half * HEAD_DIM, (half + 1) * HEAD_DIM)
            return dot(ds, ks[span, at]), dot(query_t[lines], ds), dot(scaled_t[lines], e)

        def finish(unit, one, two):
            _, _, block, span, at, _ = unit
            ready.pop((id(at), block))
            dq[span, at] = (jnp.where(low, one[0], two[0]) * HEAD_DIM**-0.5).astype(bf16)
            turned = jnp.concatenate([one[1], two[1]], axis=0) * (1.0 / LOG2E)
            dk[span, at] = turned.astype(bf16).T
            dv[span, at] = jnp.concatenate([one[2], two[2]], axis=0).astype(bf16).T

        pipeline(heads_of(turn_no), slopes, weigh, grads_of, finish)
        return carry

    lax.fori_loop(0, turns, group_back, 0)

    dl = (dot(dq[...], uq[...], 1, 1) + dot(dv[...], uv[...], 1, 1)).astype(bf16)
    gd = dot(dl, xr[...], 0, 0)
    gq = adapter_scale * dot(lora[...], dq[...], 0, 0)[:RANK]
    gv = adapter_scale * dot(lora[...], dv[...], 0, 0)[HEAD_DIM : HEAD_DIM + RANK]
    pack_grads(flat, gd, gq, gv)
    half_rows = flat.shape[0] // 2
    side = side_ref[0]
    kept = flat[pl.ds(pl.multiple_of(side * half_rows, 8), half_rows), :]
    more = first_ref.shape[0]
    send_ref[:half_rows, :] = flat[pl.ds(pl.multiple_of((1 - side) * half_rows, 8), half_rows), :]
    send_ref[half_rows:, :] = jnp.zeros((2 * more, LANES), f32)
    keep_ref[:half_rows, :] = kept
    keep_ref[half_rows : half_rows + more, :] = first_ref[...]
    keep_ref[half_rows + more :, :] = second_ref[...]

    act[:, 3 * width : 3 * width + LANES] = jnp.where(
        narrow, dl, jnp.zeros((total_rows, LANES), bf16)
    )


def token_kernel(begin, start_ref, wcat, grads, first, *rest):
    out_hbm, total, stage, sems = rest[-4:]
    total_rows, cut = total.shape
    packs = start_ref.shape[0]
    rows = total_rows // packs
    depth = wcat.shape[1]
    for c in range(cut // BIG):
        at = slice(begin + c * BIG, begin + (c + 1) * BIG)
        term = dot(grads[:, :depth], wcat[at, :], 1, 1)
        total[:, c * BIG : (c + 1) * BIG] = first[:, at] + term
    copies = []
    for pack in range(packs):
        span = pl.ds(pack * rows, rows)

        def emit(at, block, base=pack * rows):
            stage[pl.ds(base + at, 16), :] = block.astype(bf16)

        start = jnp.max(start_ref[pack : pack + 1, :]).astype(jnp.int32)
        rotate_rows(total, pack * rows, rows, rows - start, emit)
        to = out_hbm.at[span, begin : begin + cut]
        copies.append(pltpu.make_async_copy(stage.at[span, :], to, sems.at[pack]))
        copies[-1].start()
    for copy in copies:
        copy.wait()


def optimizer_kernel(places, *refs):
    steps_ref, rate_ref, place_ref, held, other, params = refs[:6]
    grad_out, new_params, first_out, second_out, total = refs[6:]
    shares, own_rows = params.shape[:2]
    half = shares // 2
    place = place_ref[0]
    side = place & 1
    for k in range(half):
        at = slice(k * own_rows, (k + 1) * own_rows)
        total[side, k] = held[at, :]
        total[1 - side, k] = other[at, :]
    norm_sq = jnp.sum(jnp.sum(total[...] * total[...], axis=(0, 1)), keepdims=True)
    clip = jnp.minimum(1.0, lax.rsqrt(norm_sq + 1e-06))

    def power(base):
        return lax.fori_loop(0, steps_ref[0], lambda _, value: value * base, jnp.float32(1.0))

    shape = (own_rows, LANES)
    fix_one = jnp.full(shape, 1.0 - power(beta_one), f32)
    fix_two = jnp.full(shape, 1.0 - power(beta_two), f32)
    grad_out[...] = total[place // half, place % half]
    for j, mask in enumerate(places + [mask ^ 1 for mask in places]):
        source, at = (held, half + 2 * j) if j < half else (other, half + 2 * (j - half))
        moment = source[at * own_rows : (at + 1) * own_rows, :]
        square = source[(at + 1) * own_rows : (at + 2) * own_rows, :]
        share = place ^ mask
        clipped = total[share // half, share % half] * clip
        first = beta_one * moment + (1.0 - beta_one) * clipped
        second = beta_two * square + (1.0 - beta_two) * clipped * clipped
        if j == 0:
            first_out[...] = first
            second_out[...] = second
        before = params[share]
        update = first / fix_one / (jnp.sqrt(second / fix_two) + adam_eps) + decay_rate * before
        rate = rate_ref[0] * jnp.where(share < half, 1.0, rate_ratio)
        new_params[share] = before - rate * update


def swap(x, axis, bit):
    n = lax.axis_size(axis)
    return lax.ppermute(x, axis, [(i, i ^ bit) for i in range(n)])


def bits_of(axis):
    n = lax.axis_size(axis)
    return [1 << k for k in range(n.bit_length() - 1)]


def shards(
    tokens,
    segment_ids,
    cotangent,
    query_frozen_weight,
    query_bias_vector,
    w_key,
    value_frozen_weight,
    value_bias_vector,
    w_out,
    b_out,
    norm1_gain,
    norm1_bias,
    w_up,
    b_up,
    w_down,
    b_down,
    norm2_gain,
    norm2_bias,
    factors,
    moment_first,
    moment_second,
    step_count,
    learn_rate,
):
    width = tokens.shape[1]
    packs, rows = segment_ids.shape
    ff = w_up.shape[1]
    total_rows = packs * rows
    flat_rows = factors.shape[0] // LANES
    shares = lax.axis_size("wide")
    own_rows = flat_rows // shares
    half_rows = flat_rows // 2
    place = lax.axis_index("wide").astype(jnp.int32)

    whole = pl.BlockSpec(memory_space=pltpu.VMEM)
    anywhere = pl.BlockSpec(memory_space=pl.ANY)
    scalars = pl.BlockSpec(memory_space=pltpu.SMEM)
    result = lambda shape, dtype: jax.ShapeDtypeStruct(shape, dtype)
    weights = (query_frozen_weight, w_key, value_frozen_weight, w_out, w_up, w_down)
    vectors = (
        query_bias_vector,
        value_bias_vector,
        b_out,
        norm1_gain,
        norm1_bias,
        b_up,
        b_down,
        norm2_gain,
        norm2_bias,
    )
    tall = lambda dtype: pltpu.VMEM((total_rows, width), dtype)
    kept, sent, output, *for_tokens = pl.pallas_call(
        main_kernel,
        out_shape=(
            pltpu.VMEM((half_rows + 2 * own_rows, LANES), f32),
            pltpu.VMEM((half_rows + 2 * own_rows, LANES), f32),
            result((total_rows, width), bf16),
            pltpu.VMEM((packs, LANES), f32),
            pltpu.VMEM((width, 3 * width + LANES), bf16),
            pltpu.VMEM((total_rows, ff), bf16),
            tall(f32),
        ),
        in_specs=[scalars] + [whole] * (4 + len(vectors)) + [anywhere] * 8,
        out_specs=[whole, whole, anywhere] + [whole] * 4,
        scratch_shapes=[pltpu.VMEM(w.shape, bf16) for w in weights[3:]]
        + [
            pltpu.SemaphoreType.DMA((8 + packs,)),
            tall(bf16),
            tall(bf16),
            tall(bf16),
            tall(bf16),
            tall(bf16),
            pltpu.VMEM((total_rows, LANES), bf16),
            pltpu.VMEM((packs * HEADS * 2, BIG, BIG), bf16),
            tall(bf16),
            tall(f32),
            tall(f32),
            pltpu.VMEM((total_rows, 1), f32),
            tall(bf16),
            pltpu.VMEM((total_rows, ff), bf16),
            pltpu.VMEM((LANES, width), bf16),
            pltpu.VMEM((LANES, width), bf16),
            pltpu.VMEM((packs, BIG, LANES), bf16),
            pltpu.VMEM((packs, BIG, LANES), bf16),
            pltpu.VMEM((flat_rows, LANES), f32),
        ],
        compiler_params=pltpu.CompilerParams(vmem_limit_bytes=VMEM_LIMIT),
    )(
        (place & 1).reshape(1),
        segment_ids,
        factors.reshape(flat_rows, LANES),
        moment_first.reshape(own_rows, LANES),
        moment_second.reshape(own_rows, LANES),
        *vectors,
        tokens,
        cotangent,
        *weights,
    )

    def token_piece(begin, cut, before, tie):
        held = [] if before is None else [before]
        start, _ = lax.optimization_barrier((for_tokens[0], tie))
        return pl.pallas_call(
            functools.partial(token_kernel, begin),
            out_shape=result((total_rows, width), bf16),
            in_specs=[whole] * 4 + [anywhere] * len(held),
            out_specs=anywhere,
            scratch_shapes=[
                pltpu.VMEM((total_rows, cut), f32),
                pltpu.VMEM((total_rows, cut), bf16),
                pltpu.SemaphoreType.DMA((packs,)),
            ],
            input_output_aliases={4: 0} if held else {},
            compiler_params=pltpu.CompilerParams(vmem_limit_bytes=16 * 2**20),
            cost_estimate=pl.CostEstimate(
                flops=2 * total_rows * cut * (3 * width + LANES),
                bytes_accessed=total_rows * cut * 2,
                transcendentals=0,
            ),
        )(start, *for_tokens[1:], *held)

    held = kept + swap(sent, "wide", 1)
    bits = bits_of("wide")[1:]
    places = [0]
    grad_tokens = None
    while bits:
        now, bits = bits[:2], bits[2:]
        masks = [now[0]] if len(now) == 1 else [now[0], now[1], now[0] | now[1]]
        got = [swap(held, "wide", mask) for mask in masks]
        if grad_tokens is None:
            grad_tokens = token_piece(0, width - BIG, None, held)
            grad_tokens, *got = lax.optimization_barrier((grad_tokens, *got))
        if len(got) == 1:
            total = held[:half_rows] + got[0][:half_rows]
        else:
            total = (held[:half_rows] + got[0][:half_rows]) + (
                got[1][:half_rows] + got[2][:half_rows]
            )
        places = places + [old ^ mask for mask in masks for old in places]
        if bits:
            held = jnp.concatenate([total] + [part[half_rows:] for part in [held] + got])
        else:
            moments = [part[half_rows:] for part in [held] + got]
    for bit in bits_of("dp"):
        got = swap(total, "dp", bit)
        if bit == bits_of("dp")[-1]:
            grad_tokens = token_piece(width - BIG, BIG, grad_tokens, total)
            grad_tokens, got = lax.optimization_barrier((grad_tokens, got))
        total = total + got
    held = jnp.concatenate([total] + moments)
    other = swap(held, "wide", 1)

    own = result((own_rows, LANES), f32)
    shaped = (shares, own_rows, LANES)
    grad_own, new_factors, new_first, new_second = pl.pallas_call(
        functools.partial(optimizer_kernel, places),
        out_shape=(own, result(shaped, f32), own, own),
        in_specs=[scalars] * 3 + [whole] * 3,
        out_specs=[whole] * 4,
        scratch_shapes=[pltpu.VMEM((2, shares // 2, own_rows, LANES), f32)],
    )(
        step_count,
        learn_rate,
        place.reshape(1),
        held,
        other,
        factors.reshape(shaped),
    )
    return (
        output,
        grad_tokens,
        grad_own.reshape(-1),
        new_factors.reshape(-1),
        new_first.reshape(-1),
        new_second.reshape(-1),
    )


def solution(mesh):
    rows = P(("dp", "wide"), None)
    in_specs = (rows,) * 3 + (P(),) * 16 + (P("wide"), P("wide"), P(), P())
    out_specs = (rows, rows, P("wide"), P(), P("wide"), P("wide"))
    return jax.shard_map(shards, mesh=mesh, in_specs=in_specs, out_specs=out_specs, check_vma=False)
```

```python
import functools

import jax
import jax.numpy as jnp
from jax import lax
from jax.experimental import pallas as pl
from jax.experimental.pallas import tpu as pltpu
from jax.sharding import PartitionSpec as P

HEADS = 12
RANK = 8
BIG = 256
HEAD_DIM = 64
LANES = 128
GROUP = 6
STEP = 256
CHUNK = 768
VMEM_LIMIT = 199 * 2**18
LOG2E = 1.4426950408889634
LOG2_ROOT = 1.3257480647361592

norm_eps = 1e-05
adapter_scale = 2.0
beta_one = 0.9
beta_two = 0.999
adam_eps = 1e-08
decay_rate = 0.01
rate_ratio = 16.0

bf16 = jnp.bfloat16
f32 = jnp.float32


def dot(left, right, ca=1, cb=0):
    return lax.dot_general(left, right, (((ca,), (cb,)), ((), ())), preferred_element_type=f32)


def line(vector):
    return vector.astype(f32).reshape(1, -1)


def unpack_factors(fac_ref, dcat, uq, uv):
    width = dcat.shape[0]
    per = width * RANK // LANES
    group = LANES // RANK
    lane = lax.broadcasted_iota(jnp.int32, (width, LANES), 1)
    sub = lax.broadcasted_iota(jnp.int32, (width, LANES), 0)
    keep = (lane // RANK) == (sub % group)
    spread = []
    for which in range(2):
        flat = fac_ref[which * per : (which + 1) * per, :].astype(bf16).astype(f32)
        wide = jnp.broadcast_to(flat[:, None, :], (per, group, LANES)).reshape(width, LANES)
        wide = jnp.where(keep, wide, 0.0)
        for hop in (8, 16, 32, 64):
            wide = wide + pltpu.roll(wide, hop, 1)
        spread.append(wide)
    dcat[...] = jnp.where(lane < HEAD_DIM, *spread).astype(bf16)
    tiles = width // LANES
    none = jnp.zeros((HEAD_DIM, width), bf16)
    for which, ref in enumerate((uq, uv)):
        base = 2 * per + which * per
        block = jnp.concatenate(
            [fac_ref[pl.ds(base + j, RANK, stride=tiles), :] for j in range(tiles)], axis=1
        )
        block = (block * adapter_scale).astype(bf16)
        half = jnp.concatenate([block] * (HEAD_DIM // RANK), axis=0)
        ref[...] = jnp.concatenate([half, none] if which == 0 else [none, half], axis=0)


def pack_grads(grad_ref, gd, gq, gv):
    width = gd.shape[1]
    per = width * RANK // LANES
    group = LANES // RANK
    tiles = width // LANES
    lane = lax.broadcasted_iota(jnp.int32, (width, LANES), 1)
    sub = lax.broadcasted_iota(jnp.int32, (width, LANES), 0)
    keep = (lane // RANK) == (sub % group)
    turned = jnp.concatenate(
        [gd[:, j * LANES : (j + 1) * LANES].T for j in range(tiles)], axis=0
    )
    other = pltpu.roll(turned, HEAD_DIM, 1)
    for which, (first, second) in enumerate(((turned, other), (other, turned))):
        full = jnp.where(lane < HEAD_DIM, first, second)
        picked = jnp.where(keep, full, 0.0).reshape(per, group, LANES)
        grad_ref[which * per : (which + 1) * per, :] = jnp.sum(picked, axis=1)
    for which, block in enumerate((gq, gv)):
        base = 2 * per + which * per
        for j in range(tiles):
            grad_ref[pl.ds(base + j, RANK, stride=tiles), :] = block[:, j * LANES : (j + 1) * LANES]


def rotate_rows(src, base, count, shift, emit):
    width = src.shape[1]
    groups = count // 8
    coarse, fine = shift // 8, shift % 8
    back = lax.rem(8 - fine, 8)
    keep = lax.broadcasted_iota(jnp.int32, (8, width), 0) < 8 - fine

    def turned(i):
        at = pl.multiple_of(base + 8 * lax.rem(coarse + i, groups), 8)
        return pltpu.roll(src[pl.ds(at, 8), :].astype(f32), back, 0)

    spun = [turned(i) for i in range(groups + 1)]
    moved = [jnp.where(keep, spun[i], spun[i + 1]) for i in range(groups)]
    for i in range(0, groups, 2):
        emit(i * 8, jnp.concatenate([moved[i], moved[i + 1]], axis=0))


def norm_rows(z):
    mean = jnp.mean(z, axis=-1, keepdims=True)
    centered = z - mean
    spread = jnp.mean(centered * centered, axis=-1, keepdims=True)
    root = lax.rsqrt(spread + norm_eps)
    return centered * root, root


def norm_rows_back(c, n, root):
    return root * (
        c - jnp.mean(c, axis=-1, keepdims=True) - n * jnp.mean(c * n, axis=-1, keepdims=True)
    )


def main_kernel(
    side_ref,
    seg_ref,
    fac_ref,
    first_ref,
    second_ref,
    bq,
    bv,
    bo,
    g1,
    b1,
    bu,
    bd,
    g2,
    b2,
    tok_hbm,
    cot_hbm,
    wq_hbm,
    wk_hbm,
    wv_hbm,
    wo_hbm,
    wu_hbm,
    wd_hbm,
    keep_ref,
    send_ref,
    out_hbm,
    start_ref,
    wcat,
    act,
    zs,
    wo,
    wu,
    wd,
    sems,
    xr,
    cr,
    qs,
    ks,
    vs,
    lora,
    probs,
    att,
    inv,
    n1,
    r1,
    hb,
    gp,
    uq,
    uv,
    own_q,
    other_k,
    flat,
):
    packs, rows = seg_ref.shape
    total_rows, width = xr.shape
    pairs = width // LANES
    wq, wk, wv = (wcat.at[:, k * width : (k + 1) * width] for k in range(3))
    dcat = wcat.at[:, 3 * width :]
    raw_tokens = act.at[:, :width]
    raw_cotangent = act.at[:, width : 2 * width]
    copies = []
    for src, dst in (
        (tok_hbm, raw_tokens),
        (wq_hbm, wq),
        (wk_hbm, wk),
        (wv_hbm, wv),
        (cot_hbm, raw_cotangent),
        (wo_hbm, wo),
        (wu_hbm, wu),
        (wd_hbm, wd),
    ):
        copies.append(pltpu.make_async_copy(src, dst, sems.at[len(copies)]))

    def depart(*which):
        for i in which:
            copies[i].start()

    def arrive(*which):
        for i in which:
            copies[i].wait()

    depart(0, 1)

    unpack_factors(fac_ref, dcat, uq, uv)

    lane = lax.broadcasted_iota(jnp.int32, (BIG, LANES), 1)
    low = lane < HEAD_DIM
    high = jnp.logical_not(low)
    used = (lane % HEAD_DIM) < 8
    none = jnp.zeros((BIG, LANES), bf16)
    ones_pair = jnp.ones((BIG, LANES), bf16)
    low_lane = lax.broadcasted_iota(jnp.int32, (1, LANES), 1) < HEAD_DIM
    slot = lax.broadcasted_iota(jnp.int32, (LANES, rows), 0) % HEAD_DIM
    ones = jnp.ones((8, rows), bf16)
    starts = []
    for pack in range(packs):
        seg = jnp.broadcast_to(seg_ref[pack : pack + 1, :], (LANES, rows))
        seg_lo = dot(ones, jnp.where(seg < slot, 1.0, 0.0).astype(bf16), 1, 1)[:1]
        seg_hi = dot(ones, jnp.where(seg <= slot, 1.0, 0.0).astype(bf16), 1, 1)[:1]
        large = low_lane & (seg_hi - seg_lo == BIG)
        start = jnp.sum(jnp.where(large, seg_lo, 0.0)).astype(jnp.int32)
        starts.append(start)
        start_ref[pack : pack + 1, :] = jnp.full((1, LANES), start.astype(f32))
        row = lax.broadcasted_iota(jnp.int32, (BIG, LANES), 0) + (BIG + start)
        row = jnp.where(row >= rows, row - rows, row)
        inside = (row >= seg_lo.astype(jnp.int32)) & (row < seg_hi.astype(jnp.int32))
        own_q[pack] = jnp.where(inside, 1.0, 0.0).astype(bf16)
        other_k[pack] = jnp.where(used & jnp.logical_not(inside), -1e30, 0.0).astype(bf16)

    def put(dst, base):
        def emit(at, block):
            dst[pl.ds(base + at, 16), :] = block.astype(dst.dtype)

        return emit

    def turn(src, dst):
        for pack in range(packs):
            rotate_rows(src, pack * rows, rows, starts[pack], put(dst, pack * rows))

    arrive(0)
    depart(2, 3)
    turn(raw_tokens, xr)

    lora[...] = dot(xr[...], dcat[...]).astype(bf16)
    narrow = lax.broadcasted_iota(jnp.int32, (total_rows, LANES), 1) % HEAD_DIM < RANK
    once = att.at[:, :LANES]
    once[...] = jnp.where(narrow, lora[...], jnp.zeros((total_rows, LANES), bf16))
    columns = [slice(c * BIG, (c + 1) * BIG) for c in range(width // BIG)]
    arrive(1)
    def by_columns(body):
        def run(c, carry):
            body(pl.ds(pl.multiple_of(c * BIG, BIG), BIG))
            return carry

        lax.fori_loop(0, width // BIG, run, 0)

    def project_query(at):
        query = dot(xr[...], wq[:, at]) + dot(once[...], uq[:, at]) + line(bq[at])
        qs[:, at] = (query * (HEAD_DIM**-0.5 * LOG2E)).astype(bf16)

    by_columns(project_query)
    arrive(2, 3)
    depart(4, 5, 6, 7)
    def project_rest(at):
        ks[:, at] = dot(xr[...], wk[:, at]).astype(bf16)
        value = dot(xr[...], wv[:, at]) + dot(once[...], uv[:, at]) + line(bv[at])
        vs[:, at] = value.astype(bf16)

    by_columns(project_rest)

    def heads_of(turn_no):
        per = pairs // GROUP
        pack, group = turn_no // per, turn_no % per
        units = []
        for k in range(GROUP):
            pair = group * GROUP + k
            at = pl.ds(pl.multiple_of(pair * LANES, LANES), LANES)
            for block in range(2):
                span = pl.ds(pl.multiple_of(pack * rows + block * BIG, BIG), BIG)
                for half in range(2):
                    place = (pack * HEADS + 2 * pair + half) * 2 + block
                    units.append((pack, place, block, span, at, half))
        return units

    def pipeline(units, first, second, third, finish):
        count = len(units)
        begun, middle, ended = {}, {}, {}

        def close(k):
            ended[k] = third(units[k], middle.pop(k))
            if k % 2:
                finish(units[k], ended.pop(k - 1), ended.pop(k))

        for k in range(min(2, count)):
            begun[k] = first(units[k])
        for k in range(count):
            if k + 2 < count:
                begun[k + 2] = first(units[k + 2])
            middle[k] = second(units[k], begun.pop(k))
            if k:
                close(k - 1)
        close(count - 1)

    def group_forward(turn_no, carry):
        def scores(unit):
            pack, _, block, span, at, half = unit
            mine = low if half == 0 else high
            if block == 0:
                return dot(qs[span, at], jnp.where(mine, ks[span, at], none), 1, 1)
            query = jnp.where(mine, qs[span, at], own_q[pack])
            return dot(query, jnp.where(mine, ks[span, at], other_k[pack]), 1, 1)

        def soften(unit, s):
            e = jnp.exp2(s - jnp.max(s, axis=-1, keepdims=True))
            low_e = e.astype(bf16)
            probs[unit[1]] = low_e
            return low_e, jnp.sum(e, axis=-1, keepdims=True)

        def mix(unit, held):
            _, _, _, span, at, _ = unit
            return dot(held[0], vs[span, at]), held[1]

        def finish(unit, one, two):
            _, _, _, span, at, _ = unit
            scale = 1.0 / jnp.where(low, one[1], two[1])
            inv[span, at] = scale
            att[span, at] = (jnp.where(low, one[0], two[0]) * scale).astype(bf16)

        pipeline(heads_of(turn_no), scores, soften, mix, finish)
        return carry

    turns = packs * pairs // GROUP
    lax.fori_loop(0, turns, group_forward, 0)

    arrive(4, 5)
    halves = [slice(pack * rows, (pack + 1) * rows) for pack in range(packs)]
    for at in halves:
        zs[at, :] = dot(att[at, :], wo[...])
    step = STEP

    def pieces_of(at):
        return [slice(k, k + step) for k in range(at.start, at.stop, step)]

    for half in halves:
        for at in pieces_of(half):
            z = xr[at, :].astype(f32) + zs[at, :] + line(bo[...])
            n, root = norm_rows(z)
            n1[at, :] = n
            r1[at, :] = root
            hb[at, :] = (n * line(g1[...]) + line(b1[...])).astype(bf16)
    turn(raw_cotangent, cr)

    arrive(6)
    chunk = CHUNK
    count = act.shape[1] // chunk

    def up(c, carry):
        at = pl.ds(pl.multiple_of(c * chunk, chunk), chunk)
        u = dot(hb[...], wu[:, at]) + line(bu[at])
        z = u * (0.5**0.5)
        half_cdf = 0.5 + 0.5 * lax.erf(z)
        act[:, at] = (u * half_cdf).astype(bf16)
        bell = jnp.exp2(z * z * -LOG2E - LOG2_ROOT)
        gp[:, at] = (half_cdf + u * bell).astype(bf16)
        return carry

    lax.fori_loop(0, count, up, 0)
    arrive(7)

    for half in halves:
        for c in range(width // BIG):
            at = slice(c * BIG, (c + 1) * BIG)
            zs[half, at] = dot(act[half, :], wd[:, at])
    results = []
    for pack in range(packs):
        for at in pieces_of(halves[pack]):
            hidden = n1[at, :] * line(g1[...]) + line(b1[...])
            z = hidden + zs[at, :] + line(bd[...])
            n, root = norm_rows(z)
            gain = line(g2[...])
            raw_tokens[at, :] = (n * gain + line(b2[...])).astype(bf16)
            d = norm_rows_back(cr[at, :].astype(f32) * gain, n, root)
            zs[at, :] = d
            hb[at, :] = d.astype(bf16)
        span = pl.ds(pack * rows, rows)
        rotate_rows(raw_tokens, pack * rows, rows, rows - starts[pack], put(cr, pack * rows))
        results.append(
            pltpu.make_async_copy(cr.at[span, :], out_hbm.at[span, :], sems.at[8 + pack])
        )
        results[-1].start()

    def up_back(c, carry):
        at = pl.ds(pl.multiple_of(c * chunk, chunk), chunk)
        t = dot(hb[...], wd[at, :], 1, 1)
        act[:, at] = (t * gp[:, at].astype(f32)).astype(bf16)
        return carry

    lax.fori_loop(0, count, up_back, 0)

    def down_back(c, carry):
        at = pl.ds(pl.multiple_of(c * BIG, BIG), BIG)
        zs[:, at] = zs[:, at] + dot(act[...], wu[at, :], 1, 1)
        return carry

    lax.fori_loop(0, width // BIG, down_back, 0)

    for copy in results:
        copy.wait()
    for half in halves:
        for at in pieces_of(half):
            d = norm_rows_back(zs[at, :] * line(g1[...]), n1[at, :], r1[at, :])
            zs[at, :] = d
            hb[at, :] = d.astype(bf16)
        cr[half, :] = dot(hb[half, :], wo[...], 1, 1).astype(bf16)

    dq, dk, dv = (act.at[:, k * width : (k + 1) * width] for k in range(3))

    def group_back(turn_no, carry):
        ready = {}

        def slopes(unit):
            _, _, block, span, at, half = unit
            if half == 0:
                scaled = cr[span, at].astype(f32) * inv[span, at]
                minus = pltpu.roll(-scaled * att[span, at].astype(f32), HEAD_DIM, 1)
                scaled = scaled.astype(bf16)
                ready[id(at), block] = scaled, minus.astype(bf16), scaled.T, qs[span, at].T
            scaled, minus = ready[id(at), block][:2]
            mine = low if half == 0 else high
            left = jnp.where(mine, scaled, minus)
            return dot(left, jnp.where(mine, vs[span, at], ones_pair), 1, 1)

        def weigh(unit, d):
            e = probs[unit[1]]
            return e * d.astype(bf16), e

        def grads_of(unit, held):
            _, _, block, span, at, half = unit
            ds, e = held
            _, _, scaled_t, query_t = ready[id(at), block]
            lines = slice(half * HEAD_DIM, (half + 1) * HEAD_DIM)
            return dot(ds, ks[span, at]), dot(query_t[lines], ds), dot(scaled_t[lines], e)

        def finish(unit, one, two):
            _, _, block, span, at, _ = unit
            ready.pop((id(at), block))
            dq[span, at] = (jnp.where(low, one[0], two[0]) * HEAD_DIM**-0.5).astype(bf16)
            turned = jnp.concatenate([one[1], two[1]], axis=0) * (1.0 / LOG2E)
            dk[span, at] = turned.astype(bf16).T
            dv[span, at] = jnp.concatenate([one[2], two[2]], axis=0).astype(bf16).T

        pipeline(heads_of(turn_no), slopes, weigh, grads_of, finish)
        return carry

    lax.fori_loop(0, turns, group_back, 0)

    dl = (dot(dq[...], uq[...], 1, 1) + dot(dv[...], uv[...], 1, 1)).astype(bf16)
    gd = dot(dl, xr[...], 0, 0)
    lora_t = lora[...].T
    gq = adapter_scale * dot(lora_t[: 2 * RANK], dq[...])[:RANK]
    gv = adapter_scale * dot(lora_t[HEAD_DIM : HEAD_DIM + 2 * RANK], dv[...])[:RANK]
    pack_grads(flat, gd, gq, gv)
    half_rows = flat.shape[0] // 2
    side = side_ref[0]
    kept = flat[pl.ds(pl.multiple_of(side * half_rows, 8), half_rows), :]
    more = first_ref.shape[0]
    send_ref[:half_rows, :] = flat[pl.ds(pl.multiple_of((1 - side) * half_rows, 8), half_rows), :]
    send_ref[half_rows:, :] = jnp.zeros((2 * more, LANES), f32)
    keep_ref[:half_rows, :] = kept
    keep_ref[half_rows : half_rows + more, :] = first_ref[...]
    keep_ref[half_rows + more :, :] = second_ref[...]

    act[:, 3 * width : 3 * width + LANES] = jnp.where(
        narrow, dl, jnp.zeros((total_rows, LANES), bf16)
    )


def token_kernel(begin, start_ref, wcat, grads, first, *rest):
    out_hbm, total, stage, sems = rest[-4:]
    total_rows, cut = total.shape
    packs = start_ref.shape[0]
    rows = total_rows // packs
    depth = wcat.shape[1]
    for c in range(cut // BIG):
        at = slice(begin + c * BIG, begin + (c + 1) * BIG)
        term = dot(grads[:, :depth], wcat[at, :], 1, 1)
        total[:, c * BIG : (c + 1) * BIG] = first[:, at] + term
    copies = []
    for pack in range(packs):
        span = pl.ds(pack * rows, rows)

        def emit(at, block, base=pack * rows):
            stage[pl.ds(base + at, 16), :] = block.astype(bf16)

        start = jnp.max(start_ref[pack : pack + 1, :]).astype(jnp.int32)
        rotate_rows(total, pack * rows, rows, rows - start, emit)
        to = out_hbm.at[span, begin : begin + cut]
        copies.append(pltpu.make_async_copy(stage.at[span, :], to, sems.at[pack]))
        copies[-1].start()
    for copy in copies:
        copy.wait()


def optimizer_kernel(places, *refs):
    steps_ref, rate_ref, place_ref, held, other, params = refs[:6]
    grad_out, new_params, first_out, second_out, total = refs[6:]
    shares, own_rows = params.shape[:2]
    half = shares // 2
    place = place_ref[0]
    side = place & 1
    for k in range(half):
        at = slice(k * own_rows, (k + 1) * own_rows)
        total[side, k] = held[at, :]
        total[1 - side, k] = other[at, :]
    norm_sq = jnp.sum(jnp.sum(total[...] * total[...], axis=(0, 1)), keepdims=True)
    clip = jnp.minimum(1.0, lax.rsqrt(norm_sq + 1e-06))

    def power(base):
        return lax.fori_loop(0, steps_ref[0], lambda _, value: value * base, jnp.float32(1.0))

    shape = (own_rows, LANES)
    fix_one = jnp.full(shape, 1.0 - power(beta_one), f32)
    fix_two = jnp.full(shape, 1.0 - power(beta_two), f32)
    grad_out[...] = total[place // half, place % half]
    for j, mask in enumerate(places + [mask ^ 1 for mask in places]):
        source, at = (held, half + 2 * j) if j < half else (other, half + 2 * (j - half))
        moment = source[at * own_rows : (at + 1) * own_rows, :]
        square = source[(at + 1) * own_rows : (at + 2) * own_rows, :]
        share = place ^ mask
        clipped = total[share // half, share % half] * clip
        first = beta_one * moment + (1.0 - beta_one) * clipped
        second = beta_two * square + (1.0 - beta_two) * clipped * clipped
        if j == 0:
            first_out[...] = first
            second_out[...] = second
        before = params[share]
        update = first / fix_one / (jnp.sqrt(second / fix_two) + adam_eps) + decay_rate * before
        rate = rate_ref[0] * jnp.where(share < half, 1.0, rate_ratio)
        new_params[share] = before - rate * update


def swap(x, axis, bit):
    n = lax.axis_size(axis)
    return lax.ppermute(x, axis, [(i, i ^ bit) for i in range(n)])


def bits_of(axis):
    n = lax.axis_size(axis)
    return [1 << k for k in range(n.bit_length() - 1)]


def shards(
    tokens,
    segment_ids,
    cotangent,
    query_frozen_weight,
    query_bias_vector,
    w_key,
    value_frozen_weight,
    value_bias_vector,
    w_out,
    b_out,
    norm1_gain,
    norm1_bias,
    w_up,
    b_up,
    w_down,
    b_down,
    norm2_gain,
    norm2_bias,
    factors,
    moment_first,
    moment_second,
    step_count,
    learn_rate,
):
    width = tokens.shape[1]
    packs, rows = segment_ids.shape
    ff = w_up.shape[1]
    total_rows = packs * rows
    flat_rows = factors.shape[0] // LANES
    shares = lax.axis_size("wide")
    own_rows = flat_rows // shares
    half_rows = flat_rows // 2
    place = lax.axis_index("wide").astype(jnp.int32)

    whole = pl.BlockSpec(memory_space=pltpu.VMEM)
    anywhere = pl.BlockSpec(memory_space=pl.ANY)
    scalars = pl.BlockSpec(memory_space=pltpu.SMEM)
    result = lambda shape, dtype: jax.ShapeDtypeStruct(shape, dtype)
    weights = (query_frozen_weight, w_key, value_frozen_weight, w_out, w_up, w_down)
    vectors = (
        query_bias_vector,
        value_bias_vector,
        b_out,
        norm1_gain,
        norm1_bias,
        b_up,
        b_down,
        norm2_gain,
        norm2_bias,
    )
    tall = lambda dtype: pltpu.VMEM((total_rows, width), dtype)
    kept, sent, output, *for_tokens = pl.pallas_call(
        main_kernel,
        out_shape=(
            pltpu.VMEM((half_rows + 2 * own_rows, LANES), f32),
            pltpu.VMEM((half_rows + 2 * own_rows, LANES), f32),
            result((total_rows, width), bf16),
            pltpu.VMEM((packs, LANES), f32),
            pltpu.VMEM((width, 3 * width + LANES), bf16),
            pltpu.VMEM((total_rows, ff), bf16),
            tall(f32),
        ),
        in_specs=[scalars] + [whole] * (4 + len(vectors)) + [anywhere] * 8,
        out_specs=[whole, whole, anywhere] + [whole] * 4,
        scratch_shapes=[pltpu.VMEM(w.shape, bf16) for w in weights[3:]]
        + [
            pltpu.SemaphoreType.DMA((8 + packs,)),
            tall(bf16),
            tall(bf16),
            tall(bf16),
            tall(bf16),
            tall(bf16),
            pltpu.VMEM((total_rows, LANES), bf16),
            pltpu.VMEM((packs * HEADS * 2, BIG, BIG), bf16),
            tall(bf16),
            tall(f32),
            tall(f32),
            pltpu.VMEM((total_rows, 1), f32),
            tall(bf16),
            pltpu.VMEM((total_rows, ff), bf16),
            pltpu.VMEM((LANES, width), bf16),
            pltpu.VMEM((LANES, width), bf16),
            pltpu.VMEM((packs, BIG, LANES), bf16),
            pltpu.VMEM((packs, BIG, LANES), bf16),
            pltpu.VMEM((flat_rows, LANES), f32),
        ],
        compiler_params=pltpu.CompilerParams(vmem_limit_bytes=VMEM_LIMIT),
    )(
        (place & 1).reshape(1),
        segment_ids,
        factors.reshape(flat_rows, LANES),
        moment_first.reshape(own_rows, LANES),
        moment_second.reshape(own_rows, LANES),
        *vectors,
        tokens,
        cotangent,
        *weights,
    )

    def token_piece(begin, cut, before, tie):
        held = [] if before is None else [before]
        start, _ = lax.optimization_barrier((for_tokens[0], tie))
        return pl.pallas_call(
            functools.partial(token_kernel, begin),
            out_shape=result((total_rows, width), bf16),
            in_specs=[whole] * 4 + [anywhere] * len(held),
            out_specs=anywhere,
            scratch_shapes=[
                pltpu.VMEM((total_rows, cut), f32),
                pltpu.VMEM((total_rows, cut), bf16),
                pltpu.SemaphoreType.DMA((packs,)),
            ],
            input_output_aliases={4: 0} if held else {},
            compiler_params=pltpu.CompilerParams(vmem_limit_bytes=16 * 2**20),
            cost_estimate=pl.CostEstimate(
                flops=2 * total_rows * cut * (3 * width + LANES),
                bytes_accessed=total_rows * cut * 2,
                transcendentals=0,
            ),
        )(start, *for_tokens[1:], *held)

    held = kept + swap(sent, "wide", 1)
    bits = bits_of("wide")[1:]
    places = [0]
    grad_tokens = None
    while bits:
        now, bits = bits[:2], bits[2:]
        masks = [now[0]] if len(now) == 1 else [now[0], now[1], now[0] | now[1]]
        got = [swap(held, "wide", mask) for mask in masks]
        if grad_tokens is None:
            grad_tokens = token_piece(0, width - BIG, None, held)
            grad_tokens, *got = lax.optimization_barrier((grad_tokens, *got))
        if len(got) == 1:
            total = held[:half_rows] + got[0][:half_rows]
        else:
            total = (held[:half_rows] + got[0][:half_rows]) + (
                got[1][:half_rows] + got[2][:half_rows]
            )
        places = places + [old ^ mask for mask in masks for old in places]
        if bits:
            held = jnp.concatenate([total] + [part[half_rows:] for part in [held] + got])
        else:
            moments = [part[half_rows:] for part in [held] + got]
    for bit in bits_of("dp"):
        got = swap(total, "dp", bit)
        if bit == 1:
            grad_tokens = token_piece(width - BIG, BIG, grad_tokens, total)
            grad_tokens, got = lax.optimization_barrier((grad_tokens, got))
        total = total + got
    held = jnp.concatenate([total] + moments)
    other = swap(held, "wide", 1)

    own = result((own_rows, LANES), f32)
    shaped = (shares, own_rows, LANES)
    grad_own, new_factors, new_first, new_second = pl.pallas_call(
        functools.partial(optimizer_kernel, places),
        out_shape=(own, result(shaped, f32), own, own),
        in_specs=[scalars] * 3 + [whole] * 3,
        out_specs=[whole] * 4,
        scratch_shapes=[pltpu.VMEM((2, shares // 2, own_rows, LANES), f32)],
    )(
        step_count,
        learn_rate,
        place.reshape(1),
        pltpu.with_memory_space_constraint(held, pltpu.VMEM),
        pltpu.with_memory_space_constraint(other, pltpu.VMEM),
        factors.reshape(shaped),
    )
    return (
        output,
        grad_tokens,
        grad_own.reshape(-1),
        new_factors.reshape(-1),
        new_first.reshape(-1),
        new_second.reshape(-1),
    )


def solution(mesh):
    rows = P(("dp", "wide"), None)
    in_specs = (rows,) * 3 + (P(),) * 16 + (P("wide"), P("wide"), P(), P())
    out_specs = (rows, rows, P("wide"), P(), P("wide"), P("wide"))
    return jax.shard_map(shards, mesh=mesh, in_specs=in_specs, out_specs=out_specs, check_vma=False)
```

```python
import functools

import jax
import jax.numpy as jnp
from jax import lax
from jax.experimental import pallas as pl
from jax.experimental.pallas import tpu as pltpu
from jax.sharding import PartitionSpec as P

HEADS = 12
RANK = 8
BIG = 256
HEAD_DIM = 64
LANES = 128
GROUP = 6
STEP = 256
CHUNK = 768
VMEM_LIMIT = 199 * 2**18
LOG2E = 1.4426950408889634
LOG2_ROOT = 1.3257480647361592

norm_eps = 1e-05
adapter_scale = 2.0
beta_one = 0.9
beta_two = 0.999
adam_eps = 1e-08
decay_rate = 0.01
rate_ratio = 16.0

bf16 = jnp.bfloat16
f32 = jnp.float32


def dot(left, right, ca=1, cb=0):
    return lax.dot_general(left, right, (((ca,), (cb,)), ((), ())), preferred_element_type=f32)


def line(vector):
    return vector.astype(f32).reshape(1, -1)


def unpack_factors(fac_ref, dcat, uq, uv):
    width = dcat.shape[0]
    per = width * RANK // LANES
    group = LANES // RANK
    lane = lax.broadcasted_iota(jnp.int32, (width, LANES), 1)
    sub = lax.broadcasted_iota(jnp.int32, (width, LANES), 0)
    keep = (lane // RANK) == (sub % group)
    spread = []
    for which in range(2):
        flat = fac_ref[which * per : (which + 1) * per, :].astype(bf16).astype(f32)
        wide = jnp.broadcast_to(flat[:, None, :], (per, group, LANES)).reshape(width, LANES)
        wide = jnp.where(keep, wide, 0.0)
        for hop in (8, 16, 32, 64):
            wide = wide + pltpu.roll(wide, hop, 1)
        spread.append(wide)
    dcat[...] = jnp.where(lane < HEAD_DIM, *spread).astype(bf16)
    tiles = width // LANES
    none = jnp.zeros((HEAD_DIM, width), bf16)
    for which, ref in enumerate((uq, uv)):
        base = 2 * per + which * per
        block = jnp.concatenate(
            [fac_ref[pl.ds(base + j, RANK, stride=tiles), :] for j in range(tiles)], axis=1
        )
        block = (block * adapter_scale).astype(bf16)
        half = jnp.concatenate([block] * (HEAD_DIM // RANK), axis=0)
        ref[...] = jnp.concatenate([half, none] if which == 0 else [none, half], axis=0)


def pack_grads(grad_ref, gd, gq, gv):
    width = gd.shape[1]
    per = width * RANK // LANES
    group = LANES // RANK
    tiles = width // LANES
    lane = lax.broadcasted_iota(jnp.int32, (width, LANES), 1)
    sub = lax.broadcasted_iota(jnp.int32, (width, LANES), 0)
    keep = (lane // RANK) == (sub % group)
    turned = jnp.concatenate(
        [gd[:, j * LANES : (j + 1) * LANES].T for j in range(tiles)], axis=0
    )
    other = pltpu.roll(turned, HEAD_DIM, 1)
    for which, (first, second) in enumerate(((turned, other), (other, turned))):
        full = jnp.where(lane < HEAD_DIM, first, second)
        picked = jnp.where(keep, full, 0.0).reshape(per, group, LANES)
        grad_ref[which * per : (which + 1) * per, :] = jnp.sum(picked, axis=1)
    for which, block in enumerate((gq, gv)):
        base = 2 * per + which * per
        for j in range(tiles):
            grad_ref[pl.ds(base + j, RANK, stride=tiles), :] = block[:, j * LANES : (j + 1) * LANES]


def rotate_rows(src, base, count, shift, emit):
    width = src.shape[1]
    groups = count // 8
    coarse, fine = shift // 8, shift % 8
    back = lax.rem(8 - fine, 8)
    keep = lax.broadcasted_iota(jnp.int32, (8, width), 0) < 8 - fine

    def turned(i):
        at = pl.multiple_of(base + 8 * lax.rem(coarse + i, groups), 8)
        return pltpu.roll(src[pl.ds(at, 8), :].astype(f32), back, 0)

    spun = [turned(i) for i in range(groups + 1)]
    moved = [jnp.where(keep, spun[i], spun[i + 1]) for i in range(groups)]
    for i in range(0, groups, 2):
        emit(i * 8, jnp.concatenate([moved[i], moved[i + 1]], axis=0))


def norm_rows(z):
    mean = jnp.mean(z, axis=-1, keepdims=True)
    centered = z - mean
    spread = jnp.mean(centered * centered, axis=-1, keepdims=True)
    root = lax.rsqrt(spread + norm_eps)
    return centered * root, root


def norm_rows_back(c, n, root):
    return root * (
        c - jnp.mean(c, axis=-1, keepdims=True) - n * jnp.mean(c * n, axis=-1, keepdims=True)
    )


def main_kernel(
    side_ref,
    seg_ref,
    fac_ref,
    first_ref,
    second_ref,
    bq,
    bv,
    bo,
    g1,
    b1,
    bu,
    bd,
    g2,
    b2,
    tok_hbm,
    cot_hbm,
    wq_hbm,
    wk_hbm,
    wv_hbm,
    wo_hbm,
    wu_hbm,
    wd_hbm,
    keep_ref,
    send_ref,
    out_hbm,
    start_ref,
    wcat,
    act,
    zs,
    wo,
    wu,
    wd,
    sems,
    xr,
    cr,
    qs,
    ks,
    vs,
    lora,
    probs,
    att,
    inv,
    n1,
    r1,
    hb,
    gp,
    uq,
    uv,
    own_q,
    other_k,
    flat,
):
    packs, rows = seg_ref.shape
    total_rows, width = xr.shape
    pairs = width // LANES
    wq, wk, wv = (wcat.at[:, k * width : (k + 1) * width] for k in range(3))
    dcat = wcat.at[:, 3 * width :]
    raw_tokens = act.at[:, :width]
    raw_cotangent = act.at[:, width : 2 * width]
    copies = []
    for src, dst in (
        (tok_hbm, raw_tokens),
        (wq_hbm, wq),
        (wk_hbm, wk),
        (wv_hbm, wv),
        (cot_hbm, raw_cotangent),
        (wo_hbm, wo),
        (wu_hbm, wu),
        (wd_hbm, wd),
    ):
        copies.append(pltpu.make_async_copy(src, dst, sems.at[len(copies)]))

    def depart(*which):
        for i in which:
            copies[i].start()

    def arrive(*which):
        for i in which:
            copies[i].wait()

    depart(0, 1)

    unpack_factors(fac_ref, dcat, uq, uv)

    lane = lax.broadcasted_iota(jnp.int32, (BIG, LANES), 1)
    low = lane < HEAD_DIM
    high = jnp.logical_not(low)
    used = (lane % HEAD_DIM) < 8
    none = jnp.zeros((BIG, LANES), bf16)
    ones_pair = jnp.ones((BIG, LANES), bf16)
    low_lane = lax.broadcasted_iota(jnp.int32, (1, LANES), 1) < HEAD_DIM
    slot = lax.broadcasted_iota(jnp.int32, (LANES, rows), 0) % HEAD_DIM
    ones = jnp.ones((8, rows), bf16)
    starts = []
    for pack in range(packs):
        seg = jnp.broadcast_to(seg_ref[pack : pack + 1, :], (LANES, rows))
        seg_lo = dot(ones, jnp.where(seg < slot, 1.0, 0.0).astype(bf16), 1, 1)[:1]
        seg_hi = dot(ones, jnp.where(seg <= slot, 1.0, 0.0).astype(bf16), 1, 1)[:1]
        large = low_lane & (seg_hi - seg_lo == BIG)
        start = jnp.sum(jnp.where(large, seg_lo, 0.0)).astype(jnp.int32)
        starts.append(start)
        start_ref[pack : pack + 1, :] = jnp.full((1, LANES), start.astype(f32))
        row = lax.broadcasted_iota(jnp.int32, (BIG, LANES), 0) + (BIG + start)
        row = jnp.where(row >= rows, row - rows, row)
        inside = (row >= seg_lo.astype(jnp.int32)) & (row < seg_hi.astype(jnp.int32))
        own_q[pack] = jnp.where(inside, 1.0, 0.0).astype(bf16)
        other_k[pack] = jnp.where(used & jnp.logical_not(inside), -1e30, 0.0).astype(bf16)

    def put(dst, base):
        def emit(at, block):
            dst[pl.ds(base + at, 16), :] = block.astype(dst.dtype)

        return emit

    def turn(src, dst):
        for pack in range(packs):
            rotate_rows(src, pack * rows, rows, starts[pack], put(dst, pack * rows))

    arrive(0)
    depart(2, 3)
    turn(raw_tokens, xr)

    lora[...] = dot(xr[...], dcat[...]).astype(bf16)
    narrow = lax.broadcasted_iota(jnp.int32, (total_rows, LANES), 1) % HEAD_DIM < RANK
    once = att.at[:, :LANES]
    once[...] = jnp.where(narrow, lora[...], jnp.zeros((total_rows, LANES), bf16))
    columns = [slice(c * BIG, (c + 1) * BIG) for c in range(width // BIG)]
    arrive(1)
    def by_columns(body):
        def run(c, carry):
            body(pl.ds(pl.multiple_of(c * BIG, BIG), BIG))
            return carry

        lax.fori_loop(0, width // BIG, run, 0)

    def project_query(at):
        query = dot(xr[...], wq[:, at]) + dot(once[...], uq[:, at]) + line(bq[at])
        qs[:, at] = (query * (HEAD_DIM**-0.5 * LOG2E)).astype(bf16)

    by_columns(project_query)
    arrive(2, 3)
    depart(4, 5, 6, 7)
    def project_rest(at):
        ks[:, at] = dot(xr[...], wk[:, at]).astype(bf16)
        value = dot(xr[...], wv[:, at]) + dot(once[...], uv[:, at]) + line(bv[at])
        vs[:, at] = value.astype(bf16)

    by_columns(project_rest)

    def heads_of(turn_no):
        per = pairs // GROUP
        pack, group = turn_no // per, turn_no % per
        units = []
        for k in range(GROUP):
            pair = group * GROUP + k
            at = pl.ds(pl.multiple_of(pair * LANES, LANES), LANES)
            for block in range(2):
                span = pl.ds(pl.multiple_of(pack * rows + block * BIG, BIG), BIG)
                for half in range(2):
                    place = (pack * HEADS + 2 * pair + half) * 2 + block
                    units.append((pack, place, block, span, at, half))
        return units

    def pipeline(units, first, second, third, finish):
        count = len(units)
        begun, middle, ended = {}, {}, {}

        def close(k):
            ended[k] = third(units[k], middle.pop(k))
            if k % 2:
                finish(units[k], ended.pop(k - 1), ended.pop(k))

        for k in range(min(2, count)):
            begun[k] = first(units[k])
        for k in range(count):
            if k + 2 < count:
                begun[k + 2] = first(units[k + 2])
            middle[k] = second(units[k], begun.pop(k))
            if k:
                close(k - 1)
        close(count - 1)

    def group_forward(turn_no, carry):
        def scores(unit):
            pack, _, block, span, at, half = unit
            mine = low if half == 0 else high
            if block == 0:
                return dot(qs[span, at], jnp.where(mine, ks[span, at], none), 1, 1)
            query = jnp.where(mine, qs[span, at], own_q[pack])
            return dot(query, jnp.where(mine, ks[span, at], other_k[pack]), 1, 1)

        def soften(unit, s):
            e = jnp.exp2(s - jnp.max(s, axis=-1, keepdims=True))
            low_e = e.astype(bf16)
            probs[unit[1]] = low_e
            return low_e, jnp.sum(e, axis=-1, keepdims=True)

        def mix(unit, held):
            _, _, _, span, at, _ = unit
            return dot(held[0], vs[span, at]), held[1]

        def finish(unit, one, two):
            _, _, _, span, at, _ = unit
            scale = 1.0 / jnp.where(low, one[1], two[1])
            inv[span, at] = scale
            att[span, at] = (jnp.where(low, one[0], two[0]) * scale).astype(bf16)

        pipeline(heads_of(turn_no), scores, soften, mix, finish)
        return carry

    turns = packs * pairs // GROUP
    lax.fori_loop(0, turns, group_forward, 0)

    arrive(4, 5)
    halves = [slice(pack * rows, (pack + 1) * rows) for pack in range(packs)]
    for at in halves:
        zs[at, :] = dot(att[at, :], wo[...])
    step = STEP

    def pieces_of(at):
        return [slice(k, k + step) for k in range(at.start, at.stop, step)]

    for half in halves:
        for at in pieces_of(half):
            z = xr[at, :].astype(f32) + zs[at, :] + line(bo[...])
            n, root = norm_rows(z)
            n1[at, :] = n
            r1[at, :] = root
            hb[at, :] = (n * line(g1[...]) + line(b1[...])).astype(bf16)
    turn(raw_cotangent, cr)

    arrive(6)
    chunk = CHUNK
    count = act.shape[1] // chunk

    def up(c, carry):
        at = pl.ds(pl.multiple_of(c * chunk, chunk), chunk)
        u = dot(hb[...], wu[:, at]) + line(bu[at])
        z = u * (0.5**0.5)
        half_cdf = 0.5 + 0.5 * lax.erf(z)
        act[:, at] = (u * half_cdf).astype(bf16)
        bell = jnp.exp2(z * z * -LOG2E - LOG2_ROOT)
        gp[:, at] = (half_cdf + u * bell).astype(bf16)
        return carry

    lax.fori_loop(0, count, up, 0)
    arrive(7)

    for half in halves:
        for c in range(width // BIG):
            at = slice(c * BIG, (c + 1) * BIG)
            zs[half, at] = dot(act[half, :], wd[:, at])
    results = []
    for pack in range(packs):
        for at in pieces_of(halves[pack]):
            hidden = n1[at, :] * line(g1[...]) + line(b1[...])
            z = hidden + zs[at, :] + line(bd[...])
            n, root = norm_rows(z)
            gain = line(g2[...])
            raw_tokens[at, :] = (n * gain + line(b2[...])).astype(bf16)
            d = norm_rows_back(cr[at, :].astype(f32) * gain, n, root)
            zs[at, :] = d
            hb[at, :] = d.astype(bf16)
        span = pl.ds(pack * rows, rows)
        rotate_rows(raw_tokens, pack * rows, rows, rows - starts[pack], put(cr, pack * rows))
        results.append(
            pltpu.make_async_copy(cr.at[span, :], out_hbm.at[span, :], sems.at[8 + pack])
        )
        results[-1].start()

    def up_back(c, carry):
        at = pl.ds(pl.multiple_of(c * chunk, chunk), chunk)
        t = dot(hb[...], wd[at, :], 1, 1)
        act[:, at] = (t * gp[:, at].astype(f32)).astype(bf16)
        return carry

    lax.fori_loop(0, count, up_back, 0)

    def down_back(c, carry):
        at = pl.ds(pl.multiple_of(c * BIG, BIG), BIG)
        zs[:, at] = zs[:, at] + dot(act[...], wu[at, :], 1, 1)
        return carry

    lax.fori_loop(0, width // BIG, down_back, 0)

    for copy in results:
        copy.wait()
    for half in halves:
        for at in pieces_of(half):
            d = norm_rows_back(zs[at, :] * line(g1[...]), n1[at, :], r1[at, :])
            zs[at, :] = d
            hb[at, :] = d.astype(bf16)
        cr[half, :] = dot(hb[half, :], wo[...], 1, 1).astype(bf16)

    dq, dk, dv = (act.at[:, k * width : (k + 1) * width] for k in range(3))

    def group_back(turn_no, carry):
        ready = {}

        def slopes(unit):
            _, _, block, span, at, half = unit
            if half == 0:
                scaled = cr[span, at].astype(f32) * inv[span, at]
                minus = pltpu.roll(-scaled * att[span, at].astype(f32), HEAD_DIM, 1)
                scaled = scaled.astype(bf16)
                ready[id(at), block] = scaled, minus.astype(bf16), scaled.T, qs[span, at].T
            scaled, minus = ready[id(at), block][:2]
            mine = low if half == 0 else high
            left = jnp.where(mine, scaled, minus)
            return dot(left, jnp.where(mine, vs[span, at], ones_pair), 1, 1)

        def weigh(unit, d):
            e = probs[unit[1]]
            return e * d.astype(bf16), e

        def grads_of(unit, held):
            _, _, block, span, at, half = unit
            ds, e = held
            _, _, scaled_t, query_t = ready[id(at), block]
            lines = slice(half * HEAD_DIM, (half + 1) * HEAD_DIM)
            return dot(ds, ks[span, at]), dot(query_t[lines], ds), dot(scaled_t[lines], e)

        def finish(unit, one, two):
            _, _, block, span, at, _ = unit
            ready.pop((id(at), block))
            dq[span, at] = (jnp.where(low, one[0], two[0]) * HEAD_DIM**-0.5).astype(bf16)
            turned = jnp.concatenate([one[1], two[1]], axis=0) * (1.0 / LOG2E)
            dk[span, at] = turned.astype(bf16).T
            dv[span, at] = jnp.concatenate([one[2], two[2]], axis=0).astype(bf16).T

        pipeline(heads_of(turn_no), slopes, weigh, grads_of, finish)
        return carry

    lax.fori_loop(0, turns, group_back, 0)

    dl = (dot(dq[...], uq[...], 1, 1) + dot(dv[...], uv[...], 1, 1)).astype(bf16)
    gd = dot(dl, xr[...], 0, 0)
    lora_t = lora[...].T
    gq = adapter_scale * dot(lora_t[: 2 * RANK], dq[...])[:RANK]
    gv = adapter_scale * dot(lora_t[HEAD_DIM : HEAD_DIM + 2 * RANK], dv[...])[:RANK]
    pack_grads(flat, gd, gq, gv)
    half_rows = flat.shape[0] // 2
    side = side_ref[0]
    kept = flat[pl.ds(pl.multiple_of(side * half_rows, 8), half_rows), :]
    more = first_ref.shape[0]
    send_ref[:half_rows, :] = flat[pl.ds(pl.multiple_of((1 - side) * half_rows, 8), half_rows), :]
    send_ref[half_rows:, :] = jnp.zeros((2 * more, LANES), f32)
    keep_ref[:half_rows, :] = kept
    keep_ref[half_rows : half_rows + more, :] = first_ref[...]
    keep_ref[half_rows + more :, :] = second_ref[...]

    act[:, 3 * width : 3 * width + LANES] = jnp.where(
        narrow, dl, jnp.zeros((total_rows, LANES), bf16)
    )


def token_kernel(begin, start_ref, wcat, grads, first, *rest):
    out_hbm, total, stage, sems = rest[-4:]
    total_rows, cut = total.shape
    packs = start_ref.shape[0]
    rows = total_rows // packs
    depth = wcat.shape[1]
    for c in range(cut // BIG):
        at = slice(begin + c * BIG, begin + (c + 1) * BIG)
        term = dot(grads[:, :depth], wcat[at, :], 1, 1)
        total[:, c * BIG : (c + 1) * BIG] = first[:, at] + term
    copies = []
    for pack in range(packs):
        span = pl.ds(pack * rows, rows)

        def emit(at, block, base=pack * rows):
            stage[pl.ds(base + at, 16), :] = block.astype(bf16)

        start = jnp.max(start_ref[pack : pack + 1, :]).astype(jnp.int32)
        rotate_rows(total, pack * rows, rows, rows - start, emit)
        to = out_hbm.at[span, begin : begin + cut]
        copies.append(pltpu.make_async_copy(stage.at[span, :], to, sems.at[pack]))
        copies[-1].start()
    for copy in copies:
        copy.wait()


def optimizer_kernel(places, *refs):
    steps_ref, rate_ref, place_ref, held, other, params = refs[:6]
    grad_out, new_params, first_out, second_out, total = refs[6:]
    shares, own_rows = params.shape[:2]
    half = shares // 2
    place = place_ref[0]
    side = place & 1
    for k in range(half):
        at = slice(k * own_rows, (k + 1) * own_rows)
        total[side, k] = held[at, :]
        total[1 - side, k] = other[at, :]
    norm_sq = jnp.sum(jnp.sum(total[...] * total[...], axis=(0, 1)), keepdims=True)
    clip = jnp.minimum(1.0, lax.rsqrt(norm_sq + 1e-06))

    def power(base):
        return lax.fori_loop(0, steps_ref[0], lambda _, value: value * base, jnp.float32(1.0))

    shape = (own_rows, LANES)
    fix_one = jnp.full(shape, 1.0 - power(beta_one), f32)
    fix_two = jnp.full(shape, 1.0 - power(beta_two), f32)
    grad_out[...] = total[place // half, place % half]
    for j, mask in enumerate(places + [mask ^ 1 for mask in places]):
        source, at = (held, half + 2 * j) if j < half else (other, half + 2 * (j - half))
        moment = source[at * own_rows : (at + 1) * own_rows, :]
        square = source[(at + 1) * own_rows : (at + 2) * own_rows, :]
        share = place ^ mask
        clipped = total[share // half, share % half] * clip
        first = beta_one * moment + (1.0 - beta_one) * clipped
        second = beta_two * square + (1.0 - beta_two) * clipped * clipped
        if j == 0:
            first_out[...] = first
            second_out[...] = second
        before = params[share]
        update = first / fix_one / (jnp.sqrt(second / fix_two) + adam_eps) + decay_rate * before
        rate = rate_ref[0] * jnp.where(share < half, 1.0, rate_ratio)
        new_params[share] = before - rate * update


def swap(x, axis, bit):
    n = lax.axis_size(axis)
    return lax.ppermute(x, axis, [(i, i ^ bit) for i in range(n)])


def bits_of(axis):
    n = lax.axis_size(axis)
    return [1 << k for k in range(n.bit_length() - 1)]


def shards(
    tokens,
    segment_ids,
    cotangent,
    query_frozen_weight,
    query_bias_vector,
    w_key,
    value_frozen_weight,
    value_bias_vector,
    w_out,
    b_out,
    norm1_gain,
    norm1_bias,
    w_up,
    b_up,
    w_down,
    b_down,
    norm2_gain,
    norm2_bias,
    factors,
    moment_first,
    moment_second,
    step_count,
    learn_rate,
):
    width = tokens.shape[1]
    packs, rows = segment_ids.shape
    ff = w_up.shape[1]
    total_rows = packs * rows
    flat_rows = factors.shape[0] // LANES
    shares = lax.axis_size("wide")
    own_rows = flat_rows // shares
    half_rows = flat_rows // 2
    place = lax.axis_index("wide").astype(jnp.int32)

    whole = pl.BlockSpec(memory_space=pltpu.VMEM)
    anywhere = pl.BlockSpec(memory_space=pl.ANY)
    scalars = pl.BlockSpec(memory_space=pltpu.SMEM)
    result = lambda shape, dtype: jax.ShapeDtypeStruct(shape, dtype)
    weights = (query_frozen_weight, w_key, value_frozen_weight, w_out, w_up, w_down)
    vectors = (
        query_bias_vector,
        value_bias_vector,
        b_out,
        norm1_gain,
        norm1_bias,
        b_up,
        b_down,
        norm2_gain,
        norm2_bias,
    )
    tall = lambda dtype: pltpu.VMEM((total_rows, width), dtype)
    kept, sent, output, *for_tokens = pl.pallas_call(
        main_kernel,
        out_shape=(
            pltpu.VMEM((half_rows + 2 * own_rows, LANES), f32),
            pltpu.VMEM((half_rows + 2 * own_rows, LANES), f32),
            result((total_rows, width), bf16),
            pltpu.VMEM((packs, LANES), f32),
            pltpu.VMEM((width, 3 * width + LANES), bf16),
            pltpu.VMEM((total_rows, ff), bf16),
            tall(f32),
        ),
        in_specs=[scalars] + [whole] * (4 + len(vectors)) + [anywhere] * 8,
        out_specs=[whole, whole, anywhere] + [whole] * 4,
        scratch_shapes=[pltpu.VMEM(w.shape, bf16) for w in weights[3:]]
        + [
            pltpu.SemaphoreType.DMA((8 + packs,)),
            tall(bf16),
            tall(bf16),
            tall(bf16),
            tall(bf16),
            tall(bf16),
            pltpu.VMEM((total_rows, LANES), bf16),
            pltpu.VMEM((packs * HEADS * 2, BIG, BIG), bf16),
            tall(bf16),
            tall(f32),
            tall(f32),
            pltpu.VMEM((total_rows, 1), f32),
            tall(bf16),
            pltpu.VMEM((total_rows, ff), bf16),
            pltpu.VMEM((LANES, width), bf16),
            pltpu.VMEM((LANES, width), bf16),
            pltpu.VMEM((packs, BIG, LANES), bf16),
            pltpu.VMEM((packs, BIG, LANES), bf16),
            pltpu.VMEM((flat_rows, LANES), f32),
        ],
        compiler_params=pltpu.CompilerParams(vmem_limit_bytes=VMEM_LIMIT),
    )(
        (place & 1).reshape(1),
        segment_ids,
        factors.reshape(flat_rows, LANES),
        moment_first.reshape(own_rows, LANES),
        moment_second.reshape(own_rows, LANES),
        *vectors,
        tokens,
        cotangent,
        *weights,
    )

    def token_piece(begin, cut, before, tie):
        held = [] if before is None else [before]
        start, _ = lax.optimization_barrier((for_tokens[0], tie))
        return pl.pallas_call(
            functools.partial(token_kernel, begin),
            out_shape=result((total_rows, width), bf16),
            in_specs=[whole] * 4 + [anywhere] * len(held),
            out_specs=anywhere,
            scratch_shapes=[
                pltpu.VMEM((total_rows, cut), f32),
                pltpu.VMEM((total_rows, cut), bf16),
                pltpu.SemaphoreType.DMA((packs,)),
            ],
            input_output_aliases={4: 0} if held else {},
            compiler_params=pltpu.CompilerParams(vmem_limit_bytes=16 * 2**20),
            cost_estimate=pl.CostEstimate(
                flops=2 * total_rows * cut * (3 * width + LANES),
                bytes_accessed=total_rows * cut * 2,
                transcendentals=0,
            ),
        )(start, *for_tokens[1:], *held)

    held = kept + swap(sent, "wide", 1)
    bits = bits_of("wide")[1:]
    places = [0]
    grad_tokens = None
    while bits:
        now, bits = bits[:2], bits[2:]
        masks = [now[0]] if len(now) == 1 else [now[0], now[1], now[0] | now[1]]
        got = [swap(held, "wide", mask) for mask in masks]
        if grad_tokens is None:
            grad_tokens = token_piece(0, width - BIG, None, held)
            grad_tokens, *got = lax.optimization_barrier((grad_tokens, *got))
        if len(got) == 1:
            total = held[:half_rows] + got[0][:half_rows]
        else:
            total = (held[:half_rows] + got[0][:half_rows]) + (
                got[1][:half_rows] + got[2][:half_rows]
            )
        places = places + [old ^ mask for mask in masks for old in places]
        if bits:
            held = jnp.concatenate([total] + [part[half_rows:] for part in [held] + got])
        else:
            moments = [part[half_rows:] for part in [held] + got]
    for bit in bits_of("dp"):
        got = swap(total, "dp", bit)
        if bit == 1:
            grad_tokens = token_piece(width - BIG, BIG, grad_tokens, total)
            grad_tokens, got = lax.optimization_barrier((grad_tokens, got))
        total = total + got
    held = jnp.concatenate([total] + moments)
    other = swap(held, "wide", 1)

    own = result((own_rows, LANES), f32)
    shaped = (shares, own_rows, LANES)
    grad_own, new_factors, new_first, new_second = pl.pallas_call(
        functools.partial(optimizer_kernel, places),
        out_shape=(own, result(shaped, f32), own, own),
        in_specs=[scalars] * 3 + [whole] * 3,
        out_specs=[whole] * 4,
        scratch_shapes=[pltpu.VMEM((2, shares // 2, own_rows, LANES), f32)],
    )(
        step_count,
        learn_rate,
        place.reshape(1),
        pltpu.with_memory_space_constraint(held, pltpu.VMEM),
        pltpu.with_memory_space_constraint(other, pltpu.VMEM),
        pltpu.with_memory_space_constraint(factors.reshape(shaped), pltpu.VMEM),
    )
    return (
        output,
        grad_tokens,
        grad_own.reshape(-1),
        new_factors.reshape(-1),
        new_first.reshape(-1),
        new_second.reshape(-1),
    )


def solution(mesh):
    rows = P(("dp", "wide"), None)
    in_specs = (rows,) * 3 + (P(),) * 16 + (P("wide"), P("wide"), P(), P())
    out_specs = (rows, rows, P("wide"), P(), P("wide"), P("wide"))
    return jax.shard_map(shards, mesh=mesh, in_specs=in_specs, out_specs=out_specs, check_vma=False)
```

```python
import functools

import jax
import jax.numpy as jnp
from jax import lax
from jax.experimental import pallas as pl
from jax.experimental.pallas import tpu as pltpu
from jax.sharding import PartitionSpec as P

HEADS = 12
RANK = 8
BIG = 256
HEAD_DIM = 64
LANES = 128
GROUP = 6
STEP = 256
CHUNK = 768
VMEM_LIMIT = 199 * 2**18
LOG2E = 1.4426950408889634
LOG2_ROOT = 1.3257480647361592

norm_eps = 1e-05
adapter_scale = 2.0
beta_one = 0.9
beta_two = 0.999
adam_eps = 1e-08
decay_rate = 0.01
rate_ratio = 16.0

bf16 = jnp.bfloat16
f32 = jnp.float32


def dot(left, right, ca=1, cb=0):
    return lax.dot_general(left, right, (((ca,), (cb,)), ((), ())), preferred_element_type=f32)


def line(vector):
    return vector.astype(f32).reshape(1, -1)


def unpack_factors(fac_ref, dcat, uq, uv):
    width = dcat.shape[0]
    per = width * RANK // LANES
    group = LANES // RANK
    lane = lax.broadcasted_iota(jnp.int32, (width, LANES), 1)
    sub = lax.broadcasted_iota(jnp.int32, (width, LANES), 0)
    keep = (lane // RANK) == (sub % group)
    spread = []
    for which in range(2):
        flat = fac_ref[which * per : (which + 1) * per, :].astype(bf16).astype(f32)
        wide = jnp.broadcast_to(flat[:, None, :], (per, group, LANES)).reshape(width, LANES)
        wide = jnp.where(keep, wide, 0.0)
        for hop in (8, 16, 32, 64):
            wide = wide + pltpu.roll(wide, hop, 1)
        spread.append(wide)
    dcat[...] = jnp.where(lane < HEAD_DIM, *spread).astype(bf16)
    tiles = width // LANES
    none = jnp.zeros((HEAD_DIM, width), bf16)
    for which, ref in enumerate((uq, uv)):
        base = 2 * per + which * per
        block = jnp.concatenate(
            [fac_ref[pl.ds(base + j, RANK, stride=tiles), :] for j in range(tiles)], axis=1
        )
        block = (block * adapter_scale).astype(bf16)
        half = jnp.concatenate([block] * (HEAD_DIM // RANK), axis=0)
        ref[...] = jnp.concatenate([half, none] if which == 0 else [none, half], axis=0)


def pack_grads(grad_ref, gd, gq, gv):
    width = gd.shape[1]
    per = width * RANK // LANES
    group = LANES // RANK
    tiles = width // LANES
    lane = lax.broadcasted_iota(jnp.int32, (width, LANES), 1)
    sub = lax.broadcasted_iota(jnp.int32, (width, LANES), 0)
    keep = (lane // RANK) == (sub % group)
    turned = jnp.concatenate(
        [gd[:, j * LANES : (j + 1) * LANES].T for j in range(tiles)], axis=0
    )
    other = pltpu.roll(turned, HEAD_DIM, 1)
    for which, (first, second) in enumerate(((turned, other), (other, turned))):
        full = jnp.where(lane < HEAD_DIM, first, second)
        picked = jnp.where(keep, full, 0.0).reshape(per, group, LANES)
        grad_ref[which * per : (which + 1) * per, :] = jnp.sum(picked, axis=1)
    for which, block in enumerate((gq, gv)):
        base = 2 * per + which * per
        for j in range(tiles):
            grad_ref[pl.ds(base + j, RANK, stride=tiles), :] = block[:, j * LANES : (j + 1) * LANES]


def rotate_rows(src, base, count, shift, emit):
    width = src.shape[1]
    groups = count // 8
    coarse, fine = shift // 8, shift % 8
    back = lax.rem(8 - fine, 8)
    keep = lax.broadcasted_iota(jnp.int32, (8, width), 0) < 8 - fine

    def turned(i):
        at = pl.multiple_of(base + 8 * lax.rem(coarse + i, groups), 8)
        return pltpu.roll(src[pl.ds(at, 8), :].astype(f32), back, 0)

    spun = [turned(i) for i in range(groups + 1)]
    moved = [jnp.where(keep, spun[i], spun[i + 1]) for i in range(groups)]
    for i in range(0, groups, 2):
        emit(i * 8, jnp.concatenate([moved[i], moved[i + 1]], axis=0))


def norm_rows(z):
    mean = jnp.mean(z, axis=-1, keepdims=True)
    centered = z - mean
    spread = jnp.mean(centered * centered, axis=-1, keepdims=True)
    root = lax.rsqrt(spread + norm_eps)
    return centered * root, root


def norm_rows_back(c, n, root):
    return root * (
        c - jnp.mean(c, axis=-1, keepdims=True) - n * jnp.mean(c * n, axis=-1, keepdims=True)
    )


def main_kernel(
    side_ref,
    seg_ref,
    fac_ref,
    first_ref,
    second_ref,
    bq,
    bv,
    bo,
    g1,
    b1,
    bu,
    bd,
    g2,
    b2,
    tok_hbm,
    cot_hbm,
    wq_hbm,
    wk_hbm,
    wv_hbm,
    wo_hbm,
    wu_hbm,
    wd_hbm,
    keep_ref,
    send_ref,
    out_hbm,
    start_ref,
    wcat,
    act,
    zs,
    wo,
    wu,
    wd,
    sems,
    xr,
    cr,
    qs,
    ks,
    vs,
    lora,
    probs,
    att,
    inv,
    n1,
    r1,
    hb,
    gp,
    uq,
    uv,
    own_q,
    other_k,
    flat,
):
    packs, rows = seg_ref.shape
    total_rows, width = xr.shape
    pairs = width // LANES
    wq, wk, wv = (wcat.at[:, k * width : (k + 1) * width] for k in range(3))
    dcat = wcat.at[:, 3 * width :]
    raw_tokens = act.at[:, :width]
    raw_cotangent = act.at[:, width : 2 * width]
    copies = []
    for src, dst in (
        (tok_hbm, raw_tokens),
        (wq_hbm, wq),
        (wk_hbm, wk),
        (wv_hbm, wv),
        (cot_hbm, raw_cotangent),
        (wo_hbm, wo),
        (wu_hbm, wu),
        (wd_hbm, wd),
    ):
        copies.append(pltpu.make_async_copy(src, dst, sems.at[len(copies)]))

    def depart(*which):
        for i in which:
            copies[i].start()

    def arrive(*which):
        for i in which:
            copies[i].wait()

    depart(0, 1)

    unpack_factors(fac_ref, dcat, uq, uv)

    lane = lax.broadcasted_iota(jnp.int32, (BIG, LANES), 1)
    low = lane < HEAD_DIM
    high = jnp.logical_not(low)
    used = (lane % HEAD_DIM) < 8
    none = jnp.zeros((BIG, LANES), bf16)
    ones_pair = jnp.ones((BIG, LANES), bf16)
    low_lane = lax.broadcasted_iota(jnp.int32, (1, LANES), 1) < HEAD_DIM
    slot = lax.broadcasted_iota(jnp.int32, (LANES, rows), 0) % HEAD_DIM
    ones = jnp.ones((8, rows), bf16)
    starts = []
    for pack in range(packs):
        seg = jnp.broadcast_to(seg_ref[pack : pack + 1, :], (LANES, rows))
        seg_lo = dot(ones, jnp.where(seg < slot, 1.0, 0.0).astype(bf16), 1, 1)[:1]
        seg_hi = dot(ones, jnp.where(seg <= slot, 1.0, 0.0).astype(bf16), 1, 1)[:1]
        large = low_lane & (seg_hi - seg_lo == BIG)
        start = jnp.sum(jnp.where(large, seg_lo, 0.0)).astype(jnp.int32)
        starts.append(start)
        start_ref[pack : pack + 1, :] = jnp.full((1, LANES), start.astype(f32))
        row = lax.broadcasted_iota(jnp.int32, (BIG, LANES), 0) + (BIG + start)
        row = jnp.where(row >= rows, row - rows, row)
        inside = (row >= seg_lo.astype(jnp.int32)) & (row < seg_hi.astype(jnp.int32))
        own_q[pack] = jnp.where(inside, 1.0, 0.0).astype(bf16)
        other_k[pack] = jnp.where(used & jnp.logical_not(inside), -1e30, 0.0).astype(bf16)

    def put(dst, base):
        def emit(at, block):
            dst[pl.ds(base + at, 16), :] = block.astype(dst.dtype)

        return emit

    def turn(src, dst):
        for pack in range(packs):
            rotate_rows(src, pack * rows, rows, starts[pack], put(dst, pack * rows))

    arrive(0)
    depart(2, 3)
    turn(raw_tokens, xr)

    lora[...] = dot(xr[...], dcat[...]).astype(bf16)
    narrow = lax.broadcasted_iota(jnp.int32, (total_rows, LANES), 1) % HEAD_DIM < RANK
    once = att.at[:, :LANES]
    once[...] = jnp.where(narrow, lora[...], jnp.zeros((total_rows, LANES), bf16))
    columns = [slice(c * BIG, (c + 1) * BIG) for c in range(width // BIG)]
    arrive(1)
    def by_columns(body):
        def run(c, carry):
            body(pl.ds(pl.multiple_of(c * BIG, BIG), BIG))
            return carry

        lax.fori_loop(0, width // BIG, run, 0)

    def project_query(at):
        query = dot(xr[...], wq[:, at]) + dot(once[...], uq[:, at]) + line(bq[at])
        qs[:, at] = (query * (HEAD_DIM**-0.5 * LOG2E)).astype(bf16)

    by_columns(project_query)
    arrive(2, 3)
    depart(4, 5, 6, 7)
    def project_rest(at):
        ks[:, at] = dot(xr[...], wk[:, at]).astype(bf16)
        value = dot(xr[...], wv[:, at]) + dot(once[...], uv[:, at]) + line(bv[at])
        vs[:, at] = value.astype(bf16)

    by_columns(project_rest)

    def heads_of(turn_no):
        per = pairs // GROUP
        pack, group = turn_no // per, turn_no % per
        units = []
        for k in range(GROUP):
            pair = group * GROUP + k
            at = pl.ds(pl.multiple_of(pair * LANES, LANES), LANES)
            for block in range(2):
                span = pl.ds(pl.multiple_of(pack * rows + block * BIG, BIG), BIG)
                for half in range(2):
                    place = (pack * HEADS + 2 * pair + half) * 2 + block
                    units.append((pack, place, block, span, at, half))
        return units

    def pipeline(units, first, second, third, finish):
        count = len(units)
        begun, middle, ended = {}, {}, {}

        def close(k):
            ended[k] = third(units[k], middle.pop(k))
            if k % 2:
                finish(units[k], ended.pop(k - 1), ended.pop(k))

        for k in range(min(2, count)):
            begun[k] = first(units[k])
        for k in range(count):
            if k + 2 < count:
                begun[k + 2] = first(units[k + 2])
            middle[k] = second(units[k], begun.pop(k))
            if k:
                close(k - 1)
        close(count - 1)

    def group_forward(turn_no, carry):
        def scores(unit):
            pack, _, block, span, at, half = unit
            mine = low if half == 0 else high
            if block == 0:
                return dot(qs[span, at], jnp.where(mine, ks[span, at], none), 1, 1)
            query = jnp.where(mine, qs[span, at], own_q[pack])
            return dot(query, jnp.where(mine, ks[span, at], other_k[pack]), 1, 1)

        def soften(unit, s):
            e = jnp.exp2(s - jnp.max(s, axis=-1, keepdims=True))
            low_e = e.astype(bf16)
            probs[unit[1]] = low_e
            return low_e, jnp.sum(e, axis=-1, keepdims=True)

        def mix(unit, held):
            _, _, _, span, at, _ = unit
            return dot(held[0], vs[span, at]), held[1]

        def finish(unit, one, two):
            _, _, _, span, at, _ = unit
            scale = 1.0 / jnp.where(low, one[1], two[1])
            inv[span, at] = scale
            att[span, at] = (jnp.where(low, one[0], two[0]) * scale).astype(bf16)

        pipeline(heads_of(turn_no), scores, soften, mix, finish)
        return carry

    turns = packs * pairs // GROUP
    lax.fori_loop(0, turns, group_forward, 0)

    arrive(4, 5)
    halves = [slice(pack * rows, (pack + 1) * rows) for pack in range(packs)]
    for at in halves:
        zs[at, :] = dot(att[at, :], wo[...])
    step = STEP

    def pieces_of(at):
        return [slice(k, k + step) for k in range(at.start, at.stop, step)]

    for half in halves:
        for at in pieces_of(half):
            z = xr[at, :].astype(f32) + zs[at, :] + line(bo[...])
            n, root = norm_rows(z)
            n1[at, :] = n
            r1[at, :] = root
            hb[at, :] = (n * line(g1[...]) + line(b1[...])).astype(bf16)
    turn(raw_cotangent, cr)

    arrive(6)
    chunk = CHUNK
    count = act.shape[1] // chunk

    def up(c, carry):
        at = pl.ds(pl.multiple_of(c * chunk, chunk), chunk)
        u = dot(hb[...], wu[:, at]) + line(bu[at])
        z = u * (0.5**0.5)
        half_cdf = 0.5 + 0.5 * lax.erf(z)
        act[:, at] = (u * half_cdf).astype(bf16)
        bell = jnp.exp2(z * z * -LOG2E - LOG2_ROOT)
        gp[:, at] = (half_cdf + u * bell).astype(bf16)
        return carry

    lax.fori_loop(0, count, up, 0)
    arrive(7)

    for half in halves:
        for c in range(width // BIG):
            at = slice(c * BIG, (c + 1) * BIG)
            zs[half, at] = dot(act[half, :], wd[:, at])
    results = []
    for pack in range(packs):
        for at in pieces_of(halves[pack]):
            hidden = n1[at, :] * line(g1[...]) + line(b1[...])
            z = hidden + zs[at, :] + line(bd[...])
            n, root = norm_rows(z)
            gain = line(g2[...])
            raw_tokens[at, :] = (n * gain + line(b2[...])).astype(bf16)
            d = norm_rows_back(cr[at, :].astype(f32) * gain, n, root)
            zs[at, :] = d
            hb[at, :] = d.astype(bf16)
        span = pl.ds(pack * rows, rows)
        rotate_rows(raw_tokens, pack * rows, rows, rows - starts[pack], put(cr, pack * rows))
        results.append(
            pltpu.make_async_copy(cr.at[span, :], out_hbm.at[span, :], sems.at[8 + pack])
        )
        results[-1].start()

    def up_back(c, carry):
        at = pl.ds(pl.multiple_of(c * chunk, chunk), chunk)
        t = dot(hb[...], wd[at, :], 1, 1)
        act[:, at] = (t * gp[:, at].astype(f32)).astype(bf16)
        return carry

    lax.fori_loop(0, count, up_back, 0)

    def down_back(c, carry):
        at = pl.ds(pl.multiple_of(c * BIG, BIG), BIG)
        zs[:, at] = zs[:, at] + dot(act[...], wu[at, :], 1, 1)
        return carry

    lax.fori_loop(0, width // BIG, down_back, 0)

    for copy in results:
        copy.wait()
    for half in halves:
        for at in pieces_of(half):
            d = norm_rows_back(zs[at, :] * line(g1[...]), n1[at, :], r1[at, :])
            zs[at, :] = d
            hb[at, :] = d.astype(bf16)
        cr[half, :] = dot(hb[half, :], wo[...], 1, 1).astype(bf16)

    dq, dk, dv = (act.at[:, k * width : (k + 1) * width] for k in range(3))

    def group_back(turn_no, carry):
        ready = {}

        def slopes(unit):
            _, _, block, span, at, half = unit
            if half == 0:
                scaled = cr[span, at].astype(f32) * inv[span, at]
                minus = pltpu.roll(-scaled * att[span, at].astype(f32), HEAD_DIM, 1)
                scaled = scaled.astype(bf16)
                ready[id(at), block] = scaled, minus.astype(bf16), scaled.T, qs[span, at].T
            scaled, minus = ready[id(at), block][:2]
            mine = low if half == 0 else high
            left = jnp.where(mine, scaled, minus)
            return dot(left, jnp.where(mine, vs[span, at], ones_pair), 1, 1)

        def weigh(unit, d):
            e = probs[unit[1]]
            return e * d.astype(bf16), e

        def grads_of(unit, held):
            _, _, block, span, at, half = unit
            ds, e = held
            _, _, scaled_t, query_t = ready[id(at), block]
            lines = slice(half * HEAD_DIM, (half + 1) * HEAD_DIM)
            return dot(ds, ks[span, at]), dot(query_t[lines], ds), dot(scaled_t[lines], e)

        def finish(unit, one, two):
            _, _, block, span, at, _ = unit
            ready.pop((id(at), block))
            dq[span, at] = (jnp.where(low, one[0], two[0]) * HEAD_DIM**-0.5).astype(bf16)
            turned = jnp.concatenate([one[1], two[1]], axis=0) * (1.0 / LOG2E)
            dk[span, at] = turned.astype(bf16).T
            dv[span, at] = jnp.concatenate([one[2], two[2]], axis=0).astype(bf16).T

        pipeline(heads_of(turn_no), slopes, weigh, grads_of, finish)
        return carry

    lax.fori_loop(0, turns, group_back, 0)

    dl = (dot(dq[...], uq[...], 1, 1) + dot(dv[...], uv[...], 1, 1)).astype(bf16)
    gd = dot(dl, xr[...], 0, 0)
    lora_t = lora[...].T
    gq = adapter_scale * dot(lora_t[: 2 * RANK], dq[...])[:RANK]
    gv = adapter_scale * dot(lora_t[HEAD_DIM : HEAD_DIM + 2 * RANK], dv[...])[:RANK]
    pack_grads(flat, gd, gq, gv)
    half_rows = flat.shape[0] // 2
    side = side_ref[0]
    kept = flat[pl.ds(pl.multiple_of(side * half_rows, 8), half_rows), :]
    more = first_ref.shape[0]
    send_ref[:half_rows, :] = flat[pl.ds(pl.multiple_of((1 - side) * half_rows, 8), half_rows), :]
    send_ref[half_rows:, :] = jnp.zeros((2 * more, LANES), f32)
    keep_ref[:half_rows, :] = kept
    keep_ref[half_rows : half_rows + more, :] = first_ref[...]
    keep_ref[half_rows + more :, :] = second_ref[...]

    act[:, 3 * width : 3 * width + LANES] = jnp.where(
        narrow, dl, jnp.zeros((total_rows, LANES), bf16)
    )


def token_kernel(begin, start_ref, wcat, grads, first, *rest):
    out_hbm, total, stage, sems = rest[-4:]
    total_rows, cut = total.shape
    packs = start_ref.shape[0]
    rows = total_rows // packs
    depth = wcat.shape[1]
    for c in range(cut // BIG):
        at = slice(begin + c * BIG, begin + (c + 1) * BIG)
        term = dot(grads[:, :depth], wcat[at, :], 1, 1)
        total[:, c * BIG : (c + 1) * BIG] = first[:, at] + term
    copies = []
    for pack in range(packs):
        span = pl.ds(pack * rows, rows)

        def emit(at, block, base=pack * rows):
            stage[pl.ds(base + at, 16), :] = block.astype(bf16)

        start = jnp.max(start_ref[pack : pack + 1, :]).astype(jnp.int32)
        rotate_rows(total, pack * rows, rows, rows - start, emit)
        to = out_hbm.at[span, begin : begin + cut]
        copies.append(pltpu.make_async_copy(stage.at[span, :], to, sems.at[pack]))
        copies[-1].start()
    for copy in copies:
        copy.wait()


def optimizer_kernel(places, *refs):
    steps_ref, rate_ref, place_ref, held, other, mine, theirs, params = refs[:8]
    grad_out, new_params, first_out, second_out, total = refs[8:]
    shares, own_rows = params.shape[:2]
    half = shares // 2
    place = place_ref[0]
    side = place & 1
    for k in range(half):
        at = slice(k * own_rows, (k + 1) * own_rows)
        total[side, k] = held[at, :]
        total[1 - side, k] = other[at, :]
    norm_sq = jnp.sum(jnp.sum(total[...] * total[...], axis=(0, 1)), keepdims=True)
    clip = jnp.minimum(1.0, lax.rsqrt(norm_sq + 1e-06))

    def power(base):
        return lax.fori_loop(0, steps_ref[0], lambda _, value: value * base, jnp.float32(1.0))

    shape = (own_rows, LANES)
    fix_one = jnp.full(shape, 1.0 - power(beta_one), f32)
    fix_two = jnp.full(shape, 1.0 - power(beta_two), f32)
    grad_out[...] = total[place // half, place % half]
    for j, mask in enumerate(places + [mask ^ 1 for mask in places]):
        source, at = (mine, 2 * j) if j < half else (theirs, 2 * (j - half))
        moment = source[at * own_rows : (at + 1) * own_rows, :]
        square = source[(at + 1) * own_rows : (at + 2) * own_rows, :]
        share = place ^ mask
        clipped = total[share // half, share % half] * clip
        first = beta_one * moment + (1.0 - beta_one) * clipped
        second = beta_two * square + (1.0 - beta_two) * clipped * clipped
        if j == 0:
            first_out[...] = first
            second_out[...] = second
        before = params[share]
        update = first / fix_one / (jnp.sqrt(second / fix_two) + adam_eps) + decay_rate * before
        rate = rate_ref[0] * jnp.where(share < half, 1.0, rate_ratio)
        new_params[share] = before - rate * update


def swap(x, axis, bit):
    n = lax.axis_size(axis)
    return lax.ppermute(x, axis, [(i, i ^ bit) for i in range(n)])


def bits_of(axis):
    n = lax.axis_size(axis)
    return [1 << k for k in range(n.bit_length() - 1)]


def shards(
    tokens,
    segment_ids,
    cotangent,
    query_frozen_weight,
    query_bias_vector,
    w_key,
    value_frozen_weight,
    value_bias_vector,
    w_out,
    b_out,
    norm1_gain,
    norm1_bias,
    w_up,
    b_up,
    w_down,
    b_down,
    norm2_gain,
    norm2_bias,
    factors,
    moment_first,
    moment_second,
    step_count,
    learn_rate,
):
    width = tokens.shape[1]
    packs, rows = segment_ids.shape
    ff = w_up.shape[1]
    total_rows = packs * rows
    flat_rows = factors.shape[0] // LANES
    shares = lax.axis_size("wide")
    own_rows = flat_rows // shares
    half_rows = flat_rows // 2
    place = lax.axis_index("wide").astype(jnp.int32)

    whole = pl.BlockSpec(memory_space=pltpu.VMEM)
    anywhere = pl.BlockSpec(memory_space=pl.ANY)
    scalars = pl.BlockSpec(memory_space=pltpu.SMEM)
    result = lambda shape, dtype: jax.ShapeDtypeStruct(shape, dtype)
    weights = (query_frozen_weight, w_key, value_frozen_weight, w_out, w_up, w_down)
    vectors = (
        query_bias_vector,
        value_bias_vector,
        b_out,
        norm1_gain,
        norm1_bias,
        b_up,
        b_down,
        norm2_gain,
        norm2_bias,
    )
    tall = lambda dtype: pltpu.VMEM((total_rows, width), dtype)
    kept, sent, output, *for_tokens = pl.pallas_call(
        main_kernel,
        out_shape=(
            pltpu.VMEM((half_rows + 2 * own_rows, LANES), f32),
            pltpu.VMEM((half_rows + 2 * own_rows, LANES), f32),
            result((total_rows, width), bf16),
            pltpu.VMEM((packs, LANES), f32),
            pltpu.VMEM((width, 3 * width + LANES), bf16),
            pltpu.VMEM((total_rows, ff), bf16),
            tall(f32),
        ),
        in_specs=[scalars] + [whole] * (4 + len(vectors)) + [anywhere] * 8,
        out_specs=[whole, whole, anywhere] + [whole] * 4,
        scratch_shapes=[pltpu.VMEM(w.shape, bf16) for w in weights[3:]]
        + [
            pltpu.SemaphoreType.DMA((8 + packs,)),
            tall(bf16),
            tall(bf16),
            tall(bf16),
            tall(bf16),
            tall(bf16),
            pltpu.VMEM((total_rows, LANES), bf16),
            pltpu.VMEM((packs * HEADS * 2, BIG, BIG), bf16),
            tall(bf16),
            tall(f32),
            tall(f32),
            pltpu.VMEM((total_rows, 1), f32),
            tall(bf16),
            pltpu.VMEM((total_rows, ff), bf16),
            pltpu.VMEM((LANES, width), bf16),
            pltpu.VMEM((LANES, width), bf16),
            pltpu.VMEM((packs, BIG, LANES), bf16),
            pltpu.VMEM((packs, BIG, LANES), bf16),
            pltpu.VMEM((flat_rows, LANES), f32),
        ],
        compiler_params=pltpu.CompilerParams(vmem_limit_bytes=VMEM_LIMIT),
    )(
        (place & 1).reshape(1),
        segment_ids,
        factors.reshape(flat_rows, LANES),
        moment_first.reshape(own_rows, LANES),
        moment_second.reshape(own_rows, LANES),
        *vectors,
        tokens,
        cotangent,
        *weights,
    )

    def token_piece(begin, cut, before, tie):
        held = [] if before is None else [before]
        start, _ = lax.optimization_barrier((for_tokens[0], tie))
        return pl.pallas_call(
            functools.partial(token_kernel, begin),
            out_shape=result((total_rows, width), bf16),
            in_specs=[whole] * 4 + [anywhere] * len(held),
            out_specs=anywhere,
            scratch_shapes=[
                pltpu.VMEM((total_rows, cut), f32),
                pltpu.VMEM((total_rows, cut), bf16),
                pltpu.SemaphoreType.DMA((packs,)),
            ],
            input_output_aliases={4: 0} if held else {},
            compiler_params=pltpu.CompilerParams(vmem_limit_bytes=16 * 2**20),
            cost_estimate=pl.CostEstimate(
                flops=2 * total_rows * cut * (3 * width + LANES),
                bytes_accessed=total_rows * cut * 2,
                transcendentals=0,
            ),
        )(start, *for_tokens[1:], *held)

    held = kept + swap(sent, "wide", 1)
    bits = bits_of("wide")[1:]
    places = [0]
    grad_tokens = None
    while bits:
        now, bits = bits[:2], bits[2:]
        masks = [now[0]] if len(now) == 1 else [now[0], now[1], now[0] | now[1]]
        got = [swap(held, "wide", mask) for mask in masks]
        if grad_tokens is None:
            grad_tokens = token_piece(0, width - BIG, None, held)
            grad_tokens, *got = lax.optimization_barrier((grad_tokens, *got))
        if len(got) == 1:
            total = held[:half_rows] + got[0][:half_rows]
        else:
            total = (held[:half_rows] + got[0][:half_rows]) + (
                got[1][:half_rows] + got[2][:half_rows]
            )
        places = places + [old ^ mask for mask in masks for old in places]
        if bits:
            held = jnp.concatenate([total] + [part[half_rows:] for part in [held] + got])
        else:
            moments = [part[half_rows:] for part in [held] + got]
    mine = jnp.concatenate(moments)
    theirs = swap(mine, "wide", 1)
    for bit in bits_of("dp"):
        got = swap(total, "dp", bit)
        if bit == 1:
            grad_tokens = token_piece(width - BIG, BIG, grad_tokens, total)
            grad_tokens, got = lax.optimization_barrier((grad_tokens, got))
        total = total + got
    other = swap(total, "wide", 1)
    placed = functools.partial(pltpu.with_memory_space_constraint, memory_space=pltpu.VMEM)

    own = result((own_rows, LANES), f32)
    shaped = (shares, own_rows, LANES)
    grad_own, new_factors, new_first, new_second = pl.pallas_call(
        functools.partial(optimizer_kernel, places),
        out_shape=(own, result(shaped, f32), own, own),
        in_specs=[scalars] * 3 + [whole] * 5,
        out_specs=[whole] * 4,
        scratch_shapes=[pltpu.VMEM((2, shares // 2, own_rows, LANES), f32)],
    )(
        step_count,
        learn_rate,
        place.reshape(1),
        placed(total),
        placed(other),
        placed(mine),
        placed(theirs),
        placed(factors.reshape(shaped)),
    )
    return (
        output,
        grad_tokens,
        grad_own.reshape(-1),
        new_factors.reshape(-1),
        new_first.reshape(-1),
        new_second.reshape(-1),
    )


def solution(mesh):
    rows = P(("dp", "wide"), None)
    in_specs = (rows,) * 3 + (P(),) * 16 + (P("wide"), P("wide"), P(), P())
    out_specs = (rows, rows, P("wide"), P(), P("wide"), P("wide"))
    return jax.shard_map(shards, mesh=mesh, in_specs=in_specs, out_specs=out_specs, check_vma=False)
```
